32 devices in a mesh: fsdp: 4 (over y, core), ctx: 2 (over x), tp: 4 (over z).
Axes of the slice: x: 2, y: 2, z: 4, core: 2. Of those that a mesh axis runs over, the one named last changes fastest.
Arguments:
- inputs: bfloat16 [32, 320, 1024], P('fsdp', 'ctx'), may hold values from -6 to 6
- cotangent: bfloat16 [32, 320, 1024], P('fsdp', 'ctx'), may hold values from -6 to 6
- visible: int32 [32, 320], P('fsdp'), may hold values from 0 to 1, as said below
- w_qkv: float32 [1024, 3, 1024], P('fsdp', None, 'tp'), may hold values from -0.1875 to 0.1875
- b_qv: float32 [2, 1024], P(None, 'tp'), may hold values from -3 to 3
- w_out: float32 [1024, 1024], P('tp', 'fsdp'), may hold values from -0.75 to 0.75
- b_out: float32 [1024], replicated, may hold values from -3 to 3
- w_up: float32 [1024, 4096], P('fsdp', 'tp'), may hold values from -0.1875 to 0.1875
- b_up: float32 [4096], P('tp'), may hold values from -3 to 3
- w_down: float32 [4096, 1024], P('tp', 'fsdp'), may hold values from -0.09375 to 0.09375
- b_down: float32 [1024], replicated, may hold values from -3 to 3
- gain_one: float32 [1024], replicated, may hold values from 0.1 to 1.9
- shift_one: float32 [1024], replicated, may hold values from -3 to 3
- gain_two: float32 [1024], replicated, may hold values from 0.1 to 1.9
- shift_two: float32 [1024], replicated, may hold values from -3 to 3
Outputs:
- output: float32 [32, 320, 1024], P('fsdp', 'ctx')
- grad_inputs: float32 [32, 320, 1024], P('fsdp', 'ctx')
- grad_w_qkv: float32 [1024, 3, 1024], P('fsdp', None, 'tp')
- grad_b_qv: float32 [2, 1024], P(None, 'tp')
- grad_w_out: float32 [1024, 1024], P('tp', 'fsdp')
- grad_b_out: float32 [1024], replicated
- grad_w_up: float32 [1024, 4096], P('fsdp', 'tp')
- grad_b_up: float32 [4096], P('tp')
- grad_w_down: float32 [4096, 1024], P('tp', 'fsdp')
- grad_b_down: float32 [1024], replicated
- grad_gain_one: float32 [1024], replicated
- grad_shift_one: float32 [1024], replicated
- grad_gain_two: float32 [1024], replicated
- grad_shift_two: float32 [1024], replicated
The draws below stay inside these ranges and needn't reach their ends.
Inputs may be any that keep to these rules, and one draw needn't show every extreme that they name: `visible`: the first 64 tokens of every image are 1; of the 256 image tokens of each image between a tenth and two fifths are 0.
All inputs are finite; a program needn't handle non-finite values.
Results may differ from the reference program's by a relative error of at most 0.012.
Values may be sent and summed in bfloat16 or wider, within the bound.
No kernel may reach another device: no remote copies, remote signals or barrier semaphores. Data moves between devices by JAX's collectives and lax.ppermute only.
A program may use at most 192 MiB of HBM per device.

```python
import jax
import jax.numpy as jnp
from jax import lax

D = 1024
HEADS = 16
HEAD = 64
FF = 4096
SEQ = 320
BUFFER = 64
IMG_DEV = 8
IMAGES = 32
PATCHES = 256


def draw_visible(key, part):
    count_key, order_key = jax.random.split(key)
    hidden_count = jax.random.randint(count_key, (IMAGES, 1), PATCHES // 10 + 1, 2 * PATCHES // 5 + 1)
    subkeys = jax.random.split(order_key, IMAGES)
    orders = jax.vmap(lambda one_key: jax.random.permutation(one_key, PATCHES))(subkeys)
    image_part = (orders >= hidden_count).astype(jnp.int32)
    return jnp.concatenate([jnp.ones((IMAGES, BUFFER), jnp.int32), image_part], axis=1)


def block_scale(own_key, extent, pieces, least, largest):
    def one(axis_at, parts):
        heights = jax.random.uniform(jax.random.fold_in(jax.random.fold_in(own_key, 6), axis_at), (parts,), jnp.float32, least / len(pieces), largest / len(pieces))
        return jnp.repeat(jnp.exp(heights), extent[axis_at] // parts).reshape((-1,) + (1,) * (len(extent) - axis_at - 1))

    level = one(*pieces[0])
    for cut in pieces[1:]:
        level = level * one(*cut)
    return level


def scatter_about(key, extent, scale, reach, shards=(), dtype=jnp.bfloat16):
    values = jax.random.normal(key, extent, jnp.float32) * scale
    if len(shards) > 0:
        values = block_scale(key, extent, shards, -0.22, 0.18) * values
    return jnp.clip(values, min=-reach, max=reach).astype(dtype)


def setup_inputs(seed: int = 0) -> dict:
    keys = jax.random.split(jax.random.key(seed), 16)
    return {
        "inputs": scatter_about(keys[0], (IMAGES, SEQ, D), 1.0, 6.0, ((0, 4), (1, 2))),
        "cotangent": scatter_about(keys[1], (IMAGES, SEQ, D), 1.0, 6.0, ((0, 4), (1, 2))),
        "visible": draw_visible(jax.random.fold_in(keys[15], 71), 0),
        "w_qkv": scatter_about(keys[3], (D, 3, D), D ** -0.5, 0.1875, ((0, 4), (2, 4)), jnp.float32),
        "b_qv": scatter_about(keys[4], (2, D), 0.5, 3.0, ((1, 4),), jnp.float32),
        "w_out": scatter_about(keys[5], (D, D), (D // 16) ** -0.5, 0.75, ((0, 4), (1, 4)), jnp.float32),
        "b_out": scatter_about(keys[6], (D,), 0.5, 3.0, (), jnp.float32),
        "w_up": scatter_about(keys[7], (D, FF), D ** -0.5, 0.1875, ((0, 4), (1, 4)), jnp.float32),
        "b_up": scatter_about(keys[8], (FF,), 0.5, 3.0, ((0, 4),), jnp.float32),
        "w_down": scatter_about(keys[9], (FF, D), FF ** -0.5, 0.09375, ((0, 4), (1, 4)), jnp.float32),
        "b_down": scatter_about(keys[10], (D,), 0.5, 3.0, (), jnp.float32),
        "gain_one": jnp.clip(1.0 + 0.18 * jax.random.normal(keys[11], (D,), jnp.float32), 0.1, 1.9),
        "shift_one": scatter_about(keys[12], (D,), 0.5, 3.0, (), jnp.float32),
        "gain_two": jnp.clip(1.0 + 0.18 * jax.random.normal(keys[13], (D,), jnp.float32), 0.1, 1.9),
        "shift_two": scatter_about(keys[14], (D,), 0.5, 3.0, (), jnp.float32),
    }


@jax.custom_vjp
def low(v):
    return lax.optimization_barrier(v.astype(jnp.bfloat16)).astype(jnp.float32)

@jax.custom_vjp
def low_back(v):
    return v

def low_keep(v):
    return (low(v), None)

def low_pass(kept, grad):
    return (grad,)

def back_keep(v):
    return (v, None)

def back_low(kept, grad):
    return (low(grad),)
low.defvjp(low_keep, low_pass)
low_back.defvjp(back_keep, back_low)
EPSILON = 1e-06
HIGH = lax.Precision.HIGHEST

def layer_norm(values, gain, shift):
    center = values - lax.optimization_barrier(jnp.mean(values, axis=-1, keepdims=True))
    spread = lax.optimization_barrier(jnp.mean(center * center, axis=-1, keepdims=True))
    return center * lax.rsqrt(spread + EPSILON) * gain + shift

def gelu_exact(values):
    return jax.nn.gelu(values, approximate=False)

def block_forward(params, images_in, visible_in):
    w_qkv, b_qv, w_out, b_out, w_up, b_up, w_down, b_down, gain_one, shift_one, gain_two, shift_two = params
    count = images_in.shape[0]
    scale_factor = HEAD ** (-0.5)
    tokens = images_in.reshape(count * SEQ, D)
    normed = low(layer_norm(tokens, gain_one, shift_one))
    bias_all = jnp.stack([b_qv[0], jnp.zeros((D,), jnp.float32), b_qv[1]])
    projected = jnp.einsum('td,dcf->tcf', normed, low(w_qkv), precision=HIGH) + bias_all
    projected = low_back(low(projected))
    queries = projected[:, 0].reshape(count, SEQ, HEADS, HEAD)
    keys_all = projected[:, 1].reshape(count, SEQ, HEADS, HEAD)
    values_all = projected[:, 2].reshape(count, SEQ, HEADS, HEAD)
    scores = low_back(jnp.einsum('iqhe,ikhe->ihqk', queries, keys_all, precision=HIGH) * scale_factor)
    key_keep = (visible_in > 0)[:, None, None, :]
    scores = jnp.where(key_keep, scores, -1e+30)
    row_max = lax.optimization_barrier(jnp.max(scores, axis=-1, keepdims=True))
    exponent = jnp.exp(scores - row_max)
    probability = exponent / lax.optimization_barrier(jnp.sum(exponent, axis=-1, keepdims=True))
    mixed_heads = jnp.einsum('ihqk,ikhe->iqhe', low(probability), values_all, precision=HIGH)
    mixed_heads = low_back(low(mixed_heads.reshape(count * SEQ, D)))
    attended = low_back(jnp.dot(mixed_heads, low(w_out), precision=HIGH) + b_out)
    residual = tokens + attended
    normed_two = low(layer_norm(residual, gain_two, shift_two))
    hidden = low_back(jnp.dot(normed_two, low(w_up), precision=HIGH) + b_up)
    active = low(gelu_exact(hidden))
    branch = low_back(jnp.dot(active, low(w_down), precision=HIGH) + b_down)
    row_keep = visible_in.reshape(count * SEQ, 1).astype(jnp.float32)
    return (row_keep * (residual + branch)).reshape(count, SEQ, D)

def reference(inputs, cotangent, visible, w_qkv, b_qv, w_out, b_out, w_up, b_up, w_down, b_down, gain_one, shift_one, gain_two, shift_two):
    groups = inputs.shape[0] // IMG_DEV
    visible_groups = visible.reshape(groups, IMG_DEV, SEQ)

    def forward(inputs_all, *params):

        def one_group(group_pair):
            return block_forward(params, group_pair[0], group_pair[1])
        grouped = inputs_all.reshape(groups, IMG_DEV, SEQ, D)
        outputs = lax.map(jax.checkpoint(one_group), (grouped, visible_groups))
        return outputs.reshape(groups * IMG_DEV, SEQ, D)
    result, pullback = jax.vjp(forward, inputs.astype(jnp.float32), w_qkv.astype(jnp.float32), b_qv.astype(jnp.float32), w_out.astype(jnp.float32), b_out.astype(jnp.float32), w_up.astype(jnp.float32), b_up.astype(jnp.float32), w_down.astype(jnp.float32), b_down.astype(jnp.float32), gain_one.astype(jnp.float32), shift_one.astype(jnp.float32), gain_two.astype(jnp.float32), shift_two.astype(jnp.float32))
    gradients = pullback(cotangent.astype(jnp.float32))
    return (result, gradients[0], gradients[1], gradients[2], gradients[3], gradients[4], gradients[5], gradients[6], gradients[7], gradients[8], gradients[9], gradients[10], gradients[11], gradients[12])
```

```python
import functools

import jax
import jax.numpy as jnp
from jax import lax
from jax.experimental import pallas as pl
from jax.experimental.pallas import tpu as pltpu
from jax.sharding import PartitionSpec as P

HEAD = 64
EPSILON = 1e-06
F32 = jnp.float32
LOW = jnp.bfloat16

NN = (((1,), (0,)), ((), ()))
NT = (((1,), (1,)), ((), ()))
TN = (((0,), (0,)), ((), ()))


def mm(left, right, dims=NN):
    return lax.dot_general(left, right, dims, preferred_element_type=F32)


def whole(shape):
    return pl.BlockSpec(shape, lambda t: (0,) * len(shape))


def part(shape):
    return pl.BlockSpec((1,) + shape, lambda t: (t,) + (0,) * len(shape))


def call(body, parts, ins, outs, args, flops, moved, exps=0):
    return pl.pallas_call(
        body,
        grid=(parts,),
        in_specs=ins,
        out_specs=[spec for spec, _ in outs],
        out_shape=[shape for _, shape in outs],
        compiler_params=pltpu.CompilerParams(
            dimension_semantics=("arbitrary",), vmem_limit_bytes=48 << 20
        ),
        cost_estimate=pl.CostEstimate(flops=flops, bytes_accessed=moved, transcendentals=exps),
    )(*args)


def attention_body(n_ref, w_ref, b_ref, keep_ref, p_ref, o_ref, l_ref):
    width = o_ref.shape[2]
    low = (mm(n_ref[...], w_ref[0]) + b_ref[0]).astype(LOW)
    p_ref[0] = low
    keep = keep_ref[...] > 0
    for head in range(width // HEAD):
        at = head * HEAD
        query = low[:, at : at + HEAD]
        key = low[:, width + at : width + at + HEAD]
        value = low[:, 2 * width + at : 2 * width + at + HEAD]
        scores = jnp.where(keep, mm(key, query, NT) * HEAD**-0.5, -1e30)
        top = jnp.max(scores, axis=0, keepdims=True)
        exponent = jnp.exp(scores - top)
        total = jnp.sum(exponent, axis=0, keepdims=True)
        probability = (exponent * (1.0 / total)).astype(LOW)
        o_ref[0, :, at : at + HEAD] = mm(probability, value, TN).astype(LOW)
        l_ref[0, head : head + 1, :] = top + jnp.log(total)


def attention(normed, weights, bias, keep):
    parts, width_in, width3 = weights.shape
    rows = normed.shape[0]
    width = width3 // 3
    heads = width // HEAD
    return call(
        attention_body,
        parts,
        [whole((rows, width_in)), part((width_in, width3)), part((1, width3)), whole((rows, 1))],
        [
            (part((rows, width3)), jax.ShapeDtypeStruct((parts, rows, width3), LOW)),
            (part((rows, width)), jax.ShapeDtypeStruct((parts, rows, width), LOW)),
            (part((heads, rows)), jax.ShapeDtypeStruct((parts, heads, rows), F32)),
        ],
        (normed, weights, bias, keep),
        2 * parts * rows * width_in * width3 + 4 * parts * rows * rows * width,
        2 * weights.size + 16 * parts * rows * width,
        parts * heads * rows * rows,
    )


def attention_back_body(d_ref, wo_ref, p_ref, l_ref, keep_ref, w_ref, dp_ref, dn_ref, db_ref):
    width = wo_ref.shape[2]
    grad_mixed = mm(d_ref[...], wo_ref[0]).astype(LOW)
    keep = keep_ref[...] > 0
    for head in range(width // HEAD):
        at = head * HEAD
        query = p_ref[0, :, at : at + HEAD]
        key = p_ref[0, :, width + at : width + at + HEAD]
        value = p_ref[0, :, 2 * width + at : 2 * width + at + HEAD]
        grad = grad_mixed[:, at : at + HEAD]
        scores = jnp.where(keep, mm(key, query, NT) * HEAD**-0.5, -1e30)
        probability = jnp.exp(scores - l_ref[0, head : head + 1, :])
        grad_probability = mm(value, grad, NT)
        grad_value = mm(probability.astype(LOW), grad)
        inner = jnp.sum(grad_probability * probability, axis=0, keepdims=True)
        grad_scores = (probability * (grad_probability - inner)).astype(LOW)
        grad_query = mm(grad_scores, key, TN) * HEAD**-0.5
        grad_key = mm(grad_scores, query) * HEAD**-0.5
        dp_ref[0, :, at : at + HEAD] = grad_query.astype(LOW)
        dp_ref[0, :, width + at : width + at + HEAD] = grad_key.astype(LOW)
        dp_ref[0, :, 2 * width + at : 2 * width + at + HEAD] = grad_value.astype(LOW)
    low = dp_ref[0]
    db_ref[0] = jnp.sum(low.astype(F32), axis=0, keepdims=True)
    grad_normed = mm(low, w_ref[0], NT)

    @pl.when(pl.program_id(0) == 0)
    def _():
        dn_ref[...] = grad_normed

    @pl.when(pl.program_id(0) > 0)
    def _():
        dn_ref[...] += grad_normed


def attention_back(grad, out_w, projected, log_total, keep, weights):
    parts, width_in, width3 = weights.shape
    rows = grad.shape[0]
    width = width3 // 3
    heads = width // HEAD
    return call(
        attention_back_body,
        parts,
        [
            whole((rows, width_in)),
            part((width_in, width)),
            part((rows, width3)),
            part((heads, rows)),
            whole((rows, 1)),
            part((width_in, width3)),
        ],
        [
            (part((rows, width3)), jax.ShapeDtypeStruct((parts, rows, width3), LOW)),
            (whole((rows, width_in)), jax.ShapeDtypeStruct((rows, width_in), F32)),
            (part((1, width3)), jax.ShapeDtypeStruct((parts, 1, width3), F32)),
        ],
        (grad, out_w, projected, log_total, keep, weights),
        2 * parts * rows * width_in * (width3 + width) + 10 * parts * rows * rows * width,
        2 * weights.size + 2 * out_w.size + 16 * parts * rows * width,
        parts * heads * rows * rows,
    )


def output_body(o_ref, w_ref, x_ref, b_ref, gain_ref, shift_ref, y_ref, n_ref):
    product = mm(o_ref[0], w_ref[0], NT)

    @pl.when(pl.program_id(0) == 0)
    def _():
        y_ref[...] = x_ref[...].astype(F32) + b_ref[...] + product

    @pl.when(pl.program_id(0) > 0)
    def _():
        y_ref[...] += product

    @pl.when(pl.program_id(0) == pl.num_programs(0) - 1)
    def _():
        n_ref[...] = layer_norm(y_ref[...], gain_ref[...], shift_ref[...]).astype(LOW)


def output_product(mixed, out_w, tokens, bias, gain, shift):
    parts, rows, width = mixed.shape
    wide = out_w.shape[1]
    return call(
        output_body,
        parts,
        [part((rows, width)), part((wide, width)), whole((rows, wide))] + [whole((1, wide))] * 3,
        [
            (whole((rows, wide)), jax.ShapeDtypeStruct((rows, wide), F32)),
            (whole((rows, wide)), jax.ShapeDtypeStruct((rows, wide), LOW)),
        ],
        (mixed, out_w, tokens, bias[None], gain[None], shift[None]),
        2 * parts * rows * width * wide,
        2 * out_w.size + 8 * rows * wide,
    )


def up_body(n_ref, w_ref, b_ref, a_ref, s_ref):
    hidden = mm(n_ref[...], w_ref[0]) + b_ref[0]
    bell = 0.5 * (1.0 + lax.erf(hidden * 0.5**0.5))
    a_ref[0] = (hidden * bell).astype(LOW)
    slope = bell + hidden * jnp.exp(hidden * hidden * -0.5) * 0.3989422804014327
    s_ref[0] = slope.astype(LOW)


def up_product(normed, weights, bias):
    parts, width_in, width = weights.shape
    rows = normed.shape[0]
    shape = jax.ShapeDtypeStruct((parts, rows, width), LOW)
    return call(
        up_body,
        parts,
        [whole((rows, width_in)), part((width_in, width)), part((1, width))],
        [(part((rows, width)), shape), (part((rows, width)), shape)],
        (normed, weights, bias),
        2 * parts * rows * width_in * width,
        2 * weights.size + 4 * parts * rows * width,
        2 * parts * rows * width,
    )


def down_body(a_ref, w_ref, g_ref, s_ref, wu_ref, r_ref, du_ref, dn_ref, db_ref):
    branch = mm(a_ref[0], w_ref[0], NT)
    low = (mm(g_ref[...], w_ref[0]) * s_ref[0].astype(F32)).astype(LOW)
    du_ref[0] = low
    db_ref[0] = jnp.sum(low.astype(F32), axis=0, keepdims=True)
    grad_normed = mm(low, wu_ref[0], NT)

    @pl.when(pl.program_id(0) == 0)
    def _():
        r_ref[...] = branch
        dn_ref[...] = grad_normed

    @pl.when(pl.program_id(0) > 0)
    def _():
        r_ref[...] += branch
        dn_ref[...] += grad_normed


def down_product(active, down_w, grad, slope, up_w):
    parts, rows, width = active.shape
    wide = down_w.shape[1]
    return call(
        down_body,
        parts,
        [
            part((rows, width)),
            part((wide, width)),
            whole((rows, wide)),
            part((rows, width)),
            part((wide, width)),
        ],
        [
            (whole((rows, wide)), jax.ShapeDtypeStruct((rows, wide), F32)),
            (part((rows, width)), jax.ShapeDtypeStruct((parts, rows, width), LOW)),
            (whole((rows, wide)), jax.ShapeDtypeStruct((rows, wide), F32)),
            (part((1, width)), jax.ShapeDtypeStruct((parts, 1, width), F32)),
        ],
        (active, down_w, grad, slope, up_w),
        6 * parts * rows * width * wide,
        4 * down_w.size + 6 * parts * rows * width + 8 * rows * wide,
    )


def weight_body(l_ref, r_ref, w_ref):
    w_ref[0] = mm(l_ref[...], r_ref[0]).astype(LOW)


def weight_product(turned, right):
    parts, rows, width = right.shape
    wide = turned.shape[0]
    return call(
        weight_body,
        parts,
        [whole((wide, rows)), part((rows, width))],
        [(part((wide, width)), jax.ShapeDtypeStruct((parts, wide, width), LOW))],
        (turned, right),
        2 * parts * rows * width * wide,
        2 * parts * width * (rows + wide),
    )[0]


def layer_norm(values, gain, shift):
    center = values - jnp.mean(values, axis=-1, keepdims=True)
    spread = jnp.mean(center * center, axis=-1, keepdims=True)
    return center * lax.rsqrt(spread + EPSILON) * gain + shift


def layer_norm_back(values, gain, grad):
    center = values - jnp.mean(values, axis=-1, keepdims=True)
    scale = lax.rsqrt(jnp.mean(center * center, axis=-1, keepdims=True) + EPSILON)
    unit = center * scale
    scaled = grad * gain
    back = scale * (
        scaled
        - jnp.mean(scaled, axis=-1, keepdims=True)
        - unit * jnp.mean(scaled * unit, axis=-1, keepdims=True)
    )
    return back, jnp.sum(grad * unit, axis=0), jnp.sum(grad, axis=0)


def on_device(
    inputs,
    cotangent,
    visible,
    w_qkv,
    b_qv,
    w_out,
    b_out,
    w_up,
    b_up,
    w_down,
    b_down,
    gain_one,
    shift_one,
    gain_two,
    shift_two,
):
    images, half, wide = inputs.shape
    ctx_at, tp_at = lax.axis_index("ctx"), lax.axis_index("tp")
    blocks, parts = lax.axis_size("ctx"), lax.axis_size("tp")
    assert blocks == 2 and images == blocks * parts
    first = blocks * tp_at
    mine, other = first + ctx_at, first + 1 - ctx_at
    spread_axes = ("tp", "fsdp")

    def swap(values):
        return lax.ppermute(values, "ctx", [(0, 1), (1, 0)])

    def pick(values, index):
        return lax.dynamic_index_in_dim(values, index, 0, keepdims=False)

    def in_order(own, received):
        first_half = jnp.where(ctx_at == 0, own, received)
        second_half = jnp.where(ctx_at == 0, received, own)
        return first_half, second_half

    def gather(shard):
        full = lax.all_gather(shard, spread_axes, axis=0, tiled=True)
        return full.reshape(parts, wide, shard.shape[1])

    heads_width = w_qkv.shape[2]
    hidden_half = w_up.shape[1] // 2
    qkv_w = gather(w_qkv.astype(LOW).reshape(-1, 3 * heads_width))
    out_w = gather(w_out.T.astype(LOW))
    up_w = gather(lax.dynamic_slice_in_dim(w_up, ctx_at * hidden_half, hidden_half, 1).astype(LOW))
    down_w = gather(
        lax.dynamic_slice_in_dim(w_down, ctx_at * hidden_half, hidden_half, 0).T.astype(LOW)
    )
    biases = lax.all_gather(jnp.concatenate([b_qv.reshape(-1), b_up]), "tp", axis=0)
    bias_q, bias_v = biases[:, :heads_width], biases[:, heads_width : 2 * heads_width]
    qkv_bias = jnp.concatenate([bias_q, jnp.zeros_like(bias_q), bias_v], axis=1)[:, None]
    up_bias = lax.dynamic_slice_in_dim(
        biases, 2 * heads_width + ctx_at * hidden_half, hidden_half, 1
    )[:, None]

    tokens = jnp.concatenate([pick(inputs, mine), swap(pick(inputs, other))], axis=0)
    cot_pair = jnp.stack([pick(cotangent, mine), pick(cotangent, other)])
    cot_swapped = swap(cot_pair)
    mine_seen = pick(visible, mine).reshape(blocks, half)
    other_seen = pick(visible, other).reshape(blocks, half)
    keep = jnp.concatenate([pick(mine_seen, ctx_at), pick(mine_seen, 1 - ctx_at)])
    keep_other = jnp.concatenate([pick(other_seen, 1 - ctx_at), pick(other_seen, ctx_at)])
    keep, keep_other = keep[:, None], keep_other[:, None]
    keep_all = jnp.concatenate([keep, keep_other]).astype(LOW)
    grad_low = (
        jnp.concatenate([cot_pair[0], cot_swapped[1], cot_swapped[0], cot_pair[1]]) * keep_all
    )
    rows = 2 * half

    flat_in = tokens.astype(F32)
    normed_low = layer_norm(flat_in, gain_one, shift_one).astype(LOW)
    projected, mixed, log_total = attention(normed_low, qkv_w, qkv_bias, keep)
    residual, normed_two = output_product(mixed, out_w, tokens, b_out, gain_two, shift_two)
    both = jnp.concatenate([normed_two, swap(normed_two)])
    active, slope = up_product(both, up_w, up_bias)
    down_grad = weight_product(grad_low.T, active)
    branch, grad_hidden, grad_both, up_bias_grad = down_product(
        active, down_w, grad_low, slope, up_w
    )
    up_grad = weight_product(both.T, grad_hidden)

    sent = jnp.concatenate([residual[half:] + branch[half:rows], branch[rows : rows + half]])
    came = swap(sent.astype(LOW)).astype(F32)
    out_mine = residual[:half] + branch[:half] + came[half:] + b_down
    out_other = branch[rows + half :] + came[:half] + b_down
    out_mine = (out_mine * keep[:half].astype(F32)).astype(LOW)
    out_other = (out_other * keep_other[half:].astype(F32)).astype(LOW)
    out_pair = jnp.stack(in_order(out_mine, out_other))
    result = lax.all_gather(out_pair, "tp", axis=0, tiled=True).astype(F32)

    grad_normed_two = grad_both[:rows] + swap(grad_both[rows:].astype(LOW)).astype(F32)
    back_two, gain_two_grad, shift_two_grad = layer_norm_back(residual, gain_two, grad_normed_two)
    grad_out = grad_low[:rows].astype(F32)
    grad_residual = grad_out + back_two
    grad_attended = grad_residual.astype(LOW)
    out_grad = weight_product(grad_attended.T, mixed)
    grad_projected, grad_normed, qkv_bias_grad = attention_back(
        grad_attended, out_w, projected, log_total, keep, qkv_w
    )
    qkv_grad = weight_product(normed_low.T, grad_projected)
    back_one, gain_one_grad, shift_one_grad = layer_norm_back(flat_in, gain_one, grad_normed)
    grad_in = (grad_residual + back_one).astype(LOW)
    grad_in_pair = jnp.stack(in_order(grad_in[:half], swap(grad_in[half:])))
    grad_inputs = lax.all_gather(grad_in_pair, "tp", axis=0, tiled=True).astype(F32)

    def scatter(grad):
        flat = grad.reshape(-1, grad.shape[2])
        return lax.psum_scatter(flat, spread_axes, scatter_dimension=0, tiled=True)

    down_own, up_own, out_own, qkv_own = (
        scatter(down_grad),
        scatter(up_grad),
        scatter(out_grad),
        scatter(qkv_grad),
    )
    out_total = out_own.astype(F32) + swap(out_own).astype(F32)
    qkv_total = qkv_own.astype(F32) + swap(qkv_own).astype(F32)
    up_total = jnp.concatenate(in_order(up_own, swap(up_own)), axis=1).astype(F32)
    down_total = jnp.concatenate(in_order(down_own, swap(down_own)), axis=1).astype(F32)

    up_bias_slot = jnp.zeros((parts, 2, hidden_half), F32)
    up_bias_slot = lax.dynamic_update_slice(up_bias_slot, up_bias_grad, (0, ctx_at, 0))
    qkv_bias_grad = qkv_bias_grad.reshape(parts, 3, heads_width)
    small = lax.psum(
        (
            qkv_bias_grad[:, 0::2],
            up_bias_slot,
            jnp.sum(grad_attended.astype(F32), axis=0),
            jnp.sum(grad_out, axis=0),
            gain_one_grad,
            shift_one_grad,
            gain_two_grad,
            shift_two_grad,
        ),
        ("fsdp", "ctx", "tp"),
    )
    return (
        result,
        grad_inputs,
        qkv_total.reshape(-1, 3, heads_width),
        pick(small[0], tp_at),
        out_total.T,
        small[2],
        up_total,
        pick(small[1], tp_at).reshape(-1),
        down_total.T,
        small[3],
        small[4],
        small[5],
        small[6],
        small[7],
    )


def solution(mesh):
    placed = (
        P("fsdp", "ctx", None),
        P("fsdp", "ctx", None),
        P("fsdp", None),
        P("fsdp", None, "tp"),
        P(None, "tp"),
        P("tp", "fsdp"),
        P(),
        P("fsdp", "tp"),
        P("tp"),
        P("tp", "fsdp"),
        P(),
        P(),
        P(),
        P(),
        P(),
    )
    return jax.shard_map(
        on_device,
        mesh=mesh,
        in_specs=placed,
        out_specs=(
            P("fsdp", "ctx", None),
            P("fsdp", "ctx", None),
            P("fsdp", None, "tp"),
            P(None, "tp"),
            P("tp", "fsdp"),
            P(),
            P("fsdp", "tp"),
            P("tp"),
            P("tp", "fsdp"),
            P(),
            P(),
            P(),
            P(),
            P(),
        ),
        check_vma=False,
    )
```

```python
import jax
import jax.numpy as jnp
from jax import lax
from jax.experimental import pallas as pl
from jax.experimental.pallas import tpu as pltpu
from jax.sharding import PartitionSpec as P

HEAD = 64
EPSILON = 1e-06
F32 = jnp.float32
LOW = jnp.bfloat16

NN = (((1,), (0,)), ((), ()))
NT = (((1,), (1,)), ((), ()))
TN = (((0,), (0,)), ((), ()))


def mm(left, right, dims=NN):
    return lax.dot_general(left, right, dims, preferred_element_type=F32)


def whole(*shape):
    return pl.BlockSpec(shape, lambda t, _: (0,) * len(shape))


def part(*shape):
    return pl.BlockSpec((1,) + shape, lambda t, _: (t,) + (0,) * len(shape))


def columns(rows, width, at):
    return pl.BlockSpec((1, rows, width), lambda t, _: (t, 0, at))


def call(body, grid, where, ins, outs, args, scratch=(), flops=0, moved=0, exps=0):
    return pl.pallas_call(
        body,
        grid_spec=pltpu.PrefetchScalarGridSpec(
            num_scalar_prefetch=1,
            grid=(grid,),
            in_specs=ins,
            out_specs=[spec for spec, _, _ in outs],
            scratch_shapes=list(scratch),
        ),
        out_shape=[jax.ShapeDtypeStruct(shape, kind) for _, shape, kind in outs],
        compiler_params=pltpu.CompilerParams(
            dimension_semantics=("arbitrary",), vmem_limit_bytes=48 << 20
        ),
        cost_estimate=pl.CostEstimate(flops=flops, bytes_accessed=moved, transcendentals=exps),
    )(where, *args)


def layer_norm(values, gain, shift):
    center = values - jnp.mean(values, axis=-1, keepdims=True)
    spread = jnp.mean(center * center, axis=-1, keepdims=True)
    return center * lax.rsqrt(spread + EPSILON) * gain + shift


def layer_norm_back(values, gain, grad):
    center = values - jnp.mean(values, axis=-1, keepdims=True)
    scale = lax.rsqrt(jnp.mean(center * center, axis=-1, keepdims=True) + EPSILON)
    unit = center * scale
    scaled = grad * gain
    back = scale * (
        scaled
        - jnp.mean(scaled, axis=-1, keepdims=True)
        - unit * jnp.mean(scaled * unit, axis=-1, keepdims=True)
    )
    return back, row_sum(grad * unit), row_sum(grad)


def row_sum(values):
    return jnp.sum(values, axis=0, keepdims=True)


def shards_body(where_ref, qkv_ref, out_ref, up_ref, down_ref, a_ref, f_ref):
    width = qkv_ref.shape[2]
    hidden = up_ref.shape[1]
    for piece in range(3):
        a_ref[:, piece * width : (piece + 1) * width] = qkv_ref[:, piece, :].astype(LOW)
    a_ref[:, 3 * width :] = out_ref[...].T.astype(LOW)
    f_ref[:, :hidden] = up_ref[...].astype(LOW)
    f_ref[:, hidden:] = down_ref[...].T.astype(LOW)


def shards(where, w_qkv, w_out, w_up, w_down):
    rows, _, width = w_qkv.shape
    hidden = w_up.shape[1] // 2
    return call(
        shards_body,
        1,
        where,
        [
            whole(rows, 3, width),
            whole(width, rows),
            pl.BlockSpec((rows, hidden), lambda t, at: (0, at[0])),
            pl.BlockSpec((hidden, rows), lambda t, at: (at[0], 0)),
        ],
        [
            (whole(rows, 4 * width), (rows, 4 * width), LOW),
            (whole(rows, 2 * hidden), (rows, 2 * hidden), LOW),
        ],
        (w_qkv, w_out, w_up, w_down),
        moved=6 * rows * (4 * width + 2 * hidden),
    )


def attention_body(
    where_ref,
    own_ref,
    far_ref,
    w_ref,
    wo_ref,
    b_ref,
    keep_ref,
    bo_ref,
    g1_ref,
    s1_ref,
    g2_ref,
    s2_ref,
    n1_ref,
    p_ref,
    o_ref,
    l_ref,
    y_ref,
    n2_ref,
):
    width = o_ref.shape[2]
    half = own_ref.shape[0]
    step = pl.program_id(0)

    @pl.when(step == 0)
    def _():
        for at, ref in ((0, own_ref), (half, far_ref)):
            tokens = ref[...].astype(F32)
            n1_ref[at : at + half] = layer_norm(tokens, g1_ref[...], s1_ref[...]).astype(LOW)
            y_ref[at : at + half] = tokens + bo_ref[...]

    low = (mm(n1_ref[...], w_ref[0]) + b_ref[0]).astype(LOW)
    p_ref[0] = low
    keep = keep_ref[...] > 0
    for head in range(width // HEAD):
        at = head * HEAD
        query = low[:, at : at + HEAD]
        key = low[:, width + at : width + at + HEAD]
        value = low[:, 2 * width + at : 2 * width + at + HEAD]
        scores = jnp.where(keep, mm(key, query, NT) * HEAD**-0.5, -1e30)
        top = jnp.max(scores, axis=0, keepdims=True)
        exponent = jnp.exp(scores - top)
        total = jnp.sum(exponent, axis=0, keepdims=True)
        probability = (exponent * (1.0 / total)).astype(LOW)
        o_ref[0, :, at : at + HEAD] = mm(probability, value, TN).astype(LOW)
        l_ref[0, head : head + 1, :] = top + jnp.log(total)
    y_ref[...] += mm(o_ref[0], wo_ref[0], NT)

    @pl.when(step == pl.num_programs(0) - 1)
    def _():
        n2_ref[...] = layer_norm(y_ref[...], g2_ref[...], s2_ref[...]).astype(LOW)


def attention(where, own, far, weights, bias, keep, b_out, norms):
    parts, wide, width4 = weights.shape
    width = width4 // 4
    half = own.shape[0]
    rows = 2 * half
    heads = width // HEAD
    return call(
        attention_body,
        parts,
        where,
        [
            whole(half, wide),
            whole(half, wide),
            columns(wide, 3 * width, 0),
            columns(wide, width, 3),
            part(1, 3 * width),
            whole(rows, 1),
        ]
        + [whole(1, wide)] * 5,
        [
            (whole(rows, wide), (rows, wide), LOW),
            (part(rows, 3 * width), (parts, rows, 3 * width), LOW),
            (part(rows, width), (parts, rows, width), LOW),
            (part(heads, rows), (parts, heads, rows), F32),
            (whole(rows, wide), (rows, wide), F32),
            (whole(rows, wide), (rows, wide), LOW),
        ],
        (own, far, weights, weights, bias, keep, b_out, *norms),
        flops=2 * parts * rows * wide * width4 + 4 * parts * rows * rows * width,
        moved=2 * weights.size + 12 * rows * wide,
        exps=parts * heads * rows * rows,
    )


def up_body(where_ref, own_ref, far_ref, w_ref, b_ref, a_ref, s_ref, both_ref):
    half = own_ref.shape[0]

    @pl.when(pl.program_id(0) == 0)
    def _():
        both_ref[:half] = own_ref[...]
        both_ref[half:] = far_ref[...]

    hidden = mm(both_ref[...], w_ref[0]) + b_ref[0]
    bell = 0.5 * (1.0 + lax.erf(hidden * 0.5**0.5))
    a_ref[0] = (hidden * bell).astype(LOW)
    slope = bell + hidden * jnp.exp(hidden * hidden * -0.5) * 0.3989422804014327
    s_ref[0] = slope.astype(LOW)


def up_product(where, own, far, weights, bias):
    parts, wide, width2 = weights.shape
    width = width2 // 2
    rows = 2 * own.shape[0]
    shape = (parts, rows, width)
    return call(
        up_body,
        parts,
        where,
        [
            whole(rows // 2, wide),
            whole(rows // 2, wide),
            columns(wide, width, 0),
            part(1, width),
        ],
        [(part(rows, width), shape, LOW), (part(rows, width), shape, LOW)],
        (own, far, weights, bias),
        [pltpu.VMEM((rows, wide), LOW)],
        flops=2 * parts * rows * wide * width,
        moved=weights.size + 4 * parts * rows * width,
        exps=2 * parts * rows * width,
    )


def down_body(
    where_ref,
    a_ref,
    wd_ref,
    g_ref,
    s_ref,
    wu_ref,
    y_ref,
    du_ref,
    db_ref,
    keep_ref,
    send_ref,
    dn_keep_ref,
    dn_send_ref,
    r_ref,
    dn_ref,
):
    step = pl.program_id(0)
    rows = y_ref.shape[0]
    half = rows // 2
    low = (mm(g_ref[...], wd_ref[0]) * s_ref[0].astype(F32)).astype(LOW)
    du_ref[0] = low
    db_ref[0] = row_sum(low.astype(F32))
    branch = mm(a_ref[0], wd_ref[0], NT)
    grad_normed = mm(low, wu_ref[0], NT)

    @pl.when(step == 0)
    def _():
        r_ref[...] = branch
        dn_ref[...] = grad_normed

    @pl.when(step > 0)
    def _():
        r_ref[...] += branch
        dn_ref[...] += grad_normed

    @pl.when(step == pl.num_programs(0) - 1)
    def _():
        keep_ref[:half] = y_ref[:half] + r_ref[:half]
        keep_ref[half:] = r_ref[rows + half :]
        send_ref[:half] = (y_ref[half:] + r_ref[half:rows]).astype(LOW)
        send_ref[half:] = r_ref[rows : rows + half].astype(LOW)
        dn_keep_ref[...] = dn_ref[:rows]
        dn_send_ref[...] = dn_ref[rows:].astype(LOW)


def down_product(where, active, weights, grad, slope, residual):
    parts, rows, width = active.shape
    wide = weights.shape[1]
    mine = rows // 2
    return call(
        down_body,
        parts,
        where,
        [
            part(rows, width),
            columns(wide, width, 1),
            whole(rows, wide),
            part(rows, width),
            columns(wide, width, 0),
            whole(mine, wide),
        ],
        [
            (part(rows, width), (parts, rows, width), LOW),
            (part(1, width), (parts, 1, width), F32),
            (whole(mine, wide), (mine, wide), F32),
            (whole(mine, wide), (mine, wide), LOW),
            (whole(mine, wide), (mine, wide), F32),
            (whole(mine, wide), (mine, wide), LOW),
        ],
        (active, weights, grad, slope, weights, residual),
        [pltpu.VMEM((rows, wide), F32), pltpu.VMEM((rows, wide), F32)],
        flops=6 * parts * rows * width * wide,
        moved=2 * weights.size + 6 * parts * rows * width + 8 * rows * wide,
    )


def weight_body(where_ref, xa_ref, xb_ref, z_ref, ya_ref, yb_ref, *rest):
    *outs, turned_ref, second_ref = rest
    near = xa_ref.shape[0]

    @pl.when(pl.program_id(0) == 0)
    def _():
        turned_ref[:, :near] = xa_ref[...].T
        if xb_ref.shape[0] == near:
            turned_ref[:, near:] = xb_ref[...].T
        second_ref[...] = z_ref[...].T

    at = ya_ref.shape[2]
    if len(outs) == 1:
        used = ya_ref.shape[1]
        outs[0][0, :, :at] = mm(turned_ref[:, :used], ya_ref[0]).astype(LOW)
        outs[0][0, :, at:] = mm(second_ref[...], yb_ref[0]).astype(LOW)
        return
    core, row = where_ref[1], where_ref[2]
    rows = outs[0].shape[2]
    used = ya_ref.shape[1]
    for which, out_ref in enumerate(outs):
        for far in range(2):
            owner = 2 * (row + far - 2 * row * far) + (core + which - 2 * core * which)
            span = pl.ds(pl.multiple_of(owner * rows, rows), rows)
            out_ref[far, 0, :, :at] = mm(turned_ref[span, :used], ya_ref[0]).astype(LOW)
            out_ref[far, 0, :, at:] = mm(second_ref[span, :], yb_ref[0]).astype(LOW)


def weight_product(where, first, second, left, right, owners):
    parts, rows, width = left.shape
    other = right.shape[2]
    wide = second.shape[1]
    xa, xb = first if len(first) == 2 else (first[0], jnp.zeros((8, wide), LOW))
    total = width + other
    if owners == 4:
        block = pl.BlockSpec(
            (2, 1, wide // 4, total), lambda t, at: (0, lax.rem(t - at[3] + parts, parts), 0, 0)
        )
        outs = [(block, (2, parts, wide // 4, total), LOW)] * 2
    else:
        outs = [(part(wide, total), (parts, wide, total), LOW)]
    return call(
        weight_body,
        parts,
        where,
        [
            whole(*xa.shape),
            whole(*xb.shape),
            whole(*second.shape),
            part(rows, width),
            part(right.shape[1], other),
        ],
        outs,
        (xa, xb, second, left, right),
        [pltpu.VMEM((wide, rows), LOW), pltpu.VMEM((wide, second.shape[0]), LOW)],
        flops=2 * parts * wide * (rows * width + right.shape[1] * other),
        moved=2 * parts * wide * total + 4 * parts * rows * total,
    )


def back_body(
    where_ref,
    y_ref,
    dn_keep_ref,
    dn_came_ref,
    gm_ref,
    g2_ref,
    wo_ref,
    p_ref,
    l_ref,
    keep_ref,
    w_ref,
    own_ref,
    far_ref,
    g1_ref,
    dyb_ref,
    dp_ref,
    db_ref,
    sums_ref,
    gi_own_ref,
    gi_far_ref,
    dy_ref,
    dn_ref,
):
    width = wo_ref.shape[2]
    step = pl.program_id(0)
    half = own_ref.shape[0]

    @pl.when(step == 0)
    def _():
        grad_normed = dn_keep_ref[...] + dn_came_ref[...].astype(F32)
        back, gain_sum, shift_sum = layer_norm_back(y_ref[...], g2_ref[...], grad_normed)
        grad_out = gm_ref[...].astype(F32)
        grad_residual = grad_out + back
        dy_ref[...] = grad_residual
        dyb_ref[...] = grad_residual.astype(LOW)
        sums_ref[0:1] = row_sum(dyb_ref[...].astype(F32))
        sums_ref[1:2] = row_sum(grad_out)
        sums_ref[2:3] = gain_sum
        sums_ref[3:4] = shift_sum
        dn_ref[...] = jnp.zeros_like(dn_ref)

    grad_mixed = mm(dyb_ref[...], wo_ref[0]).astype(LOW)
    keep = keep_ref[...] > 0
    for head in range(width // HEAD):
        at = head * HEAD
        query = p_ref[0, :, at : at + HEAD]
        key = p_ref[0, :, width + at : width + at + HEAD]
        value = p_ref[0, :, 2 * width + at : 2 * width + at + HEAD]
        grad = grad_mixed[:, at : at + HEAD]
        scores = jnp.where(keep, mm(key, query, NT) * HEAD**-0.5, -1e30)
        probability = jnp.exp(scores - l_ref[0, head : head + 1, :])
        grad_probability = mm(value, grad, NT)
        grad_value = mm(probability.astype(LOW), grad)
        inner = jnp.sum(grad_probability * probability, axis=0, keepdims=True)
        grad_scores = (probability * (grad_probability - inner)).astype(LOW)
        grad_query = mm(grad_scores, key, TN) * HEAD**-0.5
        grad_key = mm(grad_scores, query) * HEAD**-0.5
        dp_ref[0, :, at : at + HEAD] = grad_query.astype(LOW)
        dp_ref[0, :, width + at : width + at + HEAD] = grad_key.astype(LOW)
        dp_ref[0, :, 2 * width + at : 2 * width + at + HEAD] = grad_value.astype(LOW)
    db_ref[0] = row_sum(dp_ref[0].astype(F32))
    dn_ref[...] += mm(dp_ref[0], w_ref[0], NT)

    @pl.when(step == pl.num_programs(0) - 1)
    def _():
        gain_sum = shift_sum = 0.0
        for at, ref, out_ref in ((0, own_ref, gi_own_ref), (half, far_ref, gi_far_ref)):
            back, gain_add, shift_add = layer_norm_back(
                ref[...].astype(F32), g1_ref[...], dn_ref[at : at + half]
            )
            out_ref[...] = (dy_ref[at : at + half] + back).astype(LOW)
            gain_sum, shift_sum = gain_sum + gain_add, shift_sum + shift_add
        sums_ref[4:5] = gain_sum
        sums_ref[5:6] = shift_sum
        sums_ref[6:8] = jnp.zeros((2, sums_ref.shape[1]), F32)


def attention_back(
    where, residual, dn_keep, dn_came, grad, gain_two, weights, projected, logs, keep, own, far, gain
):
    parts, wide, width4 = weights.shape
    width = width4 // 4
    half = own.shape[0]
    rows = 2 * half
    heads = width // HEAD
    return call(
        back_body,
        parts,
        where,
        [
            whole(rows, wide),
            whole(rows, wide),
            whole(rows, wide),
            whole(rows, wide),
            whole(1, wide),
            columns(wide, width, 3),
            part(rows, 3 * width),
            part(heads, rows),
            whole(rows, 1),
            columns(wide, 3 * width, 0),
            whole(half, wide),
            whole(half, wide),
            whole(1, wide),
        ],
        [
            (whole(rows, wide), (rows, wide), LOW),
            (part(rows, 3 * width), (parts, rows, 3 * width), LOW),
            (part(1, 3 * width), (parts, 1, 3 * width), F32),
            (whole(8, wide), (8, wide), F32),
            (whole(half, wide), (half, wide), LOW),
            (whole(half, wide), (half, wide), LOW),
        ],
        (
            residual,
            dn_keep,
            dn_came,
            grad,
            gain_two,
            weights,
            projected,
            logs,
            keep,
            weights,
            own,
            far,
            gain,
        ),
        [pltpu.VMEM((rows, wide), F32), pltpu.VMEM((rows, wide), F32)],
        flops=2 * parts * rows * wide * width4 + 10 * parts * rows * rows * width,
        moved=2 * weights.size + 16 * parts * rows * width + 16 * rows * wide,
        exps=parts * heads * rows * rows,
    )


def on_device(
    inputs,
    cotangent,
    visible,
    w_qkv,
    b_qv,
    w_out,
    b_out,
    w_up,
    b_up,
    w_down,
    b_down,
    gain_one,
    shift_one,
    gain_two,
    shift_two,
):
    images, half, wide = inputs.shape
    ctx_at, tp_at, fsdp_at = (lax.axis_index(name) for name in ("ctx", "tp", "fsdp"))
    blocks, parts, owners = (lax.axis_size(name) for name in ("ctx", "tp", "fsdp"))
    assert blocks == 2 and images == blocks * parts
    first = blocks * tp_at
    mine, other = first + ctx_at, first + 1 - ctx_at
    where = jnp.stack([ctx_at, fsdp_at % 2, fsdp_at // 2, tp_at]).astype(jnp.int32)
    heads_width = w_qkv.shape[2]
    hidden_half = w_up.shape[1] // 2
    rows = 2 * half

    def swap(values):
        return lax.ppermute(values, "ctx", [(0, 1), (1, 0)])

    def pick(values, index):
        return lax.dynamic_index_in_dim(values, index, 0, keepdims=False)

    def in_order(own, received):
        return jnp.where(ctx_at == 0, own, received), jnp.where(ctx_at == 0, received, own)

    def gather(shard):
        full = lax.all_gather(shard, ("tp", "fsdp"), axis=0, tiled=True)
        return full.reshape(parts, wide, shard.shape[1])

    attention_shard, forward_shard = shards(where, w_qkv, w_out, w_up, w_down)
    attention_w = gather(attention_shard)
    attention_w, forward_shard = lax.optimization_barrier((attention_w, forward_shard))
    forward_w = gather(forward_shard)
    biases = lax.all_gather(jnp.concatenate([b_qv.reshape(-1), b_up]), "tp", axis=0)
    bias_q, bias_v = biases[:, :heads_width], biases[:, heads_width : 2 * heads_width]
    qkv_bias = jnp.concatenate([bias_q, jnp.zeros_like(bias_q), bias_v], axis=1)[:, None]
    up_bias = lax.dynamic_slice_in_dim(
        biases, 2 * heads_width + ctx_at * hidden_half, hidden_half, 1
    )[:, None]

    own = pick(inputs, mine)
    far = swap(pick(inputs, other))
    cot_pair = jnp.stack([pick(cotangent, mine), pick(cotangent, other)])
    cot_swapped = swap(cot_pair)
    mine_seen = pick(visible, mine).reshape(blocks, half)
    other_seen = pick(visible, other).reshape(blocks, half)
    keep = jnp.concatenate([pick(mine_seen, ctx_at), pick(mine_seen, 1 - ctx_at)])
    keep_other = jnp.concatenate([pick(other_seen, 1 - ctx_at), pick(other_seen, ctx_at)])
    keep, keep_other = keep[:, None], keep_other[:, None]
    keep_all = jnp.concatenate([keep, keep_other]).astype(LOW)
    grad_low = (
        jnp.concatenate([cot_pair[0], cot_swapped[1], cot_swapped[0], cot_pair[1]]) * keep_all
    )

    norms = (gain_one[None], shift_one[None], gain_two[None], shift_two[None])
    normed, projected, mixed, logs, residual, normed_two = attention(
        where, own, far, attention_w, qkv_bias, keep, b_out[None], norms
    )
    normed_far = swap(normed_two)
    active, slope = up_product(where, normed_two, normed_far, forward_w, up_bias)
    grad_hidden, up_bias_grad, out_keep, out_send, dn_keep, dn_send = down_product(
        where, active, forward_w, grad_low, slope, residual
    )
    dn_came = swap(dn_send)
    forward_grads = weight_product(
        where, (normed_two, normed_far), grad_low, grad_hidden, active, owners
    )

    out_came = swap(out_send).astype(F32)
    seen = jnp.concatenate([keep[:half], keep_other[half:]]).astype(F32)
    out_rows = out_keep + jnp.concatenate([out_came[half:], out_came[:half]]) + b_down
    out_rows = (out_rows * seen).astype(LOW)
    out_pair = jnp.stack(in_order(out_rows[:half], out_rows[half:]))
    result = lax.all_gather(out_pair, "tp", axis=0, tiled=True).astype(F32)

    grad_attended, grad_projected, qkv_bias_grad, sums, gi_own, gi_far = attention_back(
        where,
        residual,
        dn_keep,
        dn_came,
        grad_low[:rows],
        gain_two[None],
        attention_w,
        projected,
        logs,
        keep,
        own,
        far,
        gain_one[None],
    )
    grad_in_pair = jnp.stack(in_order(gi_own, swap(gi_far)))
    grad_inputs = lax.all_gather(grad_in_pair, "tp", axis=0, tiled=True).astype(F32)
    attention_grads = weight_product(
        where, (normed,), grad_attended, grad_projected, mixed, owners
    )

    def scatter(grads):
        if len(grads) == 1:
            flat = grads[0].reshape(-1, grads[0].shape[2])
            return lax.psum_scatter(flat, ("tp", "fsdp"), scatter_dimension=0, tiled=True)
        keep, send = grads
        came = lax.ppermute(send, "fsdp", [(0, 1), (1, 0), (2, 3), (3, 2)])
        lift = (keep[1].astype(F32) + came[1].astype(F32)).astype(LOW)
        lift = lax.ppermute(lift, "fsdp", [(0, 2), (2, 0), (1, 3), (3, 1)])

        def own_part(at):
            return keep[0, at].astype(F32) + came[0, at].astype(F32) + lift[at].astype(F32)

        total = own_part(parts - 1)
        for at in range(parts - 2, -1, -1):
            moved = lax.ppermute(
                total.astype(LOW), "tp", [(i, (i + 1) % parts) for i in range(parts)]
            )
            total = own_part(at) + moved.astype(F32)
        return total.astype(LOW)

    forward_own = scatter(forward_grads)
    forward_far = swap(forward_own)
    up_total = jnp.concatenate(
        in_order(forward_own[:, :hidden_half], forward_far[:, :hidden_half]), axis=1
    ).astype(F32)
    down_total = jnp.concatenate(
        in_order(forward_own[:, hidden_half:], forward_far[:, hidden_half:]), axis=1
    ).astype(F32)
    attention_own = scatter(attention_grads)
    attention_total = attention_own.astype(F32) + swap(attention_own).astype(F32)

    up_bias_slot = lax.dynamic_update_slice(
        jnp.zeros((parts, 2, hidden_half), F32), up_bias_grad, (0, ctx_at, 0)
    )
    small = jnp.concatenate(
        [
            sums[:6],
            up_bias_slot.reshape(-1, wide),
            qkv_bias_grad.reshape(-1, wide),
        ]
    )
    if owners == 4 and parts == 4:
        for axis, pairs in (
            ("fsdp", [(0, 1), (1, 0), (2, 3), (3, 2)]),
            ("fsdp", [(0, 2), (2, 0), (1, 3), (3, 1)]),
            ("ctx", [(0, 1), (1, 0)]),
            ("tp", [(0, 1), (1, 0), (2, 3), (3, 2)]),
            ("tp", [(0, 2), (2, 0), (1, 3), (3, 1)]),
        ):
            small = small + lax.ppermute(small, axis, pairs)
    else:
        small = lax.psum(small, ("fsdp", "ctx", "tp"))
    up_rows = parts * 2 * hidden_half // wide
    up_small = small[6 : 6 + up_rows].reshape(parts, 2 * hidden_half)
    qkv_small = small[6 + up_rows :].reshape(parts, 3, heads_width)
    return (
        result,
        grad_inputs,
        attention_total[:, : 3 * heads_width].reshape(-1, 3, heads_width),
        pick(qkv_small, tp_at)[0::2],
        attention_total[:, 3 * heads_width :].T,
        small[0],
        up_total,
        pick(up_small, tp_at),
        down_total.T,
        small[1],
        small[4],
        small[5],
        small[2],
        small[3],
    )


def solution(mesh):
    placed = (
        P("fsdp", "ctx", None),
        P("fsdp", "ctx", None),
        P("fsdp", None),
        P("fsdp", None, "tp"),
        P(None, "tp"),
        P("tp", "fsdp"),
        P(),
        P("fsdp", "tp"),
        P("tp"),
        P("tp", "fsdp"),
        P(),
        P(),
        P(),
        P(),
        P(),
    )
    return jax.shard_map(
        on_device,
        mesh=mesh,
        in_specs=placed,
        out_specs=(
            P("fsdp", "ctx", None),
            P("fsdp", "ctx", None),
            P("fsdp", None, "tp"),
            P(None, "tp"),
            P("tp", "fsdp"),
            P(),
            P("fsdp", "tp"),
            P("tp"),
            P("tp", "fsdp"),
            P(),
            P(),
            P(),
            P(),
            P(),
        ),
        check_vma=False,
    )
```

```python
import types

import jax
import jax.numpy as jnp
from jax import lax
from jax.experimental import pallas as pl
from jax.experimental.pallas import tpu as pltpu
from jax.sharding import PartitionSpec as P

HEAD = 64
EPSILON = 1e-06
EXTRA = 16
F32 = jnp.float32
LOW = jnp.bfloat16

NN = (((1,), (0,)), ((), ()))
NT = (((1,), (1,)), ((), ()))
TN = (((0,), (0,)), ((), ()))


def mm(left, right, dims=NN):
    return lax.dot_general(left, right, dims, preferred_element_type=F32)


def whole(*shape):
    return pl.BlockSpec(shape, lambda t, _: (0,) * len(shape))


def part(*shape):
    return pl.BlockSpec((1,) + shape, lambda t, _: (t,) + (0,) * len(shape))


def call(body, grid, where, ins, outs, scratch=(), pieces=(), flops=0, moved=0, exps=0):
    names = [entry[0] for entry in ins]
    later = [entry[0] for entry in outs] + [entry[0] for entry in scratch]

    def kernel(where_ref, *refs):
        r = types.SimpleNamespace(where=where_ref)
        count = len(names) + len(pieces)
        r.pieces = refs[len(names) : count]
        for name, ref in zip(names + later, refs[: len(names)] + refs[count:]):
            setattr(r, name, ref)
        body(r)

    results = pl.pallas_call(
        kernel,
        grid_spec=pltpu.PrefetchScalarGridSpec(
            num_scalar_prefetch=1,
            grid=(grid,),
            in_specs=[entry[1] for entry in ins]
            + [pl.BlockSpec(memory_space=pltpu.HBM)] * len(pieces),
            out_specs=[entry[1] for entry in outs],
            scratch_shapes=[entry[1] for entry in scratch],
        ),
        out_shape=[jax.ShapeDtypeStruct(entry[2], entry[3]) for entry in outs],
        compiler_params=pltpu.CompilerParams(
            dimension_semantics=("arbitrary",), vmem_limit_bytes=56 << 20
        ),
        cost_estimate=pl.CostEstimate(flops=flops, bytes_accessed=moved, transcendentals=exps),
    )(where, *(entry[2] for entry in ins), *pieces)
    return types.SimpleNamespace(**{entry[0]: value for entry, value in zip(outs, results)})


def at_step(step):
    return pl.when(pl.program_id(0) == step)


def at_end():
    return pl.when(pl.program_id(0) == pl.num_programs(0) - 1)


def layer_norm(values, gain, shift):
    center = values - jnp.mean(values, axis=-1, keepdims=True)
    spread = jnp.mean(center * center, axis=-1, keepdims=True)
    return center * lax.rsqrt(spread + EPSILON) * gain + shift


def layer_norm_back(values, gain, grad):
    center = values - jnp.mean(values, axis=-1, keepdims=True)
    scale = lax.rsqrt(jnp.mean(center * center, axis=-1, keepdims=True) + EPSILON)
    unit = center * scale
    scaled = grad * gain
    back = scale * (
        scaled
        - jnp.mean(scaled, axis=-1, keepdims=True)
        - unit * jnp.mean(scaled * unit, axis=-1, keepdims=True)
    )
    return back, row_sum(grad * unit), row_sum(grad)


def row_sum(values):
    return jnp.sum(values, axis=0, keepdims=True)


def fetch_scratch(pieces, width, parts, wide):
    copies = pieces[0].shape[1] if len(pieces) == 1 else 4
    return [
        ("weights", pltpu.VMEM((parts, wide, width), LOW)),
        ("extras", pltpu.VMEM((parts, EXTRA, width), LOW)),
        ("sems", pltpu.SemaphoreType.DMA((parts, copies + 1))),
    ]


def fetch(r):
    parts = r.weights.shape[0]

    def copies(at):
        if len(r.pieces) == 1:
            sources = [r.pieces[0].at[at, owner] for owner in range(r.pieces[0].shape[1])]
            owners = list(range(len(sources)))
        else:
            core, row = r.where[1], r.where[2]
            sources = [r.pieces[4 * at + which] for which in range(4)]
            owners = [
                2 * (row + up - 2 * row * up) + (core + over - 2 * core * over)
                for over in range(2)
                for up in range(2)
            ]
        rows = sources[0].shape[0] - EXTRA
        extra = sources[0].at[pl.ds(rows, EXTRA), :]
        result = [pltpu.make_async_copy(extra, r.extras.at[at], r.sems.at[at, len(sources)])]
        for which, (source, owner) in enumerate(zip(sources, owners)):
            target = r.weights.at[at, pl.ds(pl.multiple_of(owner * rows, rows), rows), :]
            result.append(
                pltpu.make_async_copy(source.at[pl.ds(0, rows), :], target, r.sems.at[at, which])
            )
        return result

    @at_step(0)
    def _():
        for at in range(parts):
            for copy in copies(at):
                copy.start()

    def wait(at):
        @at_step(at)
        def _():
            for copy in copies(at):
                copy.wait()

    for at in range(parts):
        wait(at)
    return r.weights.at[pl.program_id(0)], r.extras.at[pl.program_id(0)]


def joined(terms):
    wide = terms.astype(F32)
    return wide[0:1] + (wide[1:2] + wide[2:3])


def gradient_outs(parts, wide, total, stepwise):
    if not stepwise:
        return [("gradient", part(wide, total), (parts, wide, total), LOW)]
    shape = (2, parts, wide // 4, total)
    block = pl.BlockSpec((2, 1, wide // 4, total), lambda t, _: (0, t, 0, 0))
    return [("kept", block, shape, LOW), ("sent", block, shape, LOW)]


def store_gradient(r, pairs):
    column = 0
    for turned, right in pairs:
        span = slice(column, column + right.shape[1])
        column += right.shape[1]
        if hasattr(r, "gradient"):
            r.gradient[0, :, span] = mm(turned[...], right).astype(LOW)
            continue
        core, row = r.where[1], r.where[2]
        rows = r.kept.shape[2]
        for which, out in enumerate((r.kept, r.sent)):
            for far in range(2):
                owner = 2 * (row + far - 2 * row * far) + (core + which - 2 * core * which)
                start = pl.multiple_of(owner * rows, rows)
                out[far, 0, :, span] = mm(turned[pl.ds(start, rows), :], right).astype(LOW)


def shards_body(r):
    rows, width = r.qkv.shape[1:]
    hidden = r.up.shape[1]
    for piece in range(3):
        r.a[:rows, piece * width : (piece + 1) * width] = r.qkv[piece].astype(LOW)
    r.a[:rows, 3 * width :] = r.out[...].T.astype(LOW)
    r.f[:rows, :hidden] = r.up[...].astype(LOW)
    r.f[:rows, hidden:] = r.down[...].T.astype(LOW)
    r.a[rows:] = jnp.zeros((EXTRA, 4 * width), LOW)
    r.f[rows:] = jnp.zeros((EXTRA, 2 * hidden), LOW)
    for ref, row, shard in ((r.bqv, 0, r.a), (r.bqv, 1, r.a), (r.bup, 0, r.f)):
        left = ref[row : row + 1, :]
        for piece in range(3):
            low = left.astype(LOW)
            left = left - low.astype(F32)
            at = rows + 3 * row + piece
            shard[at : at + 1, : low.shape[1]] = low


def shards(where, w_qkv, w_out, w_up, w_down, b_qv, b_up):
    _, rows, width = w_qkv.shape
    hidden = w_up.shape[1] // 2
    got = call(
        shards_body,
        1,
        where,
        [
            ("qkv", whole(3, rows, width), w_qkv),
            ("out", whole(width, rows), w_out),
            ("up", pl.BlockSpec((rows, hidden), lambda t, at: (0, at[0])), w_up),
            ("down", pl.BlockSpec((hidden, rows), lambda t, at: (at[0], 0)), w_down),
            ("bqv", whole(2, width), b_qv),
            ("bup", pl.BlockSpec((1, hidden), lambda t, at: (0, at[0])), b_up[None]),
        ],
        [
            ("a", whole(rows + EXTRA, 4 * width), (rows + EXTRA, 4 * width), LOW),
            ("f", whole(rows + EXTRA, 2 * hidden), (rows + EXTRA, 2 * hidden), LOW),
        ],
        moved=6 * rows * (4 * width + 2 * hidden),
    )
    return got.a, got.f


def attention(where, pieces, parts, keep, first, carried, last):
    rows = keep.shape[0]
    half = rows // 2
    width = pieces[0].shape[-1] // 4
    heads = width // HEAD
    wide = first[0].shape[1] if first else carried[0].shape[1]

    def body(r):
        w, extra = fetch(r)
        normed = r.n1_out if first else r.n1

        @at_step(0)
        def _():
            if not first:
                r.y_out[...] = r.y[...]
                return
            for at, ref in ((0, r.own), (half, r.far)):
                tokens = ref[...].astype(F32)
                normed[at : at + half] = layer_norm(tokens, r.g1[...], r.s1[...]).astype(LOW)
                r.y_out[at : at + half] = tokens + r.b_out[...]

        terms = extra[...]
        bias_q, bias_v = joined(terms[0:3, :width]), joined(terms[3:6, :width])
        bias = jnp.concatenate([bias_q, jnp.zeros_like(bias_q), bias_v], axis=1)
        low = (mm(normed[...], w[:, : 3 * width]) + bias).astype(LOW)
        r.p[0] = low
        seen = r.keep[...] > 0
        for head in range(heads):
            at = head * HEAD
            query = low[:, at : at + HEAD]
            key = low[:, width + at : width + at + HEAD]
            value = low[:, 2 * width + at : 2 * width + at + HEAD]
            scores = jnp.where(seen, mm(key, query, NT) * HEAD**-0.5, -1e30)
            top = jnp.max(scores, axis=0, keepdims=True)
            exponent = jnp.exp(scores - top)
            total = jnp.sum(exponent, axis=0, keepdims=True)
            probability = (exponent * (1.0 / total)).astype(LOW)
            r.o[0, :, at : at + HEAD] = mm(probability, value, TN).astype(LOW)
            r.l[0, head : head + 1, :] = top + jnp.log(total)
        r.y_out[...] += mm(r.o[0], w[:, 3 * width :], NT)

        if last:

            @at_end()
            def _():
                r.n2[...] = layer_norm(r.y_out[...], r.g2[...], r.s2[...]).astype(LOW)

    line = whole(1, wide)
    ins = [("keep", whole(rows, 1), keep)]
    outs = [
        ("p", part(rows, 3 * width), (parts, rows, 3 * width), LOW),
        ("o", part(rows, width), (parts, rows, width), LOW),
        ("l", part(heads, rows), (parts, heads, rows), F32),
        ("y_out", whole(rows, wide), (rows, wide), F32),
    ]
    if first:
        specs = [whole(half, wide)] * 2 + [line] * 3
        ins += list(zip(("own", "far", "b_out", "g1", "s1"), specs, first))
        outs.append(("n1_out", whole(rows, wide), (rows, wide), LOW))
    else:
        ins += list(zip(("n1", "y"), [whole(rows, wide)] * 2, carried))
    if last:
        ins += list(zip(("g2", "s2"), [line] * 2, last))
        outs.append(("n2", whole(rows, wide), (rows, wide), LOW))
    return call(
        body,
        parts,
        where,
        ins,
        outs,
        fetch_scratch(pieces, 4 * width, parts, wide),
        pieces,
        flops=8 * parts * rows * wide * width + 4 * parts * rows * rows * width,
        moved=8 * parts * wide * width + 12 * rows * wide,
        exps=parts * heads * rows * rows,
    )


def forward(where, pieces, parts, own, far, grad, carried, residual, stepwise):
    rows, wide = own.shape
    half = rows // 2
    width = pieces[0].shape[-1] // 2

    def body(r):
        w, extra = fetch(r)

        @at_step(0)
        def _():
            r.both[:rows] = r.own[...]
            r.both[rows:] = r.far[...]
            r.turned[...] = r.both[...].T
            r.turned_grad[...] = r.grad[...].T
            r.branch_sum[...] = r.branch_in[...] if carried else jnp.zeros((2 * rows, wide), F32)
            r.grad_sum[...] = r.grad_in[...] if carried else jnp.zeros((2 * rows, wide), F32)

        hidden = mm(r.both[...], w[:, :width]) + joined(extra[0:3, :width])
        bell = 0.5 * (1.0 + lax.erf(hidden * 0.5**0.5))
        active = (hidden * bell).astype(LOW)
        slope = bell + hidden * jnp.exp(hidden * hidden * -0.5) * 0.3989422804014327
        r.branch_sum[...] += mm(active, w[:, width:], NT)
        grad_hidden = (mm(r.grad[...], w[:, width:]) * slope).astype(LOW)
        r.db[0] = row_sum(grad_hidden.astype(F32))
        r.grad_sum[...] += mm(grad_hidden, w[:, :width], NT)
        store_gradient(r, [(r.turned, grad_hidden), (r.turned_grad, active)])

        if residual is None:
            return

        @at_end()
        def _():
            r.out_keep[:half] = r.y[:half] + r.branch_sum[:half]
            r.out_keep[half:] = r.branch_sum[rows + half :]
            r.out_send[:half] = (r.y[half:] + r.branch_sum[half:rows]).astype(LOW)
            r.out_send[half:] = r.branch_sum[rows : rows + half].astype(LOW)
            r.dn_keep[...] = r.grad_sum[:rows]
            r.dn_send[...] = r.grad_sum[rows:].astype(LOW)

    mine, double = whole(rows, wide), whole(2 * rows, wide)
    sums = [("branch_sum", (2 * rows, wide), F32), ("grad_sum", (2 * rows, wide), F32)]
    ins = [("own", mine, own), ("far", mine, far), ("grad", double, grad)]
    outs = [("db", part(1, width), (parts, 1, width), F32)]
    scratch = [
        ("both", pltpu.VMEM((2 * rows, wide), LOW)),
        ("turned", pltpu.VMEM((wide, 2 * rows), LOW)),
        ("turned_grad", pltpu.VMEM((wide, 2 * rows), LOW)),
    ]
    if carried:
        ins += [("branch_in", double, carried[0]), ("grad_in", double, carried[1])]
    if residual is None:
        outs += [(name, double, shape, kind) for name, shape, kind in sums]
    else:
        ins.append(("y", mine, residual))
        outs += [
            ("out_keep", mine, (rows, wide), F32),
            ("out_send", mine, (rows, wide), LOW),
            ("dn_keep", mine, (rows, wide), F32),
            ("dn_send", mine, (rows, wide), LOW),
        ]
        scratch += [(name, pltpu.VMEM(shape, kind)) for name, shape, kind in sums]
    outs += gradient_outs(parts, wide, 2 * width, stepwise)
    return call(
        body,
        parts,
        where,
        ins,
        outs,
        scratch + fetch_scratch(pieces, 2 * width, parts, wide),
        pieces,
        flops=24 * parts * rows * width * wide,
        moved=8 * parts * wide * width + 12 * rows * wide,
        exps=4 * parts * rows * width,
    )


def backward(where, pieces, parts, saved, keep, normed, first, carried, last, stepwise):
    rows, wide = normed.shape
    half = rows // 2
    width = saved.o.shape[2]
    heads = width // HEAD

    def body(r):
        w, _ = fetch(r)
        low_grad = r.dyb_out if first else r.dyb

        @at_step(0)
        def _():
            if first:
                grad_normed = r.dn_keep[...] + r.dn_came[...].astype(F32)
                back, gain_sum, shift_sum = layer_norm_back(r.y[...], r.g2[...], grad_normed)
                grad_out = r.grad[...].astype(F32)
                r.dy_sum[...] = grad_out + back
                low_grad[...] = r.dy_sum[...].astype(LOW)
                r.sums[0:1] = row_sum(low_grad[...].astype(F32))
                r.sums[1:2] = row_sum(grad_out)
                r.sums[2:3] = gain_sum
                r.sums[3:4] = shift_sum
                r.sums[4:8] = jnp.zeros((4, wide), F32)
                r.dn_sum[...] = jnp.zeros_like(r.dn_sum)
            else:
                r.dn_sum[...] = r.dn[...]
            r.turned[...] = r.n1[...].T
            r.turned_grad[...] = low_grad[...].T

        grad_mixed = mm(low_grad[...], w[:, 3 * width :]).astype(LOW)
        seen = r.keep[...] > 0
        for head in range(heads):
            at = head * HEAD
            query = r.p[0, :, at : at + HEAD]
            key = r.p[0, :, width + at : width + at + HEAD]
            value = r.p[0, :, 2 * width + at : 2 * width + at + HEAD]
            grad = grad_mixed[:, at : at + HEAD]
            scores = jnp.where(seen, mm(key, query, NT) * HEAD**-0.5, -1e30)
            probability = jnp.exp(scores - r.l[0, head : head + 1, :])
            grad_probability = mm(value, grad, NT)
            grad_value = mm(probability.astype(LOW), grad)
            inner = jnp.sum(grad_probability * probability, axis=0, keepdims=True)
            grad_scores = (probability * (grad_probability - inner)).astype(LOW)
            grad_query = mm(grad_scores, key, TN) * HEAD**-0.5
            grad_key = mm(grad_scores, query) * HEAD**-0.5
            r.dp[:, at : at + HEAD] = grad_query.astype(LOW)
            r.dp[:, width + at : width + at + HEAD] = grad_key.astype(LOW)
            r.dp[:, 2 * width + at : 2 * width + at + HEAD] = grad_value.astype(LOW)
        r.db[0] = row_sum(r.dp[...].astype(F32))
        r.dn_sum[...] += mm(r.dp[...], w[:, : 3 * width], NT)
        store_gradient(r, [(r.turned, r.dp[...]), (r.turned_grad, r.o[0])])

        if not last:
            return

        @at_end()
        def _():
            dy = r.dy_sum if first else r.dy
            gain_sum = shift_sum = 0.0
            for at, ref, out in ((0, r.own, r.gi_own), (half, r.far, r.gi_far)):
                back, gain_add, shift_add = layer_norm_back(
                    ref[...].astype(F32), r.g1[...], r.dn_sum[at : at + half]
                )
                out[...] = (dy[at : at + half] + back).astype(LOW)
                gain_sum, shift_sum = gain_sum + gain_add, shift_sum + shift_add
            r.end_sums[0:1] = gain_sum
            r.end_sums[1:2] = shift_sum
            r.end_sums[2:8] = jnp.zeros((6, wide), F32)

    mine, line, eight = whole(rows, wide), whole(1, wide), whole(8, wide)
    ins = [
        ("p", part(rows, 3 * width), saved.p),
        ("o", part(rows, width), saved.o),
        ("l", part(heads, rows), saved.l),
        ("keep", whole(rows, 1), keep),
        ("n1", mine, normed),
    ]
    outs = [("db", part(1, 3 * width), (parts, 1, 3 * width), F32)]
    scratch = [
        ("dp", pltpu.VMEM((rows, 3 * width), LOW)),
        ("turned", pltpu.VMEM((wide, rows), LOW)),
        ("turned_grad", pltpu.VMEM((wide, rows), LOW)),
    ]
    sums = [("dn_sum", (rows, wide), F32)]
    if first:
        ins += list(zip(("y", "dn_keep", "dn_came", "grad", "g2"), [mine] * 4 + [line], first))
        outs += [("dyb_out", mine, (rows, wide), LOW), ("sums", eight, (8, wide), F32)]
        sums.append(("dy_sum", (rows, wide), F32))
    else:
        ins += list(zip(("dyb", "dy", "dn"), [mine] * 3, carried))
    if last:
        ins += list(zip(("own", "far", "g1"), [whole(half, wide)] * 2 + [line], last))
        outs += [
            ("gi_own", whole(half, wide), (half, wide), LOW),
            ("gi_far", whole(half, wide), (half, wide), LOW),
            ("end_sums", eight, (8, wide), F32),
        ]
        scratch += [(name, pltpu.VMEM(shape, kind)) for name, shape, kind in sums]
    else:
        outs += [(name, mine, shape, kind) for name, shape, kind in sums]
    outs += gradient_outs(parts, wide, 4 * width, stepwise)
    return call(
        body,
        parts,
        where,
        ins,
        outs,
        scratch + fetch_scratch(pieces, 4 * width, parts, wide),
        pieces,
        flops=16 * parts * rows * wide * width + 10 * parts * rows * rows * width,
        moved=16 * parts * wide * width + 16 * rows * wide,
        exps=parts * heads * rows * rows,
    )


def spread(where, pieces, parts):
    def body(r):
        for at in range(parts):

            @at_step(at)
            def _(ref=getattr(r, f"piece{at}")):
                r.out[...] = ref[...].astype(F32)

    pair = pieces[0].shape
    block = pl.BlockSpec(pair, lambda t, at: (lax.rem(at[3] - t + parts, parts), 0, 0))
    return call(
        body,
        parts,
        where,
        [(f"piece{at}", whole(*pair), piece) for at, piece in enumerate(pieces)],
        [("out", block, (parts * pair[0],) + pair[1:], F32)],
        moved=6 * parts * pieces[0].size,
    ).out


def forward_total(where, own, far):
    rows, width = own.shape[0], own.shape[1] // 2

    def body(r):
        for flip, ref in ((0, r.own), (1, r.far)):
            block = r.where[0] + flip - 2 * r.where[0] * flip
            span = pl.ds(pl.multiple_of(block * width, width), width)
            r.up[:, span] = ref[:, :width].astype(F32)
            r.down[span, :] = ref[:, width:].astype(F32).T

    got = call(
        body,
        1,
        where,
        [("own", whole(rows, 2 * width), own), ("far", whole(rows, 2 * width), far)],
        [
            ("up", whole(rows, 2 * width), (rows, 2 * width), F32),
            ("down", whole(2 * width, rows), (2 * width, rows), F32),
        ],
        moved=24 * rows * width,
    )
    return got.up, got.down


def attention_total(where, grad):
    rows, width = grad.shape[0], grad.shape[1] // 4

    def body(r):
        for piece in range(3):
            r.qkv[piece] = r.grad[:, piece * width : (piece + 1) * width]
        r.out[...] = r.grad[:, 3 * width :].T

    got = call(
        body,
        1,
        where,
        [("grad", whole(rows, 4 * width), grad)],
        [
            ("qkv", whole(3, rows, width), (3, rows, width), F32),
            ("out", whole(width, rows), (width, rows), F32),
        ],
        moved=32 * rows * width,
    )
    return got.qkv, got.out


def on_device(
    inputs,
    cotangent,
    visible,
    w_qkv,
    b_qv,
    w_out,
    b_out,
    w_up,
    b_up,
    w_down,
    b_down,
    gain_one,
    shift_one,
    gain_two,
    shift_two,
):
    images, half, wide = inputs.shape
    ctx_at, tp_at, fsdp_at = (lax.axis_index(name) for name in ("ctx", "tp", "fsdp"))
    blocks, parts, owners = (lax.axis_size(name) for name in ("ctx", "tp", "fsdp"))
    assert blocks == 2 and images == blocks * parts
    first = blocks * tp_at
    mine, other = first + ctx_at, first + 1 - ctx_at
    where = jnp.stack([ctx_at, fsdp_at % 2, fsdp_at // 2, tp_at]).astype(jnp.int32)
    heads_width = w_qkv.shape[2]
    hidden_half = w_up.shape[1] // 2
    rows = 2 * half

    def swap(values):
        return lax.ppermute(values, "ctx", [(0, 1), (1, 0)])

    def pick(values, index):
        return lax.dynamic_index_in_dim(values, index, 0, keepdims=False)

    def in_order(own, received):
        return jnp.where(ctx_at == 0, own, received), jnp.where(ctx_at == 0, received, own)

    stepwise = owners == 4 and parts == 4
    behind = jnp.mod(tp_at - jnp.arange(parts), parts) if stepwise else jnp.arange(parts)

    def to_core(values):
        return lax.ppermute(values, "fsdp", [(0, 1), (1, 0), (2, 3), (3, 2)])

    def to_y(values):
        return lax.ppermute(values, "fsdp", [(0, 2), (2, 0), (1, 3), (3, 1)])

    def to_tp(values):
        return lax.ppermute(values, "tp", [(i, (i + 1) % parts) for i in range(parts)])

    def gather(shard):
        full = lax.all_gather(shard, ("tp", "fsdp"), axis=0, tiled=True)
        return [full.reshape(parts, owners, *shard.shape)]

    def scatter(gradient):
        flat = gradient.reshape(-1, gradient.shape[2])
        return lax.psum_scatter(flat, ("tp", "fsdp"), scatter_dimension=0, tiled=True)

    def raised(upper, came):
        return upper.astype(F32) + came.astype(F32)

    def onward(total):
        return to_tp(total.astype(LOW))

    tie = lax.optimization_barrier

    a0, b0 = shards(where, w_qkv.transpose(1, 0, 2), w_out, w_up, w_down, b_qv, b_up)
    own = pick(inputs, mine)
    cot_pair = jnp.stack([pick(cotangent, mine), pick(cotangent, other)])
    mine_seen = pick(visible, mine).reshape(blocks, half)
    other_seen = pick(visible, other).reshape(blocks, half)
    keep = jnp.concatenate([pick(mine_seen, ctx_at), pick(mine_seen, 1 - ctx_at)])
    keep_other = jnp.concatenate([pick(other_seen, 1 - ctx_at), pick(other_seen, ctx_at)])
    keep, keep_other = keep[:, None], keep_other[:, None]
    keep_all = jnp.concatenate([keep, keep_other]).astype(LOW)
    norm_one, norm_two = (gain_one[None], shift_one[None]), (gain_two[None], shift_two[None])
    far = swap(pick(inputs, other))

    def hidden_gradient(swapped):
        rows_of = [cot_pair[0], swapped[1], swapped[0], cot_pair[1]]
        return jnp.concatenate(rows_of) * keep_all

    def output_pair(kept, came):
        seen = jnp.concatenate([keep[:half], keep_other[half:]]).astype(F32)
        came = came.astype(F32)
        rows_of = kept + jnp.concatenate([came[half:], came[:half]]) + b_down
        rows_of = (rows_of * seen).astype(LOW)
        return jnp.stack(in_order(rows_of[:half], rows_of[half:]))

    if stepwise:
        a0, b0, a1, ya0, far = tie((a0, b0, to_tp(a0), to_y(a0), far))

        a1, a2, ya1, ca0, cya0, cot_swapped = tie(
            (a1, to_tp(a1), to_y(a1), to_core(a0), to_core(ya0), swap(cot_pair))
        )

        a2, a3, ya2, ca1, cya1 = tie((a2, to_tp(a2), to_y(a2), to_core(a1), to_core(ya1)))

        start = (own, far, b_out[None]) + norm_one
        early = attention(
            where, [a0, ya0, ca0, cya0, a1, ya1, ca1, cya1], 2, keep, start, None, None
        )
        grad_low = hidden_gradient(cot_swapped)
        normed, total_y, grad_low, a3, b0, ya3, b1, ca2, cya2 = tie(
            (
                early.n1_out,
                early.y_out,
                grad_low,
                a3,
                b0,
                to_y(a3),
                to_tp(b0),
                to_core(a2),
                to_core(ya2),
            )
        )

        b2, yb0 = to_tp(b1), to_y(b0)
        ca3, cya3 = to_core(a3), to_core(ya3)
        late = attention(
            where,
            [a2, ya2, ca2, cya2, a3, ya3, ca3, cya3],
            2,
            keep,
            None,
            (normed, total_y),
            norm_two,
        )
        normed_two, residual = late.n2, late.y_out
        normed_two, b2, yb0 = tie((normed_two, b2, yb0))

        normed_far, b3, yb1, cb0, cyb0 = tie(
            (swap(normed_two), to_tp(b2), to_y(b1), to_core(b0), to_core(yb0))
        )

        def block(pieces, carried, last):
            return forward(
                where, pieces, 1, normed_two, normed_far, grad_low, carried, last, True
            )

        def sums(got):
            return got.branch_sum, got.grad_sum

        f0 = block([b0, yb0, cb0, cyb0], None, None)
        sums0, sent0, yb2, cb1, cyb1 = tie(
            (sums(f0), f0.sent, to_y(b2), to_core(b1), to_core(yb1))
        )

        f1 = block([b1, yb1, cb1, cyb1], sums0, None)
        sums1, sent1, came0, yb3, cb2, cyb2 = tie(
            (sums(f1), f1.sent, to_core(sent0), to_y(b3), to_core(b2), to_core(yb2))
        )

        f2 = block([b2, yb2, cb2, cyb2], sums1, None)
        sums2, sent2, came1, cb3, cyb3 = tie(
            (sums(f2), f2.sent, to_core(sent1), to_core(b3), to_core(yb3))
        )

        def upper(got, came):
            return to_y(raised(got.kept[1, 0], came[1, 0]).astype(LOW))

        def lower(got, came, lift):
            return raised(got.kept[0, 0], came[0, 0]) + lift.astype(F32)

        lift1 = upper(f1, came1)
        f3 = block([b3, yb3, cb3, cyb3], sums2, residual)
        dn_send, out_send, sent3, came2 = tie(
            (f3.dn_send, f3.out_send, f3.sent, to_core(sent2))
        )

        lift2 = upper(f2, came2)
        dn_came, came3, lift1 = tie((swap(dn_send), to_core(sent3), lift1))

        ring_sum = onward(lower(f1, came1, lift1))
        out_came = swap(out_send)
        begin = (residual, f3.dn_keep, dn_came, grad_low[:rows], gain_two[None])
        g_early = backward(
            where,
            [a0, ya0, ca0, cya0, a1, ya1, ca1, cya1],
            2,
            early,
            keep,
            normed,
            begin,
            None,
            None,
            True,
        )
        carried, sent_early, ring_sum, out_came, lift2 = tie(
            (
                (g_early.dyb_out, g_early.dy_sum, g_early.dn_sum),
                g_early.sent,
                ring_sum,
                out_came,
                lift2,
            )
        )

        lift3 = upper(f3, came3)
        ring_sum = onward(ring_sum.astype(F32) + lower(f2, came2, lift2))
        h0 = output_pair(f3.out_keep, out_came)
        h1 = to_tp(h0)
        came_early = to_core(sent_early)
        g_late = backward(
            where,
            [a2, ya2, ca2, cya2, a3, ya3, ca3, cya3],
            2,
            late,
            keep,
            normed,
            None,
            carried,
            (own, far, gain_one[None]),
            True,
        )
        gi_far, sent_late, came_early, ring_sum, lift3 = tie(
            (g_late.gi_far, g_late.sent, came_early, ring_sum, lift3)
        )

        quarter = wide // owners // 4

        def rows_of(values, axis, block):
            return lax.dynamic_slice_in_dim(values, block * quarter, quarter, axis)

        def both(kept, came, block):
            return raised(rows_of(kept, 2, block), rows_of(came, 2, block))

        def first_sends(got, came):
            across = swap(both(got.kept, came, 1 - ctx_at).astype(LOW))
            second = raised(got.kept[1, :, 2 * quarter :], came[1, :, 2 * quarter :])
            return across, to_y(second.astype(LOW))

        def second_sends(got, came, across, up):
            near = both(got.kept, came, ctx_at) + across.astype(F32)
            second = raised(got.kept[0, :, 2 * quarter :], came[0, :, 2 * quarter :])
            second = second + up.astype(F32)
            return (
                near[0],
                to_y(near[1].astype(LOW)),
                rows_of(second, 1, ctx_at),
                swap(rows_of(second, 1, 1 - ctx_at).astype(LOW)),
            )

        def third(near, lifted, second, across):
            return jnp.concatenate(
                [near + lifted.astype(F32), second + across.astype(F32)], axis=1
            )

        up_bias = jnp.concatenate([f0.db, f1.db, f2.db, f3.db])
        qkv_bias = jnp.concatenate([g_early.db, g_late.db])
        up_bias = lax.dynamic_update_slice(
            jnp.zeros((parts, 2, hidden_half), F32), up_bias, (0, ctx_at, 0)
        )
        small = jnp.concatenate(
            [
                g_early.sums[:4],
                g_late.end_sums[:2],
                up_bias[behind].reshape(-1, wide),
                qkv_bias[behind].reshape(-1, wide),
            ]
        )
        ring_sum = onward(ring_sum.astype(F32) + lower(f3, came3, lift3))
        side0, up0 = first_sends(g_early, came_early)
        gi_far, came_late, small, small_came, h1 = tie(
            (swap(gi_far), to_core(sent_late), small, to_core(small), h1)
        )

        g0 = jnp.stack(in_order(g_late.gi_own, gi_far))
        h2, g1 = to_tp(h1), to_tp(g0)
        side1, up1 = first_sends(g_late, came_late)
        lift0 = upper(f0, came0)
        small = small + small_came
        side0, up0, ring_sum, h2, small, small_came = tie(
            (side0, up0, ring_sum, h2, small, to_y(small))
        )

        h3 = to_tp(h2)
        sends0 = second_sends(g_early, came_early, side0, up0)
        small = small + small_came
        sends0, g1, side1, up1, lift0, small, small_came = tie(
            (sends0, g1, side1, up1, lift0, small, swap(small))
        )

        g2 = to_tp(g1)
        forward_own = (ring_sum.astype(F32) + lower(f0, came0, lift0)).astype(LOW)
        sends1 = second_sends(g_late, came_late, side1, up1)
        halves0 = third(*sends0)
        small = small + small_came
        sends1, h3, forward_own, small, small_came = tie(
            (
                sends1,
                h3,
                forward_own,
                small,
                lax.ppermute(small, "tp", [(0, 1), (1, 0), (2, 3), (3, 2)]),
            )
        )

        total = onward(halves0[1])
        forward_far = swap(forward_own)
        result = spread(where, [h0, h1, h2, h3], parts)
        halves1 = third(*sends1)
        small = small + small_came
        total, g2, result, small, small_came = tie(
            (
                total,
                g2,
                result,
                small,
                lax.ppermute(small, "tp", [(0, 2), (2, 0), (1, 3), (3, 1)]),
            )
        )

        g3 = to_tp(g2)
        small = small + small_came
        total, forward_far = tie((onward(total.astype(F32) + halves1[0]), forward_far))

        up_total, down_total = forward_total(where, forward_own, forward_far)
        total, g3, up_total = tie((onward(total.astype(F32) + halves1[1]), g3, up_total))

        mine_half = (total.astype(F32) + halves0[0]).astype(LOW)
        far_half = swap(mine_half)
        grad_inputs = spread(where, [g0, g1, g2, g3], parts)
        lows, highs = in_order(mine_half, far_half)
        attention_sum = jnp.concatenate(
            [lows[:quarter], highs[:quarter], lows[quarter:], highs[quarter:]]
        ).astype(F32)
    else:
        attention_w, forward_w = gather(a0), gather(b0)
        grad_low = hidden_gradient(swap(cot_pair))
        start = (own, far, b_out[None]) + norm_one
        got = attention(where, attention_w, parts, keep, start, None, norm_two)
        end = forward(
            where,
            forward_w,
            parts,
            got.n2,
            swap(got.n2),
            grad_low,
            None,
            got.y_out,
            False,
        )
        h0 = output_pair(end.out_keep, swap(end.out_send))
        result = lax.all_gather(h0, "tp", axis=0, tiled=True).astype(F32)
        begin = (got.y_out, end.dn_keep, swap(end.dn_send), grad_low[:rows], gain_two[None])
        back = backward(
            where,
            attention_w,
            parts,
            got,
            keep,
            got.n1_out,
            begin,
            None,
            (own, far, gain_one[None]),
            False,
        )
        g0 = jnp.stack(in_order(back.gi_own, swap(back.gi_far)))
        grad_inputs = lax.all_gather(g0, "tp", axis=0, tiled=True).astype(F32)
        forward_own = scatter(end.gradient)
        attention_own = scatter(back.gradient)
        attention_sum = attention_own.astype(F32) + swap(attention_own).astype(F32)
        up_total, down_total = forward_total(where, forward_own, swap(forward_own))
        up_bias = lax.dynamic_update_slice(
            jnp.zeros((parts, 2, hidden_half), F32), end.db, (0, ctx_at, 0)
        )
        small = jnp.concatenate(
            [
                back.sums[:4],
                back.end_sums[:2],
                up_bias.reshape(-1, wide),
                back.db.reshape(-1, wide),
            ]
        )
        small = lax.psum(small, ("fsdp", "ctx", "tp"))
    qkv_total, out_total = attention_total(where, attention_sum)

    up_rows = parts * 2 * hidden_half // wide
    up_small = small[6 : 6 + up_rows].reshape(parts, 2 * hidden_half)
    qkv_small = small[6 + up_rows :].reshape(parts, 3, heads_width)
    return (
        result,
        grad_inputs,
        qkv_total.transpose(1, 0, 2),
        pick(qkv_small, tp_at)[0::2],
        out_total,
        small[0],
        up_total,
        pick(up_small, tp_at),
        down_total,
        small[1],
        small[4],
        small[5],
        small[2],
        small[3],
    )


def solution(mesh):
    placed = (
        P("fsdp", "ctx", None),
        P("fsdp", "ctx", None),
        P("fsdp", None),
        P("fsdp", None, "tp"),
        P(None, "tp"),
        P("tp", "fsdp"),
        P(),
        P("fsdp", "tp"),
        P("tp"),
        P("tp", "fsdp"),
        P(),
        P(),
        P(),
        P(),
        P(),
    )
    return jax.shard_map(
        on_device,
        mesh=mesh,
        in_specs=placed,
        out_specs=(
            P("fsdp", "ctx", None),
            P("fsdp", "ctx", None),
            P("fsdp", None, "tp"),
            P(None, "tp"),
            P("tp", "fsdp"),
            P(),
            P("fsdp", "tp"),
            P("tp"),
            P("tp", "fsdp"),
            P(),
            P(),
            P(),
            P(),
            P(),
        ),
        check_vma=False,
    )
```

```python
import types

import jax
import jax.numpy as jnp
from jax import lax
from jax.experimental import pallas as pl
from jax.experimental.pallas import tpu as pltpu
from jax.sharding import PartitionSpec as P

HEAD = 64
EPSILON = 1e-06
EXTRA = 16
F32 = jnp.float32
LOW = jnp.bfloat16

NN = (((1,), (0,)), ((), ()))
NT = (((1,), (1,)), ((), ()))
TN = (((0,), (0,)), ((), ()))


def mm(left, right, dims=NN):
    return lax.dot_general(left, right, dims, preferred_element_type=F32)


def whole(*shape):
    return pl.BlockSpec(shape, lambda t, _: (0,) * len(shape))


def part(*shape):
    return pl.BlockSpec((1,) + shape, lambda t, _: (t,) + (0,) * len(shape))


def call(
    body, grid, where, ins, outs, scratch=(), pieces=(), flops=0, moved=0, exps=0, vmem=24, placed=()
):
    names = [entry[0] for entry in ins]
    later = [entry[0] for entry in outs] + [entry[0] for entry in scratch]

    def kernel(where_ref, *refs):
        r = types.SimpleNamespace(where=where_ref)
        count = len(names) + len(pieces)
        r.pieces = refs[len(names) : count]
        for name, ref in zip(names + later, refs[: len(names)] + refs[count:]):
            setattr(r, name, ref)
        body(r)

    results = pl.pallas_call(
        kernel,
        grid_spec=pltpu.PrefetchScalarGridSpec(
            num_scalar_prefetch=1,
            grid=(grid,),
            in_specs=[entry[1] for entry in ins]
            + [pl.BlockSpec(memory_space=pl.ANY)] * len(pieces),
            out_specs=[entry[1] for entry in outs],
            scratch_shapes=[entry[1] for entry in scratch],
        ),
        out_shape=[
            (pltpu.HBM if entry[0] in placed else jax.ShapeDtypeStruct)(entry[2], entry[3])
            for entry in outs
        ],
        compiler_params=pltpu.CompilerParams(
            dimension_semantics=("arbitrary",), vmem_limit_bytes=vmem << 20
        ),
        cost_estimate=pl.CostEstimate(flops=flops, bytes_accessed=moved, transcendentals=exps),
    )(where, *(entry[2] for entry in ins), *pieces)
    return types.SimpleNamespace(**{entry[0]: value for entry, value in zip(outs, results)})


def at_step(step):
    return pl.when(pl.program_id(0) == step)


def at_end():
    return pl.when(pl.program_id(0) == pl.num_programs(0) - 1)


def layer_norm(values, gain, shift):
    center = values - jnp.mean(values, axis=-1, keepdims=True)
    spread = jnp.mean(center * center, axis=-1, keepdims=True)
    return center * lax.rsqrt(spread + EPSILON) * gain + shift


def layer_norm_back(values, gain, grad):
    center = values - jnp.mean(values, axis=-1, keepdims=True)
    scale = lax.rsqrt(jnp.mean(center * center, axis=-1, keepdims=True) + EPSILON)
    unit = center * scale
    scaled = grad * gain
    back = scale * (
        scaled
        - jnp.mean(scaled, axis=-1, keepdims=True)
        - unit * jnp.mean(scaled * unit, axis=-1, keepdims=True)
    )
    return back, row_sum(grad * unit), row_sum(grad)


def row_sum(values):
    return jnp.sum(values, axis=0, keepdims=True)


def fetch_scratch(pieces, width, parts, wide):
    copies = pieces[0].shape[1] if len(pieces) == 1 else 4
    return [
        ("weights", pltpu.VMEM((parts, wide, width), LOW)),
        ("extras", pltpu.VMEM((parts, EXTRA, width), LOW)),
        ("sems", pltpu.SemaphoreType.DMA((parts, copies + 1))),
    ]


def fetch(r):
    parts = r.weights.shape[0]

    def copies(at):
        if len(r.pieces) == 1:
            sources = [r.pieces[0].at[at, owner] for owner in range(r.pieces[0].shape[1])]
            owners = list(range(len(sources)))
        else:
            core, row = r.where[1], r.where[2]
            sources = [r.pieces[4 * at + which] for which in range(4)]
            owners = [
                2 * (row + up - 2 * row * up) + (core + over - 2 * core * over)
                for over in range(2)
                for up in range(2)
            ]
        rows = sources[0].shape[0] - EXTRA
        extra = sources[0].at[pl.ds(rows, EXTRA), :]
        result = [pltpu.make_async_copy(extra, r.extras.at[at], r.sems.at[at, len(sources)])]
        for which, (source, owner) in enumerate(zip(sources, owners)):
            target = r.weights.at[at, pl.ds(pl.multiple_of(owner * rows, rows), rows), :]
            result.append(
                pltpu.make_async_copy(source.at[pl.ds(0, rows), :], target, r.sems.at[at, which])
            )
        return result

    @at_step(0)
    def _():
        for at in range(parts):
            for copy in copies(at):
                copy.start()

    def wait(at):
        @at_step(at)
        def _():
            for copy in copies(at):
                copy.wait()

    for at in range(parts):
        wait(at)
    return r.weights.at[pl.program_id(0)], r.extras.at[pl.program_id(0)]


def joined(terms):
    wide = terms.astype(F32)
    return wide[0:1] + (wide[1:2] + wide[2:3])


def gradient_outs(parts, wide, total, stepwise):
    if not stepwise:
        return [("gradient", part(wide, total), (parts, wide, total), LOW)]
    shape = (2, parts, wide // 4, total)
    block = pl.BlockSpec((2, 1, wide // 4, total), lambda t, _: (0, t, 0, 0))
    return [("kept", block, shape, LOW), ("sent", block, shape, LOW)]


def store_gradient(r, pairs):
    column = 0
    for turned, right in pairs:
        span = slice(column, column + right.shape[1])
        column += right.shape[1]
        if hasattr(r, "gradient"):
            r.gradient[0, :, span] = mm(turned[...], right).astype(LOW)
            continue
        core, row = r.where[1], r.where[2]
        rows = r.kept.shape[2]
        for which, out in enumerate((r.kept, r.sent)):
            for far in range(2):
                owner = 2 * (row + far - 2 * row * far) + (core + which - 2 * core * which)
                start = pl.multiple_of(owner * rows, rows)
                out[far, 0, :, span] = mm(turned[pl.ds(start, rows), :], right).astype(LOW)


def shards_body(r):
    rows, width = r.qkv.shape[1:]
    hidden = r.up.shape[1]
    for piece in range(3):
        r.a[:rows, piece * width : (piece + 1) * width] = r.qkv[piece].astype(LOW)
    r.a[:rows, 3 * width :] = r.out[...].T.astype(LOW)
    r.f[:rows, :hidden] = r.up[...].astype(LOW)
    r.f[:rows, hidden:] = r.down[...].T.astype(LOW)
    r.a[rows:] = jnp.zeros((EXTRA, 4 * width), LOW)
    r.f[rows:] = jnp.zeros((EXTRA, 2 * hidden), LOW)
    for ref, row, shard in ((r.bqv, 0, r.a), (r.bqv, 1, r.a), (r.bup, 0, r.f)):
        left = ref[row : row + 1, :]
        for piece in range(3):
            low = left.astype(LOW)
            left = left - low.astype(F32)
            at = rows + 3 * row + piece
            shard[at : at + 1, : low.shape[1]] = low


def shards(where, w_qkv, w_out, w_up, w_down, b_qv, b_up):
    _, rows, width = w_qkv.shape
    hidden = w_up.shape[1] // 2
    got = call(
        shards_body,
        1,
        where,
        [
            ("qkv", whole(3, rows, width), w_qkv),
            ("out", whole(width, rows), w_out),
            ("up", pl.BlockSpec((rows, hidden), lambda t, at: (0, at[0])), w_up),
            ("down", pl.BlockSpec((hidden, rows), lambda t, at: (at[0], 0)), w_down),
            ("bqv", whole(2, width), b_qv),
            ("bup", pl.BlockSpec((1, hidden), lambda t, at: (0, at[0])), b_up[None]),
        ],
        [
            ("a", whole(rows + EXTRA, 4 * width), (rows + EXTRA, 4 * width), LOW),
            ("f", whole(rows + EXTRA, 2 * hidden), (rows + EXTRA, 2 * hidden), LOW),
        ],
        moved=6 * rows * (4 * width + 2 * hidden),
    )
    return got.a, got.f


def attention(where, pieces, parts, keep, first, carried, last):
    rows = keep.shape[0]
    half = rows // 2
    width = pieces[0].shape[-1] // 4
    heads = width // HEAD
    wide = first[0].shape[1] if first else carried[0].shape[1]

    def body(r):
        w, extra = fetch(r)
        normed = r.n1_out if first else r.n1

        @at_step(0)
        def _():
            if not first:
                r.y_out[...] = r.y[...]
                return
            for at, ref in ((0, r.own), (half, r.far)):
                tokens = ref[...].astype(F32)
                normed[at : at + half] = layer_norm(tokens, r.g1[...], r.s1[...]).astype(LOW)
                r.y_out[at : at + half] = tokens + r.b_out[...]

        terms = extra[...]
        bias_q, bias_v = joined(terms[0:3, :width]), joined(terms[3:6, :width])
        bias = jnp.concatenate([bias_q, jnp.zeros_like(bias_q), bias_v], axis=1)
        low = (mm(normed[...], w[:, : 3 * width]) + bias).astype(LOW)
        r.p[0] = low
        seen = r.keep[...] > 0
        for head in range(heads):
            at = head * HEAD
            query = low[:, at : at + HEAD]
            key = low[:, width + at : width + at + HEAD]
            value = low[:, 2 * width + at : 2 * width + at + HEAD]
            scores = jnp.where(seen, mm(key, query, NT) * HEAD**-0.5, -1e30)
            top = jnp.max(scores, axis=0, keepdims=True)
            exponent = jnp.exp(scores - top)
            total = jnp.sum(exponent, axis=0, keepdims=True)
            probability = (exponent * (1.0 / total)).astype(LOW)
            r.o[0, :, at : at + HEAD] = mm(probability, value, TN).astype(LOW)
            r.l[0, head : head + 1, :] = top + jnp.log(total)
        r.y_out[...] += mm(r.o[0], w[:, 3 * width :], NT)

        if last:

            @at_end()
            def _():
                r.n2[...] = layer_norm(r.y_out[...], r.g2[...], r.s2[...]).astype(LOW)

    line = whole(1, wide)
    ins = [("keep", whole(rows, 1), keep)]
    outs = [
        ("p", part(rows, 3 * width), (parts, rows, 3 * width), LOW),
        ("o", part(rows, width), (parts, rows, width), LOW),
        ("l", part(heads, rows), (parts, heads, rows), F32),
        ("y_out", whole(rows, wide), (rows, wide), F32),
    ]
    if first:
        specs = [whole(half, wide)] * 2 + [line] * 3
        ins += list(zip(("own", "far", "b_out", "g1", "s1"), specs, first))
        outs.append(("n1_out", whole(rows, wide), (rows, wide), LOW))
    else:
        ins += list(zip(("n1", "y"), [whole(rows, wide)] * 2, carried))
    if last:
        ins += list(zip(("g2", "s2"), [line] * 2, last))
        outs.append(("n2", whole(rows, wide), (rows, wide), LOW))
    return call(
        body,
        parts,
        where,
        ins,
        outs,
        fetch_scratch(pieces, 4 * width, parts, wide),
        pieces,
        flops=8 * parts * rows * wide * width + 4 * parts * rows * rows * width,
        moved=8 * parts * wide * width + 12 * rows * wide,
        exps=parts * heads * rows * rows,
        vmem=24 if parts <= 2 else 56,
    )


def forward(where, pieces, parts, own, far, grad, carried, residual, stepwise):
    rows, wide = own.shape
    half = rows // 2
    width = pieces[0].shape[-1] // 2

    def body(r):
        w, extra = fetch(r)

        @at_step(0)
        def _():
            r.both[:rows] = r.own[...]
            r.both[rows:] = r.far[...]
            r.turned[...] = r.both[...].T
            r.turned_grad[...] = r.grad[...].T
            r.branch_sum[...] = r.branch_in[...] if carried else jnp.zeros((2 * rows, wide), F32)
            r.grad_sum[...] = r.grad_in[...] if carried else jnp.zeros((2 * rows, wide), F32)

        hidden = mm(r.both[...], w[:, :width]) + joined(extra[0:3, :width])
        bell = 0.5 * (1.0 + lax.erf(hidden * 0.5**0.5))
        active = (hidden * bell).astype(LOW)
        slope = bell + hidden * jnp.exp(hidden * hidden * -0.5) * 0.3989422804014327
        r.branch_sum[...] += mm(active, w[:, width:], NT)
        grad_hidden = (mm(r.grad[...], w[:, width:]) * slope).astype(LOW)
        r.db[0] = row_sum(grad_hidden.astype(F32))
        r.grad_sum[...] += mm(grad_hidden, w[:, :width], NT)
        store_gradient(r, [(r.turned, grad_hidden), (r.turned_grad, active)])

        if residual is None:
            return

        @at_end()
        def _():
            r.out_keep[:half] = r.y[:half] + r.branch_sum[:half]
            r.out_keep[half:] = r.branch_sum[rows + half :]
            r.out_send[:half] = (r.y[half:] + r.branch_sum[half:rows]).astype(LOW)
            r.out_send[half:] = r.branch_sum[rows : rows + half].astype(LOW)
            r.dn_keep[...] = r.grad_sum[:rows]
            r.dn_send[...] = r.grad_sum[rows:].astype(LOW)

    mine, double = whole(rows, wide), whole(2 * rows, wide)
    sums = [("branch_sum", (2 * rows, wide), F32), ("grad_sum", (2 * rows, wide), F32)]
    ins = [("own", mine, own), ("far", mine, far), ("grad", double, grad)]
    outs = [("db", part(1, width), (parts, 1, width), F32)]
    scratch = [
        ("both", pltpu.VMEM((2 * rows, wide), LOW)),
        ("turned", pltpu.VMEM((wide, 2 * rows), LOW)),
        ("turned_grad", pltpu.VMEM((wide, 2 * rows), LOW)),
    ]
    if carried:
        ins += [("branch_in", double, carried[0]), ("grad_in", double, carried[1])]
    if residual is None:
        outs += [(name, double, shape, kind) for name, shape, kind in sums]
    else:
        ins.append(("y", mine, residual))
        outs += [
            ("out_keep", mine, (rows, wide), F32),
            ("out_send", mine, (rows, wide), LOW),
            ("dn_keep", mine, (rows, wide), F32),
            ("dn_send", mine, (rows, wide), LOW),
        ]
        scratch += [(name, pltpu.VMEM(shape, kind)) for name, shape, kind in sums]
    outs += gradient_outs(parts, wide, 2 * width, stepwise)
    return call(
        body,
        parts,
        where,
        ins,
        outs,
        scratch + fetch_scratch(pieces, 2 * width, parts, wide),
        pieces,
        flops=24 * parts * rows * width * wide,
        moved=8 * parts * wide * width + 12 * rows * wide,
        exps=4 * parts * rows * width,
        vmem=24 if parts <= 2 else 56,
    )


def backward(where, pieces, parts, saved, keep, normed, first, carried, last, stepwise):
    rows, wide = normed.shape
    half = rows // 2
    width = saved.o.shape[2]
    heads = width // HEAD

    def body(r):
        w, _ = fetch(r)
        low_grad = r.dyb_out if first else r.dyb

        @at_step(0)
        def _():
            if first:
                grad_normed = r.dn_keep[...] + r.dn_came[...].astype(F32)
                back, gain_sum, shift_sum = layer_norm_back(r.y[...], r.g2[...], grad_normed)
                grad_out = r.grad[...].astype(F32)
                r.dy_sum[...] = grad_out + back
                low_grad[...] = r.dy_sum[...].astype(LOW)
                r.sums[0:1] = row_sum(low_grad[...].astype(F32))
                r.sums[1:2] = row_sum(grad_out)
                r.sums[2:3] = gain_sum
                r.sums[3:4] = shift_sum
                r.sums[4:8] = jnp.zeros((4, wide), F32)
                r.dn_sum[...] = jnp.zeros_like(r.dn_sum)
            else:
                r.dn_sum[...] = r.dn[...]
            r.turned[...] = r.n1[...].T
            r.turned_grad[...] = low_grad[...].T

        grad_mixed = mm(low_grad[...], w[:, 3 * width :]).astype(LOW)
        seen = r.keep[...] > 0
        for head in range(heads):
            at = head * HEAD
            query = r.p[0, :, at : at + HEAD]
            key = r.p[0, :, width + at : width + at + HEAD]
            value = r.p[0, :, 2 * width + at : 2 * width + at + HEAD]
            grad = grad_mixed[:, at : at + HEAD]
            scores = jnp.where(seen, mm(key, query, NT) * HEAD**-0.5, -1e30)
            probability = jnp.exp(scores - r.l[0, head : head + 1, :])
            grad_probability = mm(value, grad, NT)
            grad_value = mm(probability.astype(LOW), grad)
            inner = jnp.sum(grad_probability * probability, axis=0, keepdims=True)
            grad_scores = (probability * (grad_probability - inner)).astype(LOW)
            grad_query = mm(grad_scores, key, TN) * HEAD**-0.5
            grad_key = mm(grad_scores, query) * HEAD**-0.5
            r.dp[:, at : at + HEAD] = grad_query.astype(LOW)
            r.dp[:, width + at : width + at + HEAD] = grad_key.astype(LOW)
            r.dp[:, 2 * width + at : 2 * width + at + HEAD] = grad_value.astype(LOW)
        r.db[0] = row_sum(r.dp[...].astype(F32))
        r.dn_sum[...] += mm(r.dp[...], w[:, : 3 * width], NT)
        store_gradient(r, [(r.turned, r.dp[...]), (r.turned_grad, r.o[0])])

        if not last:
            return

        @at_end()
        def _():
            dy = r.dy_sum if first else r.dy
            gain_sum = shift_sum = 0.0
            for at, ref, out in ((0, r.own, r.gi_own), (half, r.far, r.gi_far)):
                back, gain_add, shift_add = layer_norm_back(
                    ref[...].astype(F32), r.g1[...], r.dn_sum[at : at + half]
                )
                out[...] = (dy[at : at + half] + back).astype(LOW)
                gain_sum, shift_sum = gain_sum + gain_add, shift_sum + shift_add
            r.end_sums[0:1] = gain_sum
            r.end_sums[1:2] = shift_sum
            r.end_sums[2:8] = jnp.zeros((6, wide), F32)

    mine, line, eight = whole(rows, wide), whole(1, wide), whole(8, wide)
    ins = [
        ("p", part(rows, 3 * width), saved.p),
        ("o", part(rows, width), saved.o),
        ("l", part(heads, rows), saved.l),
        ("keep", whole(rows, 1), keep),
        ("n1", mine, normed),
    ]
    outs = [("db", part(1, 3 * width), (parts, 1, 3 * width), F32)]
    scratch = [
        ("dp", pltpu.VMEM((rows, 3 * width), LOW)),
        ("turned", pltpu.VMEM((wide, rows), LOW)),
        ("turned_grad", pltpu.VMEM((wide, rows), LOW)),
    ]
    sums = [("dn_sum", (rows, wide), F32)]
    if first:
        ins += list(zip(("y", "dn_keep", "dn_came", "grad", "g2"), [mine] * 4 + [line], first))
        outs += [("dyb_out", mine, (rows, wide), LOW), ("sums", eight, (8, wide), F32)]
        sums.append(("dy_sum", (rows, wide), F32))
    else:
        ins += list(zip(("dyb", "dy", "dn"), [mine] * 3, carried))
    if last:
        ins += list(zip(("own", "far", "g1"), [whole(half, wide)] * 2 + [line], last))
        outs += [
            ("gi_own", whole(half, wide), (half, wide), LOW),
            ("gi_far", whole(half, wide), (half, wide), LOW),
            ("end_sums", eight, (8, wide), F32),
        ]
        scratch += [(name, pltpu.VMEM(shape, kind)) for name, shape, kind in sums]
    else:
        outs += [(name, mine, shape, kind) for name, shape, kind in sums]
    outs += gradient_outs(parts, wide, 4 * width, stepwise)
    return call(
        body,
        parts,
        where,
        ins,
        outs,
        scratch + fetch_scratch(pieces, 4 * width, parts, wide),
        pieces,
        placed=("dyb_out", "dy_sum", "dn_sum", "kept", "sent", "gi_own", "gi_far"),
        flops=16 * parts * rows * wide * width + 10 * parts * rows * rows * width,
        moved=16 * parts * wide * width + 16 * rows * wide,
        exps=parts * heads * rows * rows,
        vmem=24 if parts <= 2 else 56,
    )


def spread(where, pieces, parts):
    def body(r):
        for at in range(parts):

            @at_step(at)
            def _(ref=getattr(r, f"piece{at}")):
                r.out[...] = ref[...].astype(F32)

    pair = pieces[0].shape
    block = pl.BlockSpec(pair, lambda t, at: (lax.rem(at[3] - t + parts, parts), 0, 0))
    return call(
        body,
        parts,
        where,
        [(f"piece{at}", whole(*pair), piece) for at, piece in enumerate(pieces)],
        [("out", block, (parts * pair[0],) + pair[1:], F32)],
        moved=6 * parts * pieces[0].size,
    ).out


def forward_total(where, own, far):
    rows, width = own.shape[0], own.shape[1] // 2

    def body(r):
        for flip, ref in ((0, r.own), (1, r.far)):
            block = r.where[0] + flip - 2 * r.where[0] * flip
            span = pl.ds(pl.multiple_of(block * width, width), width)
            r.up[:, span] = ref[:, :width].astype(F32)
            r.down[span, :] = ref[:, width:].astype(F32).T

    got = call(
        body,
        1,
        where,
        [("own", whole(rows, 2 * width), own), ("far", whole(rows, 2 * width), far)],
        [
            ("up", whole(rows, 2 * width), (rows, 2 * width), F32),
            ("down", whole(2 * width, rows), (2 * width, rows), F32),
        ],
        moved=24 * rows * width,
    )
    return got.up, got.down


def attention_total(where, grad):
    rows, width = grad.shape[0], grad.shape[1] // 4

    def body(r):
        for piece in range(3):
            r.qkv[piece] = r.grad[:, piece * width : (piece + 1) * width]
        r.out[...] = r.grad[:, 3 * width :].T

    got = call(
        body,
        1,
        where,
        [("grad", whole(rows, 4 * width), grad)],
        [
            ("qkv", whole(3, rows, width), (3, rows, width), F32),
            ("out", whole(width, rows), (width, rows), F32),
        ],
        moved=32 * rows * width,
    )
    return got.qkv, got.out


def on_device(
    inputs,
    cotangent,
    visible,
    w_qkv,
    b_qv,
    w_out,
    b_out,
    w_up,
    b_up,
    w_down,
    b_down,
    gain_one,
    shift_one,
    gain_two,
    shift_two,
):
    images, half, wide = inputs.shape
    ctx_at, tp_at, fsdp_at = (lax.axis_index(name) for name in ("ctx", "tp", "fsdp"))
    blocks, parts, owners = (lax.axis_size(name) for name in ("ctx", "tp", "fsdp"))
    assert blocks == 2 and images == blocks * parts
    first = blocks * tp_at
    mine, other = first + ctx_at, first + 1 - ctx_at
    where = jnp.stack([ctx_at, fsdp_at % 2, fsdp_at // 2, tp_at]).astype(jnp.int32)
    heads_width = w_qkv.shape[2]
    hidden_half = w_up.shape[1] // 2
    rows = 2 * half

    def swap(values):
        return lax.ppermute(values, "ctx", [(0, 1), (1, 0)])

    def pick(values, index):
        return lax.dynamic_index_in_dim(values, index, 0, keepdims=False)

    def in_order(own, received):
        return jnp.where(ctx_at == 0, own, received), jnp.where(ctx_at == 0, received, own)

    stepwise = owners == 4 and parts == 4
    behind = jnp.mod(tp_at - jnp.arange(parts), parts) if stepwise else jnp.arange(parts)

    def to_core(values):
        return lax.ppermute(values, "fsdp", [(0, 1), (1, 0), (2, 3), (3, 2)])

    def to_y(values):
        return lax.ppermute(values, "fsdp", [(0, 2), (2, 0), (1, 3), (3, 1)])

    def to_tp(values):
        return lax.ppermute(values, "tp", [(i, (i + 1) % parts) for i in range(parts)])

    def gather(shard):
        full = lax.all_gather(shard, ("tp", "fsdp"), axis=0, tiled=True)
        return [full.reshape(parts, owners, *shard.shape)]

    def scatter(gradient):
        flat = gradient.reshape(-1, gradient.shape[2])
        return lax.psum_scatter(flat, ("tp", "fsdp"), scatter_dimension=0, tiled=True)

    def raised(upper, came):
        return upper.astype(F32) + came.astype(F32)

    def onward(total):
        return to_tp(total.astype(LOW))

    tie = lax.optimization_barrier

    a0, b0 = shards(where, w_qkv.transpose(1, 0, 2), w_out, w_up, w_down, b_qv, b_up)
    own = pick(inputs, mine)
    cot_pair = jnp.stack([pick(cotangent, mine), pick(cotangent, other)])
    mine_seen = pick(visible, mine).reshape(blocks, half)
    other_seen = pick(visible, other).reshape(blocks, half)
    keep = jnp.concatenate([pick(mine_seen, ctx_at), pick(mine_seen, 1 - ctx_at)])
    keep_other = jnp.concatenate([pick(other_seen, 1 - ctx_at), pick(other_seen, ctx_at)])
    keep, keep_other = keep[:, None], keep_other[:, None]
    keep_all = jnp.concatenate([keep, keep_other]).astype(LOW)
    norm_one, norm_two = (gain_one[None], shift_one[None]), (gain_two[None], shift_two[None])
    far = swap(pick(inputs, other))

    def hidden_gradient(swapped):
        rows_of = [cot_pair[0], swapped[1], swapped[0], cot_pair[1]]
        return jnp.concatenate(rows_of) * keep_all

    def output_pair(kept, came):
        seen = jnp.concatenate([keep[:half], keep_other[half:]]).astype(F32)
        came = came.astype(F32)
        rows_of = kept + jnp.concatenate([came[half:], came[:half]]) + b_down
        rows_of = (rows_of * seen).astype(LOW)
        return jnp.stack(in_order(rows_of[:half], rows_of[half:]))

    if stepwise:
        a0, b0, a1, ya0 = tie((a0, b0, to_tp(a0), to_y(a0)))

        a1, a2, ya1, ca0, cya0, far = tie(
            (a1, to_tp(a1), to_y(a1), to_core(a0), to_core(ya0), far)
        )

        a2, a3, ya2, ca1, cya1, cot_swapped = tie(
            (a2, to_tp(a2), to_y(a2), to_core(a1), to_core(ya1), swap(cot_pair))
        )

        start = (own, far, b_out[None]) + norm_one
        early = attention(
            where, [a0, ya0, ca0, cya0, a1, ya1, ca1, cya1], 2, keep, start, None, None
        )
        grad_low = hidden_gradient(cot_swapped)
        normed, total_y, grad_low, a3, b0, ya3, b1, ca2, cya2 = tie(
            (
                early.n1_out,
                early.y_out,
                grad_low,
                a3,
                b0,
                to_y(a3),
                to_tp(b0),
                to_core(a2),
                to_core(ya2),
            )
        )

        b2, yb0 = to_tp(b1), to_y(b0)
        ca3, cya3 = to_core(a3), to_core(ya3)
        late = attention(
            where,
            [a2, ya2, ca2, cya2, a3, ya3, ca3, cya3],
            2,
            keep,
            None,
            (normed, total_y),
            norm_two,
        )
        normed_two, residual = late.n2, late.y_out
        b2, yb0 = tie((b2, yb0))

        normed_far, b3, yb1, cb0, cyb0 = tie(
            (swap(normed_two), to_tp(b2), to_y(b1), to_core(b0), to_core(yb0))
        )

        def block(pieces, carried, last):
            return forward(
                where, pieces, 1, normed_two, normed_far, grad_low, carried, last, True
            )

        def sums(got):
            return got.branch_sum, got.grad_sum

        f0 = block([b0, yb0, cb0, cyb0], None, None)
        sums0, sent0, yb2, cb1, cyb1 = tie(
            (sums(f0), f0.sent, to_y(b2), to_core(b1), to_core(yb1))
        )

        f1 = block([b1, yb1, cb1, cyb1], sums0, None)
        sums1, sent1, came0, yb3, cb2, cyb2 = tie(
            (sums(f1), f1.sent, to_core(sent0), to_y(b3), to_core(b2), to_core(yb2))
        )

        f2 = block([b2, yb2, cb2, cyb2], sums1, None)
        sums2, sent2, came1, cb3, cyb3 = tie(
            (sums(f2), f2.sent, to_core(sent1), to_core(b3), to_core(yb3))
        )

        def upper(got, came):
            return to_y(raised(got.kept[1, 0], came[1, 0]).astype(LOW))

        def lower(got, came, lift):
            return raised(got.kept[0, 0], came[0, 0]) + lift.astype(F32)

        lift1 = upper(f1, came1)
        f3 = block([b3, yb3, cb3, cyb3], sums2, residual)
        dn_send, out_send, sent3, came2, lift1 = tie(
            (f3.dn_send, f3.out_send, f3.sent, to_core(sent2), lift1)
        )

        ring_sum = onward(lower(f1, came1, lift1))
        lift2 = upper(f2, came2)
        dn_came, came3, lift2, ring_sum = tie((swap(dn_send), to_core(sent3), lift2, ring_sum))

        out_came = swap(out_send)
        lift3 = upper(f3, came3)
        ring_sum = onward(ring_sum.astype(F32) + lower(f2, came2, lift2))
        begin = (residual, f3.dn_keep, dn_came, grad_low[:rows], gain_two[None])
        g_early = backward(
            where,
            [a0, ya0, ca0, cya0, a1, ya1, ca1, cya1],
            2,
            early,
            keep,
            normed,
            begin,
            None,
            None,
            True,
        )
        carried, sent_early, ring_sum, out_came, lift3 = tie(
            (
                (g_early.dyb_out, g_early.dy_sum, g_early.dn_sum),
                g_early.sent,
                ring_sum,
                out_came,
                lift3,
            )
        )

        lift0 = upper(f0, came0)
        h0, carried = tie((output_pair(f3.out_keep, out_came), carried))
        h1 = to_tp(h0)
        came_early = to_core(sent_early)
        g_late = backward(
            where,
            [a2, ya2, ca2, cya2, a3, ya3, ca3, cya3],
            2,
            late,
            keep,
            normed,
            None,
            carried,
            (own, far, gain_one[None]),
            True,
        )
        gi_far, sent_late, came_early, lift0, h1 = tie(
            (g_late.gi_far, g_late.sent, came_early, lift0, h1)
        )

        quarter = wide // owners // 4

        def rows_of(values, axis, block):
            return lax.dynamic_slice_in_dim(values, block * quarter, quarter, axis)

        def both(kept, came, block):
            return raised(rows_of(kept, 2, block), rows_of(came, 2, block))

        def first_sends(got, came):
            across = swap(both(got.kept, came, 1 - ctx_at).astype(LOW))
            second = raised(got.kept[1, :, 2 * quarter :], came[1, :, 2 * quarter :])
            return across, to_y(second.astype(LOW))

        def second_sends(got, came, across, up):
            near = both(got.kept, came, ctx_at) + across.astype(F32)
            second = raised(got.kept[0, :, 2 * quarter :], came[0, :, 2 * quarter :])
            second = second + up.astype(F32)
            return (
                near[0],
                to_y(near[1].astype(LOW)),
                rows_of(second, 1, ctx_at),
                swap(rows_of(second, 1, 1 - ctx_at).astype(LOW)),
            )

        def third(near, lifted, second, across):
            return jnp.concatenate(
                [near + lifted.astype(F32), second + across.astype(F32)], axis=1
            )

        up_bias = jnp.concatenate([f0.db, f1.db, f2.db, f3.db])
        qkv_bias = jnp.concatenate([g_early.db, g_late.db])
        up_bias = lax.dynamic_update_slice(
            jnp.zeros((parts, 2, hidden_half), F32), up_bias, (0, ctx_at, 0)
        )
        small = jnp.concatenate(
            [
                g_early.sums[:4],
                g_late.end_sums[:2],
                up_bias[behind].reshape(-1, wide),
                qkv_bias[behind].reshape(-1, wide),
            ]
        )
        ring_sum = onward(ring_sum.astype(F32) + lower(f3, came3, lift3))
        h2 = to_tp(h1)
        side0, up0 = first_sends(g_early, came_early)
        gi_far, came_late, small, small_came = tie(
            (swap(gi_far), to_core(sent_late), small, to_core(small))
        )

        g0 = jnp.stack(in_order(g_late.gi_own, gi_far))
        g1 = to_tp(g0)
        side1, up1 = first_sends(g_late, came_late)
        small = small + small_came
        side0, up0, ring_sum, h2, small, small_came = tie(
            (side0, up0, ring_sum, h2, small, to_y(small))
        )

        h3 = to_tp(h2)
        forward_own = (ring_sum.astype(F32) + lower(f0, came0, lift0)).astype(LOW)
        sends0 = second_sends(g_early, came_early, side0, up0)
        small = small + small_came
        forward_own, g1, side1, up1, small, small_came = tie(
            (forward_own, g1, side1, up1, small, swap(small))
        )

        sends1 = second_sends(g_late, came_late, side1, up1)
        forward_far = swap(forward_own)
        sends0 = tie(sends0)
        halves0 = third(*sends0)
        total = onward(halves0[1])
        small = small + small_came
        sends1, h3, total, small, small_came = tie(
            (
                sends1,
                h3,
                total,
                small,
                lax.ppermute(small, "tp", [(0, 1), (1, 0), (2, 3), (3, 2)]),
            )
        )

        halves1 = third(*sends1)
        small = small + small_came
        total = onward(total.astype(F32) + halves1[0])
        g2 = to_tp(g1)
        result = spread(where, [h0, h1, h2, h3], parts)
        total, result, small, small_came, forward_far = tie(
            (
                total,
                result,
                small,
                lax.ppermute(small, "tp", [(0, 2), (2, 0), (1, 3), (3, 1)]),
                forward_far,
            )
        )

        small = small + small_came
        total = onward(total.astype(F32) + halves1[1])
        up_total, down_total = forward_total(where, forward_own, forward_far)
        total, g2, up_total = tie((total, g2, up_total))
        g3 = to_tp(g2)

        mine_half = (total.astype(F32) + halves0[0]).astype(LOW)
        far_half = swap(mine_half)
        grad_inputs = spread(where, [g0, g1, g2, g3], parts)
        lows, highs = in_order(mine_half, far_half)
        attention_sum = jnp.concatenate(
            [lows[:quarter], highs[:quarter], lows[quarter:], highs[quarter:]]
        ).astype(F32)
    else:
        attention_w, forward_w = gather(a0), gather(b0)
        grad_low = hidden_gradient(swap(cot_pair))
        start = (own, far, b_out[None]) + norm_one
        got = attention(where, attention_w, parts, keep, start, None, norm_two)
        end = forward(
            where,
            forward_w,
            parts,
            got.n2,
            swap(got.n2),
            grad_low,
            None,
            got.y_out,
            False,
        )
        h0 = output_pair(end.out_keep, swap(end.out_send))
        result = lax.all_gather(h0, "tp", axis=0, tiled=True).astype(F32)
        begin = (got.y_out, end.dn_keep, swap(end.dn_send), grad_low[:rows], gain_two[None])
        back = backward(
            where,
            attention_w,
            parts,
            got,
            keep,
            got.n1_out,
            begin,
            None,
            (own, far, gain_one[None]),
            False,
        )
        g0 = jnp.stack(in_order(back.gi_own, swap(back.gi_far)))
        grad_inputs = lax.all_gather(g0, "tp", axis=0, tiled=True).astype(F32)
        forward_own = scatter(end.gradient)
        attention_own = scatter(back.gradient)
        attention_sum = attention_own.astype(F32) + swap(attention_own).astype(F32)
        up_total, down_total = forward_total(where, forward_own, swap(forward_own))
        up_bias = lax.dynamic_update_slice(
            jnp.zeros((parts, 2, hidden_half), F32), end.db, (0, ctx_at, 0)
        )
        small = jnp.concatenate(
            [
                back.sums[:4],
                back.end_sums[:2],
                up_bias.reshape(-1, wide),
                back.db.reshape(-1, wide),
            ]
        )
        small = lax.psum(small, ("fsdp", "ctx", "tp"))
    qkv_total, out_total = attention_total(where, attention_sum)

    up_rows = parts * 2 * hidden_half // wide
    up_small = small[6 : 6 + up_rows].reshape(parts, 2 * hidden_half)
    qkv_small = small[6 + up_rows :].reshape(parts, 3, heads_width)
    return (
        result,
        grad_inputs,
        qkv_total.transpose(1, 0, 2),
        pick(qkv_small, tp_at)[0::2],
        out_total,
        small[0],
        up_total,
        pick(up_small, tp_at),
        down_total,
        small[1],
        small[4],
        small[5],
        small[2],
        small[3],
    )


def solution(mesh):
    placed = (
        P("fsdp", "ctx", None),
        P("fsdp", "ctx", None),
        P("fsdp", None),
        P("fsdp", None, "tp"),
        P(None, "tp"),
        P("tp", "fsdp"),
        P(),
        P("fsdp", "tp"),
        P("tp"),
        P("tp", "fsdp"),
        P(),
        P(),
        P(),
        P(),
        P(),
    )
    return jax.shard_map(
        on_device,
        mesh=mesh,
        in_specs=placed,
        out_specs=(
            P("fsdp", "ctx", None),
            P("fsdp", "ctx", None),
            P("fsdp", None, "tp"),
            P(None, "tp"),
            P("tp", "fsdp"),
            P(),
            P("fsdp", "tp"),
            P("tp"),
            P("tp", "fsdp"),
            P(),
            P(),
            P(),
            P(),
            P(),
        ),
        check_vma=False,
    )
```

```python
import types

import jax
import jax.numpy as jnp
from jax import lax
from jax.experimental import pallas as pl
from jax.experimental.pallas import tpu as pltpu
from jax.sharding import PartitionSpec as P

HEAD = 64
EPSILON = 1e-06
EXTRA = 16
F32 = jnp.float32
LOW = jnp.bfloat16

NN = (((1,), (0,)), ((), ()))
NT = (((1,), (1,)), ((), ()))
TN = (((0,), (0,)), ((), ()))


def mm(left, right, dims=NN):
    return lax.dot_general(left, right, dims, preferred_element_type=F32)


def whole(*shape):
    return pl.BlockSpec(shape, lambda t, _: (0,) * len(shape))


def part(*shape):
    return pl.BlockSpec((1,) + shape, lambda t, _: (t,) + (0,) * len(shape))


def call(
    body, grid, where, ins, outs, scratch=(), pieces=(), flops=0, moved=0, exps=0, vmem=24, placed=(), home=pltpu.HBM
):
    names = [entry[0] for entry in ins]
    later = [entry[0] for entry in outs] + [entry[0] for entry in scratch]

    def kernel(where_ref, *refs):
        r = types.SimpleNamespace(where=where_ref)
        count = len(names) + len(pieces)
        r.pieces = refs[len(names) : count]
        for name, ref in zip(names + later, refs[: len(names)] + refs[count:]):
            setattr(r, name, ref)
        body(r)

    results = pl.pallas_call(
        kernel,
        grid_spec=pltpu.PrefetchScalarGridSpec(
            num_scalar_prefetch=1,
            grid=(grid,),
            in_specs=[entry[1] for entry in ins]
            + [pl.BlockSpec(memory_space=home)] * len(pieces),
            out_specs=[entry[1] for entry in outs],
            scratch_shapes=[entry[1] for entry in scratch],
        ),
        out_shape=[
            (pltpu.HBM if entry[0] in placed else jax.ShapeDtypeStruct)(entry[2], entry[3])
            for entry in outs
        ],
        compiler_params=pltpu.CompilerParams(
            dimension_semantics=("arbitrary",), vmem_limit_bytes=vmem << 20
        ),
        cost_estimate=pl.CostEstimate(flops=flops, bytes_accessed=moved, transcendentals=exps),
    )(
        where,
        *(
            pltpu.with_memory_space_constraint(entry[2], pltpu.HBM)
            if entry[0] in placed
            else entry[2]
            for entry in ins
        ),
        *(pltpu.with_memory_space_constraint(piece, home) for piece in pieces),
    )
    return types.SimpleNamespace(**{entry[0]: value for entry, value in zip(outs, results)})


def at_step(step):
    return pl.when(pl.program_id(0) == step)


def at_end():
    return pl.when(pl.program_id(0) == pl.num_programs(0) - 1)


def layer_norm(values, gain, shift):
    center = values - jnp.mean(values, axis=-1, keepdims=True)
    spread = jnp.mean(center * center, axis=-1, keepdims=True)
    return center * lax.rsqrt(spread + EPSILON) * gain + shift


def layer_norm_back(values, gain, grad):
    center = values - jnp.mean(values, axis=-1, keepdims=True)
    scale = lax.rsqrt(jnp.mean(center * center, axis=-1, keepdims=True) + EPSILON)
    unit = center * scale
    scaled = grad * gain
    back = scale * (
        scaled
        - jnp.mean(scaled, axis=-1, keepdims=True)
        - unit * jnp.mean(scaled * unit, axis=-1, keepdims=True)
    )
    return back, row_sum(grad * unit), row_sum(grad)


def row_sum(values):
    return jnp.sum(values, axis=0, keepdims=True)


def fetch_scratch(pieces, width, parts, wide):
    copies = pieces[0].shape[1] if len(pieces) == 1 else 4
    return [
        ("weights", pltpu.VMEM((parts, wide, width), LOW)),
        ("extras", pltpu.VMEM((parts, EXTRA, width), LOW)),
        ("sems", pltpu.SemaphoreType.DMA((parts, copies + 1))),
    ]


def fetch(r):
    parts = r.weights.shape[0]

    def copies(at):
        if len(r.pieces) == 1:
            sources = [r.pieces[0].at[at, owner] for owner in range(r.pieces[0].shape[1])]
            owners = list(range(len(sources)))
        else:
            core, row = r.where[1], r.where[2]
            sources = [r.pieces[4 * at + which] for which in range(4)]
            owners = [
                2 * (row + up - 2 * row * up) + (core + over - 2 * core * over)
                for over in range(2)
                for up in range(2)
            ]
        rows = sources[0].shape[0] - EXTRA
        extra = sources[0].at[pl.ds(rows, EXTRA), :]
        result = [pltpu.make_async_copy(extra, r.extras.at[at], r.sems.at[at, len(sources)])]
        for which, (source, owner) in enumerate(zip(sources, owners)):
            target = r.weights.at[at, pl.ds(pl.multiple_of(owner * rows, rows), rows), :]
            result.append(
                pltpu.make_async_copy(source.at[pl.ds(0, rows), :], target, r.sems.at[at, which])
            )
        return result

    @at_step(0)
    def _():
        for at in range(parts):
            for copy in copies(at):
                copy.start()

    def wait(at):
        @at_step(at)
        def _():
            for copy in copies(at):
                copy.wait()

    for at in range(parts):
        wait(at)
    return r.weights.at[pl.program_id(0)], r.extras.at[pl.program_id(0)]


def joined(terms):
    wide = terms.astype(F32)
    return wide[0:1] + (wide[1:2] + wide[2:3])


def gradient_outs(parts, wide, total, stepwise):
    if not stepwise:
        return [("gradient", part(wide, total), (parts, wide, total), LOW)]
    shape = (2, parts, wide // 4, total)
    block = pl.BlockSpec((2, 1, wide // 4, total), lambda t, _: (0, t, 0, 0))
    return [("kept", block, shape, LOW), ("sent", block, shape, LOW)]


def store_gradient(r, pairs):
    column = 0
    for turned, right in pairs:
        span = slice(column, column + right.shape[1])
        column += right.shape[1]
        if hasattr(r, "gradient"):
            r.gradient[0, :, span] = mm(turned[...], right).astype(LOW)
            continue
        core, row = r.where[1], r.where[2]
        rows = r.kept.shape[2]
        for which, out in enumerate((r.kept, r.sent)):
            for far in range(2):
                owner = 2 * (row + far - 2 * row * far) + (core + which - 2 * core * which)
                start = pl.multiple_of(owner * rows, rows)
                out[far, 0, :, span] = mm(turned[pl.ds(start, rows), :], right).astype(LOW)


def shards_body(r):
    rows, width = r.qkv.shape[1:]
    hidden = r.up.shape[1]
    for piece in range(3):
        r.a[:rows, piece * width : (piece + 1) * width] = r.qkv[piece].astype(LOW)
    r.a[:rows, 3 * width :] = r.out[...].T.astype(LOW)
    r.f[:rows, :hidden] = r.up[...].astype(LOW)
    r.f[:rows, hidden:] = r.down[...].T.astype(LOW)
    r.a[rows:] = jnp.zeros((EXTRA, 4 * width), LOW)
    r.f[rows:] = jnp.zeros((EXTRA, 2 * hidden), LOW)
    for ref, row, shard in ((r.bqv, 0, r.a), (r.bqv, 1, r.a), (r.bup, 0, r.f)):
        left = ref[row : row + 1, :]
        for piece in range(3):
            low = left.astype(LOW)
            left = left - low.astype(F32)
            at = rows + 3 * row + piece
            shard[at : at + 1, : low.shape[1]] = low


def shards(where, w_qkv, w_out, w_up, w_down, b_qv, b_up):
    _, rows, width = w_qkv.shape
    hidden = w_up.shape[1] // 2
    got = call(
        shards_body,
        1,
        where,
        [
            ("qkv", whole(3, rows, width), w_qkv),
            ("out", whole(width, rows), w_out),
            ("up", pl.BlockSpec((rows, hidden), lambda t, at: (0, at[0])), w_up),
            ("down", pl.BlockSpec((hidden, rows), lambda t, at: (at[0], 0)), w_down),
            ("bqv", whole(2, width), b_qv),
            ("bup", pl.BlockSpec((1, hidden), lambda t, at: (0, at[0])), b_up[None]),
        ],
        [
            ("a", whole(rows + EXTRA, 4 * width), (rows + EXTRA, 4 * width), LOW),
            ("f", whole(rows + EXTRA, 2 * hidden), (rows + EXTRA, 2 * hidden), LOW),
        ],
        moved=6 * rows * (4 * width + 2 * hidden),
    )
    return got.a, got.f


def attention(where, pieces, parts, keep, first, carried, last):
    rows = keep.shape[0]
    half = rows // 2
    width = pieces[0].shape[-1] // 4
    heads = width // HEAD
    wide = first[0].shape[1] if first else carried[0].shape[1]

    def body(r):
        w, extra = fetch(r)
        normed = r.n1_out if first else r.n1

        @at_step(0)
        def _():
            if not first:
                r.y_out[...] = r.y[...]
                return
            for at, ref in ((0, r.own), (half, r.far)):
                tokens = ref[...].astype(F32)
                normed[at : at + half] = layer_norm(tokens, r.g1[...], r.s1[...]).astype(LOW)
                r.y_out[at : at + half] = tokens + r.b_out[...]

        terms = extra[...]
        bias_q, bias_v = joined(terms[0:3, :width]), joined(terms[3:6, :width])
        bias = jnp.concatenate([bias_q, jnp.zeros_like(bias_q), bias_v], axis=1)
        low = (mm(normed[...], w[:, : 3 * width]) + bias).astype(LOW)
        r.p[0] = low
        seen = r.keep[...] > 0
        for head in range(heads):
            at = head * HEAD
            query = low[:, at : at + HEAD]
            key = low[:, width + at : width + at + HEAD]
            value = low[:, 2 * width + at : 2 * width + at + HEAD]
            scores = jnp.where(seen, mm(key, query, NT) * HEAD**-0.5, -1e30)
            top = jnp.max(scores, axis=0, keepdims=True)
            exponent = jnp.exp(scores - top)
            total = jnp.sum(exponent, axis=0, keepdims=True)
            probability = (exponent * (1.0 / total)).astype(LOW)
            r.o[0, :, at : at + HEAD] = mm(probability, value, TN).astype(LOW)
            r.l[0, head : head + 1, :] = top + jnp.log(total)
        r.y_out[...] += mm(r.o[0], w[:, 3 * width :], NT)

        if last:

            @at_end()
            def _():
                r.n2[...] = layer_norm(r.y_out[...], r.g2[...], r.s2[...]).astype(LOW)

    line = whole(1, wide)
    ins = [("keep", whole(rows, 1), keep)]
    outs = [
        ("p", part(rows, 3 * width), (parts, rows, 3 * width), LOW),
        ("o", part(rows, width), (parts, rows, width), LOW),
        ("l", part(heads, rows), (parts, heads, rows), F32),
        ("y_out", whole(rows, wide), (rows, wide), F32),
    ]
    if first:
        specs = [whole(half, wide)] * 2 + [line] * 3
        ins += list(zip(("own", "far", "b_out", "g1", "s1"), specs, first))
        outs.append(("n1_out", whole(rows, wide), (rows, wide), LOW))
    else:
        ins += list(zip(("n1", "y"), [whole(rows, wide)] * 2, carried))
    if last:
        ins += list(zip(("g2", "s2"), [line] * 2, last))
        outs.append(("n2", whole(rows, wide), (rows, wide), LOW))
    return call(
        body,
        parts,
        where,
        ins,
        outs,
        fetch_scratch(pieces, 4 * width, parts, wide),
        pieces,
        flops=8 * parts * rows * wide * width + 4 * parts * rows * rows * width,
        moved=8 * parts * wide * width + 12 * rows * wide,
        exps=parts * heads * rows * rows,
        vmem=24 if parts <= 2 else 56,
    )


def forward_up(where, pieces, parts, own, far, branch, residual):
    rows, wide = own.shape
    half = rows // 2
    width = pieces[0].shape[-1] // 2

    def body(r):
        w, extra = fetch(r)

        @at_step(0)
        def _():
            r.both[:rows] = r.own[...]
            r.both[rows:] = r.far[...]
            r.branch_sum[...] = r.branch_in[...]

        hidden = mm(r.both[...], w[:, :width]) + joined(extra[0:3, :width])
        bell = 0.5 * (1.0 + lax.erf(hidden * 0.5**0.5))
        active = (hidden * bell).astype(LOW)
        slope = bell + hidden * jnp.exp(hidden * hidden * -0.5) * 0.3989422804014327
        r.branch_sum[...] += mm(active, w[:, width:], NT)
        r.active[0] = active
        r.slope[0] = slope.astype(LOW)

        @at_end()
        def _():
            r.out_keep[:half] = r.y[:half] + r.branch_sum[:half]
            r.out_keep[half:] = r.branch_sum[rows + half :]
            r.out_send[:half] = (r.y[half:] + r.branch_sum[half:rows]).astype(LOW)
            r.out_send[half:] = r.branch_sum[rows : rows + half].astype(LOW)

    mine = whole(rows, wide)
    shape = (parts, 2 * rows, width)
    return call(
        body,
        parts,
        where,
        [
            ("own", mine, own),
            ("far", mine, far),
            ("branch_in", whole(2 * rows, wide), branch),
            ("y", mine, residual),
        ],
        [
            ("active", part(2 * rows, width), shape, LOW),
            ("slope", part(2 * rows, width), shape, LOW),
            ("out_keep", mine, (rows, wide), F32),
            ("out_send", mine, (rows, wide), LOW),
        ],
        [
            ("both", pltpu.VMEM((2 * rows, wide), LOW)),
            ("branch_sum", pltpu.VMEM((2 * rows, wide), F32)),
        ]
        + fetch_scratch(pieces, 2 * width, parts, wide),
        pieces,
        flops=8 * parts * rows * width * wide,
        moved=4 * parts * wide * width + 12 * rows * wide,
        exps=4 * parts * rows * width,
    )


def forward_down(where, pieces, own, far, grad, carried, active, slope):
    rows, wide = own.shape
    parts, _, width = active.shape

    def body(r):
        w, _ = fetch(r)

        @at_step(0)
        def _():
            r.turned[:, :rows] = r.own[...].T
            r.turned[:, rows:] = r.far[...].T
            r.turned_grad[...] = r.grad[...].T
            r.grad_sum[...] = r.grad_in[...]

        grad_active = mm(r.grad[...], w[:, width:])
        grad_hidden = (grad_active * r.slope[0].astype(F32)).astype(LOW)
        r.db[0] = row_sum(grad_hidden.astype(F32))
        r.grad_sum[...] += mm(grad_hidden, w[:, :width], NT)
        store_gradient(r, [(r.turned, grad_hidden), (r.turned_grad, r.active[0])])

        @at_end()
        def _():
            r.dn_keep[...] = r.grad_sum[:rows]
            r.dn_send[...] = r.grad_sum[rows:].astype(LOW)

    mine, double = whole(rows, wide), whole(2 * rows, wide)
    return call(
        body,
        parts,
        where,
        [
            ("own", mine, own),
            ("far", mine, far),
            ("grad", double, grad),
            ("grad_in", double, carried),
            ("active", part(2 * rows, width), active),
            ("slope", part(2 * rows, width), slope),
        ],
        [
            ("db", part(1, width), (parts, 1, width), F32),
            ("dn_keep", mine, (rows, wide), F32),
            ("dn_send", mine, (rows, wide), LOW),
        ]
        + gradient_outs(parts, wide, 2 * width, True),
        [
            ("turned", pltpu.VMEM((wide, 2 * rows), LOW)),
            ("turned_grad", pltpu.VMEM((wide, 2 * rows), LOW)),
            ("grad_sum", pltpu.VMEM((2 * rows, wide), F32)),
        ]
        + fetch_scratch(pieces, 2 * width, parts, wide),
        pieces,
        flops=16 * parts * rows * width * wide,
        moved=8 * parts * wide * width + 12 * rows * wide,
    )


def forward(where, pieces, parts, own, far, grad, carried, residual, stepwise):
    rows, wide = own.shape
    half = rows // 2
    width = pieces[0].shape[-1] // 2

    def body(r):
        w, extra = fetch(r)

        @at_step(0)
        def _():
            r.both[:rows] = r.own[...]
            r.both[rows:] = r.far[...]
            r.turned[...] = r.both[...].T
            r.turned_grad[...] = r.grad[...].T
            r.branch_sum[...] = r.branch_in[...] if carried else jnp.zeros((2 * rows, wide), F32)
            r.grad_sum[...] = r.grad_in[...] if carried else jnp.zeros((2 * rows, wide), F32)

        hidden = mm(r.both[...], w[:, :width]) + joined(extra[0:3, :width])
        bell = 0.5 * (1.0 + lax.erf(hidden * 0.5**0.5))
        active = (hidden * bell).astype(LOW)
        slope = bell + hidden * jnp.exp(hidden * hidden * -0.5) * 0.3989422804014327
        r.branch_sum[...] += mm(active, w[:, width:], NT)
        grad_hidden = (mm(r.grad[...], w[:, width:]) * slope).astype(LOW)
        r.db[0] = row_sum(grad_hidden.astype(F32))
        r.grad_sum[...] += mm(grad_hidden, w[:, :width], NT)
        store_gradient(r, [(r.turned, grad_hidden), (r.turned_grad, active)])

        if residual is None:
            return

        @at_end()
        def _():
            r.out_keep[:half] = r.y[:half] + r.branch_sum[:half]
            r.out_keep[half:] = r.branch_sum[rows + half :]
            r.out_send[:half] = (r.y[half:] + r.branch_sum[half:rows]).astype(LOW)
            r.out_send[half:] = r.branch_sum[rows : rows + half].astype(LOW)
            r.dn_keep[...] = r.grad_sum[:rows]
            r.dn_send[...] = r.grad_sum[rows:].astype(LOW)

    mine, double = whole(rows, wide), whole(2 * rows, wide)
    sums = [("branch_sum", (2 * rows, wide), F32), ("grad_sum", (2 * rows, wide), F32)]
    ins = [("own", mine, own), ("far", mine, far), ("grad", double, grad)]
    outs = [("db", part(1, width), (parts, 1, width), F32)]
    scratch = [
        ("both", pltpu.VMEM((2 * rows, wide), LOW)),
        ("turned", pltpu.VMEM((wide, 2 * rows), LOW)),
        ("turned_grad", pltpu.VMEM((wide, 2 * rows), LOW)),
    ]
    if carried:
        ins += [("branch_in", double, carried[0]), ("grad_in", double, carried[1])]
    if residual is None:
        outs += [(name, double, shape, kind) for name, shape, kind in sums]
    else:
        ins.append(("y", mine, residual))
        outs += [
            ("out_keep", mine, (rows, wide), F32),
            ("out_send", mine, (rows, wide), LOW),
            ("dn_keep", mine, (rows, wide), F32),
            ("dn_send", mine, (rows, wide), LOW),
        ]
        scratch += [(name, pltpu.VMEM(shape, kind)) for name, shape, kind in sums]
    outs += gradient_outs(parts, wide, 2 * width, stepwise)
    return call(
        body,
        parts,
        where,
        ins,
        outs,
        scratch + fetch_scratch(pieces, 2 * width, parts, wide),
        pieces,
        flops=24 * parts * rows * width * wide,
        moved=8 * parts * wide * width + 12 * rows * wide,
        exps=4 * parts * rows * width,
        vmem=24 if parts <= 2 else 56,
    )


def backward(where, pieces, parts, saved, keep, normed, first, carried, last, stepwise):
    rows, wide = normed.shape
    half = rows // 2
    width = saved.o.shape[2]
    heads = width // HEAD

    def body(r):
        w, _ = fetch(r)
        low_grad = r.dyb_out if first else r.dyb

        @at_step(0)
        def _():
            if first:
                grad_normed = r.dn_keep[...] + r.dn_came[...].astype(F32)
                back, gain_sum, shift_sum = layer_norm_back(r.y[...], r.g2[...], grad_normed)
                grad_out = r.grad[...].astype(F32)
                r.dy_sum[...] = grad_out + back
                low_grad[...] = r.dy_sum[...].astype(LOW)
                r.sums[0:1] = row_sum(low_grad[...].astype(F32))
                r.sums[1:2] = row_sum(grad_out)
                r.sums[2:3] = gain_sum
                r.sums[3:4] = shift_sum
                r.sums[4:8] = jnp.zeros((4, wide), F32)
                r.dn_sum[...] = jnp.zeros_like(r.dn_sum)
            else:
                r.dn_sum[...] = r.dn[...]
            r.turned[...] = r.n1[...].T
            r.turned_grad[...] = low_grad[...].T

        grad_mixed = mm(low_grad[...], w[:, 3 * width :]).astype(LOW)
        seen = r.keep[...] > 0
        for head in range(heads):
            at = head * HEAD
            query = r.p[0, :, at : at + HEAD]
            key = r.p[0, :, width + at : width + at + HEAD]
            value = r.p[0, :, 2 * width + at : 2 * width + at + HEAD]
            grad = grad_mixed[:, at : at + HEAD]
            scores = jnp.where(seen, mm(key, query, NT) * HEAD**-0.5, -1e30)
            probability = jnp.exp(scores - r.l[0, head : head + 1, :])
            grad_probability = mm(value, grad, NT)
            grad_value = mm(probability.astype(LOW), grad)
            inner = jnp.sum(grad_probability * probability, axis=0, keepdims=True)
            grad_scores = (probability * (grad_probability - inner)).astype(LOW)
            grad_query = mm(grad_scores, key, TN) * HEAD**-0.5
            grad_key = mm(grad_scores, query) * HEAD**-0.5
            r.dp[:, at : at + HEAD] = grad_query.astype(LOW)
            r.dp[:, width + at : width + at + HEAD] = grad_key.astype(LOW)
            r.dp[:, 2 * width + at : 2 * width + at + HEAD] = grad_value.astype(LOW)
        r.db[0] = row_sum(r.dp[...].astype(F32))
        r.dn_sum[...] += mm(r.dp[...], w[:, : 3 * width], NT)
        store_gradient(r, [(r.turned, r.dp[...]), (r.turned_grad, r.o[0])])

        if not last:
            return

        @at_end()
        def _():
            dy = r.dy_sum if first else r.dy
            gain_sum = shift_sum = 0.0
            for at, ref, out in ((0, r.own, r.gi_own), (half, r.far, r.gi_far)):
                back, gain_add, shift_add = layer_norm_back(
                    ref[...].astype(F32), r.g1[...], r.dn_sum[at : at + half]
                )
                out[...] = (dy[at : at + half] + back).astype(LOW)
                gain_sum, shift_sum = gain_sum + gain_add, shift_sum + shift_add
            r.end_sums[0:1] = gain_sum
            r.end_sums[1:2] = shift_sum
            r.end_sums[2:8] = jnp.zeros((6, wide), F32)

    mine, line, eight = whole(rows, wide), whole(1, wide), whole(8, wide)
    ins = [
        ("p", part(rows, 3 * width), saved.p),
        ("o", part(rows, width), saved.o),
        ("l", part(heads, rows), saved.l),
        ("keep", whole(rows, 1), keep),
        ("n1", mine, normed),
    ]
    outs = [("db", part(1, 3 * width), (parts, 1, 3 * width), F32)]
    scratch = [
        ("dp", pltpu.VMEM((rows, 3 * width), LOW)),
        ("turned", pltpu.VMEM((wide, rows), LOW)),
        ("turned_grad", pltpu.VMEM((wide, rows), LOW)),
    ]
    sums = [("dn_sum", (rows, wide), F32)]
    if first:
        ins += list(zip(("y", "dn_keep", "dn_came", "grad", "g2"), [mine] * 4 + [line], first))
        outs += [("dyb_out", mine, (rows, wide), LOW), ("sums", eight, (8, wide), F32)]
        sums.append(("dy_sum", (rows, wide), F32))
    else:
        ins += list(zip(("dyb", "dy", "dn"), [mine] * 3, carried))
    if last:
        ins += list(zip(("own", "far", "g1"), [whole(half, wide)] * 2 + [line], last))
        outs += [
            ("gi_own", whole(half, wide), (half, wide), LOW),
            ("gi_far", whole(half, wide), (half, wide), LOW),
            ("end_sums", eight, (8, wide), F32),
        ]
        scratch += [(name, pltpu.VMEM(shape, kind)) for name, shape, kind in sums]
    else:
        outs += [(name, mine, shape, kind) for name, shape, kind in sums]
    outs += gradient_outs(parts, wide, 4 * width, stepwise)
    return call(
        body,
        parts,
        where,
        ins,
        outs,
        scratch + fetch_scratch(pieces, 4 * width, parts, wide),
        pieces,
        placed=("dyb_out", "dy_sum", "dn_sum", "kept", "sent", "gi_own", "gi_far")
        + ("dyb", "dy", "dn"),
        home=pltpu.HBM,
        flops=16 * parts * rows * wide * width + 10 * parts * rows * rows * width,
        moved=16 * parts * wide * width + 16 * rows * wide,
        exps=parts * heads * rows * rows,
        vmem=24 if parts <= 2 else 56,
    )


def spread(where, pieces, parts):
    def body(r):
        for at in range(parts):

            @at_step(at)
            def _(ref=getattr(r, f"piece{at}")):
                r.out[...] = ref[...].astype(F32)

    pair = pieces[0].shape
    block = pl.BlockSpec(pair, lambda t, at: (lax.rem(at[3] - t + parts, parts), 0, 0))
    return call(
        body,
        parts,
        where,
        [(f"piece{at}", whole(*pair), piece) for at, piece in enumerate(pieces)],
        [("out", block, (parts * pair[0],) + pair[1:], F32)],
        moved=6 * parts * pieces[0].size,
    ).out


def forward_total(where, own, far):
    rows, width = own.shape[0], own.shape[1] // 2

    def body(r):
        for flip, ref in ((0, r.own), (1, r.far)):
            block = r.where[0] + flip - 2 * r.where[0] * flip
            span = pl.ds(pl.multiple_of(block * width, width), width)
            r.up[:, span] = ref[:, :width].astype(F32)
            r.down[span, :] = ref[:, width:].astype(F32).T

    got = call(
        body,
        1,
        where,
        [("own", whole(rows, 2 * width), own), ("far", whole(rows, 2 * width), far)],
        [
            ("up", whole(rows, 2 * width), (rows, 2 * width), F32),
            ("down", whole(2 * width, rows), (2 * width, rows), F32),
        ],
        moved=24 * rows * width,
    )
    return got.up, got.down


def attention_total(where, grad):
    rows, width = grad.shape[0], grad.shape[1] // 4

    def body(r):
        for piece in range(3):
            r.qkv[piece] = r.grad[:, piece * width : (piece + 1) * width]
        r.out[...] = r.grad[:, 3 * width :].T

    got = call(
        body,
        1,
        where,
        [("grad", whole(rows, 4 * width), grad)],
        [
            ("qkv", whole(3, rows, width), (3, rows, width), F32),
            ("out", whole(width, rows), (width, rows), F32),
        ],
        moved=32 * rows * width,
    )
    return got.qkv, got.out


def on_device(
    inputs,
    cotangent,
    visible,
    w_qkv,
    b_qv,
    w_out,
    b_out,
    w_up,
    b_up,
    w_down,
    b_down,
    gain_one,
    shift_one,
    gain_two,
    shift_two,
):
    images, half, wide = inputs.shape
    ctx_at, tp_at, fsdp_at = (lax.axis_index(name) for name in ("ctx", "tp", "fsdp"))
    blocks, parts, owners = (lax.axis_size(name) for name in ("ctx", "tp", "fsdp"))
    assert blocks == 2 and images == blocks * parts
    first = blocks * tp_at
    mine, other = first + ctx_at, first + 1 - ctx_at
    where = jnp.stack([ctx_at, fsdp_at % 2, fsdp_at // 2, tp_at]).astype(jnp.int32)
    heads_width = w_qkv.shape[2]
    hidden_half = w_up.shape[1] // 2
    rows = 2 * half

    def swap(values):
        return lax.ppermute(values, "ctx", [(0, 1), (1, 0)])

    def pick(values, index):
        return lax.dynamic_index_in_dim(values, index, 0, keepdims=False)

    def in_order(own, received):
        return jnp.where(ctx_at == 0, own, received), jnp.where(ctx_at == 0, received, own)

    stepwise = owners == 4 and parts == 4
    behind = jnp.mod(tp_at - jnp.arange(parts), parts) if stepwise else jnp.arange(parts)

    def to_core(values):
        return lax.ppermute(values, "fsdp", [(0, 1), (1, 0), (2, 3), (3, 2)])

    def to_y(values):
        return lax.ppermute(values, "fsdp", [(0, 2), (2, 0), (1, 3), (3, 1)])

    def to_tp(values):
        return lax.ppermute(values, "tp", [(i, (i + 1) % parts) for i in range(parts)])

    def gather(shard):
        full = lax.all_gather(shard, ("tp", "fsdp"), axis=0, tiled=True)
        return [full.reshape(parts, owners, *shard.shape)]

    def scatter(gradient):
        flat = gradient.reshape(-1, gradient.shape[2])
        return lax.psum_scatter(flat, ("tp", "fsdp"), scatter_dimension=0, tiled=True)

    def raised(upper, came):
        return upper.astype(F32) + came.astype(F32)

    def onward(total):
        return to_tp(total.astype(LOW))

    tie = lax.optimization_barrier

    a0, b0 = shards(where, w_qkv.transpose(1, 0, 2), w_out, w_up, w_down, b_qv, b_up)
    own = pick(inputs, mine)
    cot_pair = jnp.stack([pick(cotangent, mine), pick(cotangent, other)])
    mine_seen = pick(visible, mine).reshape(blocks, half)
    other_seen = pick(visible, other).reshape(blocks, half)
    keep = jnp.concatenate([pick(mine_seen, ctx_at), pick(mine_seen, 1 - ctx_at)])
    keep_other = jnp.concatenate([pick(other_seen, 1 - ctx_at), pick(other_seen, ctx_at)])
    keep, keep_other = keep[:, None], keep_other[:, None]
    keep_all = jnp.concatenate([keep, keep_other]).astype(LOW)
    norm_one, norm_two = (gain_one[None], shift_one[None]), (gain_two[None], shift_two[None])

    def hidden_gradient(swapped):
        rows_of = [cot_pair[0], swapped[1], swapped[0], cot_pair[1]]
        return jnp.concatenate(rows_of) * keep_all

    def output_pair(kept, came):
        seen = jnp.concatenate([keep[:half], keep_other[half:]]).astype(F32)
        came = came.astype(F32)
        rows_of = kept + jnp.concatenate([came[half:], came[:half]]) + b_down
        rows_of = (rows_of * seen).astype(LOW)
        return jnp.stack(in_order(rows_of[:half], rows_of[half:]))

    if stepwise:
        far = pick(inputs, other)
        a0, b0, a1, ya0, far, cot_pair = tie((a0, b0, to_tp(a0), to_y(a0), far, cot_pair))

        a1, a2, ya1, ca0, cya0, far = tie(
            (a1, to_tp(a1), to_y(a1), to_core(a0), to_core(ya0), swap(far))
        )

        a2, a3, ya2, ca1, cya1 = tie((a2, to_tp(a2), to_y(a2), to_core(a1), to_core(ya1)))

        start = (own, far, b_out[None]) + norm_one
        early = attention(
            where, [a0, ya0, ca0, cya0, a1, ya1, ca1, cya1], 2, keep, start, None, None
        )
        cot_swapped = swap(cot_pair)
        normed, total_y, a3, b0, ya3, b1, ca2, cya2 = tie(
            (
                early.n1_out,
                early.y_out,
                a3,
                b0,
                to_y(a3),
                to_tp(b0),
                to_core(a2),
                to_core(ya2),
            )
        )

        b2, yb0 = to_tp(b1), to_y(b0)
        ca3, cya3 = to_core(a3), to_core(ya3)
        late = attention(
            where,
            [a2, ya2, ca2, cya2, a3, ya3, ca3, cya3],
            2,
            keep,
            None,
            (normed, total_y),
            norm_two,
        )
        normed_two, residual = late.n2, late.y_out
        b2, yb0, cot_swapped = tie((b2, yb0, cot_swapped))
        grad_low = hidden_gradient(cot_swapped)

        normed_far, b3, yb1, cb0, cyb0 = tie(
            (swap(normed_two), to_tp(b2), to_y(b1), to_core(b0), to_core(yb0))
        )

        def block(pieces, carried, last):
            return forward(
                where, pieces, 2, normed_two, normed_far, grad_low, carried, last, True
            )

        yb2, cb1, cyb1 = tie((to_y(b2), to_core(b1), to_core(yb1)))

        f01 = block([b0, yb0, cb0, cyb0, b1, yb1, cb1, cyb1], None, None)
        sums, sent, yb3, cb2, cyb2 = tie(
            (
                (f01.branch_sum, f01.grad_sum),
                f01.sent,
                to_y(b3),
                to_core(b2),
                to_core(yb2),
            )
        )

        came01, cb3, cyb3 = tie((to_core(sent), to_core(b3), to_core(yb3)))

        def upper(got, came, at):
            return to_y(raised(got.kept[1, at], came[1, at]).astype(LOW))

        def lower(got, came, at, lift):
            return raised(got.kept[0, at], came[0, at]) + lift.astype(F32)

        lift1 = upper(f01, came01, 1)
        late_pieces = [b2, yb2, cb2, cyb2, b3, yb3, cb3, cyb3]
        up23 = forward_up(
            where, late_pieces, 2, normed_two, normed_far, sums[0], residual
        )
        out_send, active, slope = tie((up23.out_send, up23.active, up23.slope))

        f23 = forward_down(
            where, late_pieces, normed_two, normed_far, grad_low, sums[1], active, slope
        )
        dn_send, sent, out_came, lift1 = tie((f23.dn_send, f23.sent, swap(out_send), lift1))

        ring_sum = onward(lower(f01, came01, 1, lift1))
        lift0 = upper(f01, came01, 0)
        h0 = output_pair(up23.out_keep, out_came)
        dn_came, came23, lift0, ring_sum, h0 = tie(
            (swap(dn_send), to_core(sent), lift0, ring_sum, h0)
        )

        h1 = to_tp(h0)
        lift2 = upper(f23, came23, 0)
        begin = (residual, f23.dn_keep, dn_came, grad_low[:rows], gain_two[None])
        g_early = backward(
            where,
            [a0, ya0, ca0, cya0, a1, ya1, ca1, cya1],
            2,
            early,
            keep,
            normed,
            begin,
            None,
            None,
            True,
        )
        carried, sent_early, h1, lift2 = tie(
            (
                (g_early.dyb_out, g_early.dy_sum, g_early.dn_sum),
                g_early.sent,
                h1,
                lift2,
            )
        )

        h2 = to_tp(h1)
        lift3 = upper(f23, came23, 1)
        came_early = to_core(sent_early)
        g_late = backward(
            where,
            [a2, ya2, ca2, cya2, a3, ya3, ca3, cya3],
            2,
            late,
            keep,
            normed,
            None,
            carried,
            (own, far, gain_one[None]),
            True,
        )
        gi_far, sent_late, came_early, h2, lift3 = tie(
            (g_late.gi_far, g_late.sent, came_early, h2, lift3)
        )

        quarter = wide // owners // 4

        def rows_of(values, axis, block):
            return lax.dynamic_slice_in_dim(values, block * quarter, quarter, axis)

        def both(kept, came, block):
            return raised(rows_of(kept, 2, block), rows_of(came, 2, block))

        def first_sends(got, came):
            across = swap(both(got.kept, came, 1 - ctx_at).astype(LOW))
            second = raised(got.kept[1, :, 2 * quarter :], came[1, :, 2 * quarter :])
            return across, to_y(second.astype(LOW))

        def second_sends(got, came, across, up):
            near = both(got.kept, came, ctx_at) + across.astype(F32)
            second = raised(got.kept[0, :, 2 * quarter :], came[0, :, 2 * quarter :])
            second = second + up.astype(F32)
            return (
                near[0],
                to_y(near[1].astype(LOW)),
                rows_of(second, 1, ctx_at),
                swap(rows_of(second, 1, 1 - ctx_at).astype(LOW)),
            )

        def third(near, lifted, second, across):
            return jnp.concatenate(
                [near + lifted.astype(F32), second + across.astype(F32)], axis=1
            )

        up_bias = jnp.concatenate([f01.db, f23.db])
        qkv_bias = jnp.concatenate([g_early.db, g_late.db])
        up_bias = lax.dynamic_update_slice(
            jnp.zeros((parts, 2, hidden_half), F32), up_bias, (0, ctx_at, 0)
        )
        small = jnp.concatenate(
            [
                g_early.sums[:4],
                g_late.end_sums[:2],
                up_bias[behind].reshape(-1, wide),
                qkv_bias[behind].reshape(-1, wide),
            ]
        )
        ring_sum = onward(ring_sum.astype(F32) + lower(f23, came23, 0, lift2))
        side0, up0 = first_sends(g_early, came_early)
        gi_far, came_late, small, small_came, ring_sum, up0 = tie(
            (
                swap(gi_far),
                to_core(sent_late),
                small,
                to_core(small),
                ring_sum,
                up0,
            )
        )

        ring_sum = onward(ring_sum.astype(F32) + lower(f23, came23, 1, lift3))
        g0 = jnp.stack(in_order(g_late.gi_own, gi_far))
        side1, up1 = first_sends(g_late, came_late)
        small = small + small_came
        g1, h3, side0, side1, up1, small, small_came = tie(
            (to_tp(g0), to_tp(h2), side0, side1, up1, small, to_y(small))
        )

        sends0 = second_sends(g_early, came_early, side0, up0)
        sends1 = second_sends(g_late, came_late, side1, up1)
        small = small + small_came
        ring_sum, sends0, sends1, small, small_came = tie(
            (ring_sum, sends0, sends1, small, swap(small))
        )

        halves0, halves1 = third(*sends0), third(*sends1)
        total = onward(halves0[1])
        forward_own = (ring_sum.astype(F32) + lower(f01, came01, 0, lift0)).astype(LOW)
        small = small + small_came
        total, forward_far, halves0, halves1, g2, small, small_came = tie(
            (
                total,
                swap(forward_own),
                halves0,
                halves1,
                to_tp(g1),
                small,
                lax.ppermute(small, "tp", [(0, 1), (1, 0), (2, 3), (3, 2)]),
            )
        )

        total = onward(total.astype(F32) + halves1[0])
        up_total, down_total = forward_total(where, forward_own, forward_far)
        result = spread(where, [h0, h1, h2, h3], parts)
        small = small + small_came
        small_came = lax.ppermute(small, "tp", [(0, 2), (2, 0), (1, 3), (3, 1)])
        total, g2, up_total, small, small_came, result = tie(
            (total, g2, up_total, small, small_came, result)
        )

        small = small + small_came

        total = tie(onward(total.astype(F32) + halves1[1]))
        g3 = to_tp(g2)

        mine_half = (total.astype(F32) + halves0[0]).astype(LOW)
        far_half = swap(mine_half)
        lows, highs = in_order(mine_half, far_half)
        attention_sum = jnp.concatenate(
            [lows[:quarter], highs[:quarter], lows[quarter:], highs[quarter:]]
        ).astype(F32)
        qkv_total, out_total = attention_total(where, attention_sum)
        g3, qkv_total = tie((g3, qkv_total))
        grad_inputs = spread(where, [g0, g1, g2, g3], parts)
    else:
        attention_w, forward_w = gather(a0), gather(b0)
        far = swap(pick(inputs, other))
        grad_low = hidden_gradient(swap(cot_pair))
        start = (own, far, b_out[None]) + norm_one
        got = attention(where, attention_w, parts, keep, start, None, norm_two)
        end = forward(
            where,
            forward_w,
            parts,
            got.n2,
            swap(got.n2),
            grad_low,
            None,
            got.y_out,
            False,
        )
        h0 = output_pair(end.out_keep, swap(end.out_send))
        result = lax.all_gather(h0, "tp", axis=0, tiled=True).astype(F32)
        begin = (got.y_out, end.dn_keep, swap(end.dn_send), grad_low[:rows], gain_two[None])
        back = backward(
            where,
            attention_w,
            parts,
            got,
            keep,
            got.n1_out,
            begin,
            None,
            (own, far, gain_one[None]),
            False,
        )
        g0 = jnp.stack(in_order(back.gi_own, swap(back.gi_far)))
        grad_inputs = lax.all_gather(g0, "tp", axis=0, tiled=True).astype(F32)
        forward_own = scatter(end.gradient)
        attention_own = scatter(back.gradient)
        attention_sum = attention_own.astype(F32) + swap(attention_own).astype(F32)
        up_total, down_total = forward_total(where, forward_own, swap(forward_own))
        up_bias = lax.dynamic_update_slice(
            jnp.zeros((parts, 2, hidden_half), F32), end.db, (0, ctx_at, 0)
        )
        small = jnp.concatenate(
            [
                back.sums[:4],
                back.end_sums[:2],
                up_bias.reshape(-1, wide),
                back.db.reshape(-1, wide),
            ]
        )
        small = lax.psum(small, ("fsdp", "ctx", "tp"))
        qkv_total, out_total = attention_total(where, attention_sum)
    up_rows = parts * 2 * hidden_half // wide
    up_small = small[6 : 6 + up_rows].reshape(parts, 2 * hidden_half)
    qkv_small = small[6 + up_rows :].reshape(parts, 3, heads_width)
    return (
        result,
        grad_inputs,
        qkv_total.transpose(1, 0, 2),
        pick(qkv_small, tp_at)[0::2],
        out_total,
        small[0],
        up_total,
        pick(up_small, tp_at),
        down_total,
        small[1],
        small[4],
        small[5],
        small[2],
        small[3],
    )


def solution(mesh):
    placed = (
        P("fsdp", "ctx", None),
        P("fsdp", "ctx", None),
        P("fsdp", None),
        P("fsdp", None, "tp"),
        P(None, "tp"),
        P("tp", "fsdp"),
        P(),
        P("fsdp", "tp"),
        P("tp"),
        P("tp", "fsdp"),
        P(),
        P(),
        P(),
        P(),
        P(),
    )
    return jax.shard_map(
        on_device,
        mesh=mesh,
        in_specs=placed,
        out_specs=(
            P("fsdp", "ctx", None),
            P("fsdp", "ctx", None),
            P("fsdp", None, "tp"),
            P(None, "tp"),
            P("tp", "fsdp"),
            P(),
            P("fsdp", "tp"),
            P("tp"),
            P("tp", "fsdp"),
            P(),
            P(),
            P(),
            P(),
            P(),
        ),
        check_vma=False,
    )
```

```python
import types

import jax
import jax.numpy as jnp
from jax import lax
from jax.experimental import pallas as pl
from jax.experimental.pallas import tpu as pltpu
from jax.sharding import PartitionSpec as P

HEAD = 64
EPSILON = 1e-06
EXTRA = 16
F32 = jnp.float32
LOW = jnp.bfloat16

NN = (((1,), (0,)), ((), ()))
NT = (((1,), (1,)), ((), ()))
TN = (((0,), (0,)), ((), ()))


def mm(left, right, dims=NN):
    return lax.dot_general(left, right, dims, preferred_element_type=F32)


def whole(*shape):
    return pl.BlockSpec(shape, lambda t, _: (0,) * len(shape))


def part(*shape):
    return pl.BlockSpec((1,) + shape, lambda t, _: (t,) + (0,) * len(shape))


def call(
    body, grid, where, ins, outs, scratch=(), pieces=(), flops=0, moved=0, exps=0, vmem=24, placed=(), home=pltpu.HBM
):
    names = [entry[0] for entry in ins]
    later = [entry[0] for entry in outs] + [entry[0] for entry in scratch]

    def kernel(where_ref, *refs):
        r = types.SimpleNamespace(where=where_ref)
        count = len(names) + len(pieces)
        r.pieces = refs[len(names) : count]
        for name, ref in zip(names + later, refs[: len(names)] + refs[count:]):
            setattr(r, name, ref)
        body(r)

    results = pl.pallas_call(
        kernel,
        grid_spec=pltpu.PrefetchScalarGridSpec(
            num_scalar_prefetch=1,
            grid=(grid,),
            in_specs=[entry[1] for entry in ins]
            + [pl.BlockSpec(memory_space=home)] * len(pieces),
            out_specs=[entry[1] for entry in outs],
            scratch_shapes=[entry[1] for entry in scratch],
        ),
        out_shape=[
            (pltpu.HBM if entry[0] in placed else jax.ShapeDtypeStruct)(entry[2], entry[3])
            for entry in outs
        ],
        compiler_params=pltpu.CompilerParams(
            dimension_semantics=("arbitrary",), vmem_limit_bytes=vmem << 20
        ),
        cost_estimate=pl.CostEstimate(flops=flops, bytes_accessed=moved, transcendentals=exps),
    )(
        where,
        *(
            pltpu.with_memory_space_constraint(entry[2], pltpu.HBM)
            if entry[0] in placed
            else entry[2]
            for entry in ins
        ),
        *(pltpu.with_memory_space_constraint(piece, home) for piece in pieces),
    )
    return types.SimpleNamespace(**{entry[0]: value for entry, value in zip(outs, results)})


def at_step(step):
    return pl.when(pl.program_id(0) == step)


def at_end():
    return pl.when(pl.program_id(0) == pl.num_programs(0) - 1)


def layer_norm(values, gain, shift):
    center = values - jnp.mean(values, axis=-1, keepdims=True)
    spread = jnp.mean(center * center, axis=-1, keepdims=True)
    return center * lax.rsqrt(spread + EPSILON) * gain + shift


def layer_norm_back(values, gain, grad):
    center = values - jnp.mean(values, axis=-1, keepdims=True)
    scale = lax.rsqrt(jnp.mean(center * center, axis=-1, keepdims=True) + EPSILON)
    unit = center * scale
    scaled = grad * gain
    back = scale * (
        scaled
        - jnp.mean(scaled, axis=-1, keepdims=True)
        - unit * jnp.mean(scaled * unit, axis=-1, keepdims=True)
    )
    return back, row_sum(grad * unit), row_sum(grad)


def row_sum(values):
    return jnp.sum(values, axis=0, keepdims=True)


def fetch_scratch(pieces, width, parts, wide):
    copies = pieces[0].shape[1] if len(pieces) == 1 else 4
    return [
        ("weights", pltpu.VMEM((parts, wide, width), LOW)),
        ("extras", pltpu.VMEM((parts, EXTRA, width), LOW)),
        ("sems", pltpu.SemaphoreType.DMA((parts, copies + 1))),
    ]


def fetch(r):
    parts = r.weights.shape[0]

    def copies(at):
        if len(r.pieces) == 1:
            sources = [r.pieces[0].at[at, owner] for owner in range(r.pieces[0].shape[1])]
            owners = list(range(len(sources)))
        else:
            core, row = r.where[1], r.where[2]
            sources = [r.pieces[4 * at + which] for which in range(4)]
            owners = [
                2 * (row + up - 2 * row * up) + (core + over - 2 * core * over)
                for over in range(2)
                for up in range(2)
            ]
        rows = sources[0].shape[0] - EXTRA
        extra = sources[0].at[pl.ds(rows, EXTRA), :]
        result = [pltpu.make_async_copy(extra, r.extras.at[at], r.sems.at[at, len(sources)])]
        for which, (source, owner) in enumerate(zip(sources, owners)):
            target = r.weights.at[at, pl.ds(pl.multiple_of(owner * rows, rows), rows), :]
            result.append(
                pltpu.make_async_copy(source.at[pl.ds(0, rows), :], target, r.sems.at[at, which])
            )
        return result

    @at_step(0)
    def _():
        for at in range(parts):
            for copy in copies(at):
                copy.start()

    def wait(at):
        @at_step(at)
        def _():
            for copy in copies(at):
                copy.wait()

    for at in range(parts):
        wait(at)
    return r.weights.at[pl.program_id(0)], r.extras.at[pl.program_id(0)]


def joined(terms):
    wide = terms.astype(F32)
    return wide[0:1] + (wide[1:2] + wide[2:3])


def gradient_outs(parts, wide, total, stepwise):
    if not stepwise:
        return [("gradient", part(wide, total), (parts, wide, total), LOW)]
    shape = (2, parts, wide // 4, total)
    block = pl.BlockSpec((2, 1, wide // 4, total), lambda t, _: (0, t, 0, 0))
    return [("kept", block, shape, LOW), ("sent", block, shape, LOW)]


def store_gradient(r, pairs):
    column = 0
    for turned, right in pairs:
        span = slice(column, column + right.shape[1])
        column += right.shape[1]
        if hasattr(r, "gradient"):
            r.gradient[0, :, span] = mm(turned[...], right).astype(LOW)
            continue
        core, row = r.where[1], r.where[2]
        rows = r.kept.shape[2]
        for which, out in enumerate((r.kept, r.sent)):
            for far in range(2):
                owner = 2 * (row + far - 2 * row * far) + (core + which - 2 * core * which)
                start = pl.multiple_of(owner * rows, rows)
                out[far, 0, :, span] = mm(turned[pl.ds(start, rows), :], right).astype(LOW)


def shards_body(r):
    rows, width = r.qkv.shape[1:]
    hidden = r.up.shape[1]
    for piece in range(3):
        r.a[:rows, piece * width : (piece + 1) * width] = r.qkv[piece].astype(LOW)
    r.a[:rows, 3 * width :] = r.out[...].T.astype(LOW)
    r.f[:rows, :hidden] = r.up[...].astype(LOW)
    r.f[:rows, hidden:] = r.down[...].T.astype(LOW)
    r.a[rows:] = jnp.zeros((EXTRA, 4 * width), LOW)
    r.f[rows:] = jnp.zeros((EXTRA, 2 * hidden), LOW)
    for ref, row, shard in ((r.bqv, 0, r.a), (r.bqv, 1, r.a), (r.bup, 0, r.f)):
        left = ref[row : row + 1, :]
        for piece in range(3):
            low = left.astype(LOW)
            left = left - low.astype(F32)
            at = rows + 3 * row + piece
            shard[at : at + 1, : low.shape[1]] = low


def shards(where, w_qkv, w_out, w_up, w_down, b_qv, b_up):
    _, rows, width = w_qkv.shape
    hidden = w_up.shape[1] // 2
    got = call(
        shards_body,
        1,
        where,
        [
            ("qkv", whole(3, rows, width), w_qkv),
            ("out", whole(width, rows), w_out),
            ("up", pl.BlockSpec((rows, hidden), lambda t, at: (0, at[0])), w_up),
            ("down", pl.BlockSpec((hidden, rows), lambda t, at: (at[0], 0)), w_down),
            ("bqv", whole(2, width), b_qv),
            ("bup", pl.BlockSpec((1, hidden), lambda t, at: (0, at[0])), b_up[None]),
        ],
        [
            ("a", whole(rows + EXTRA, 4 * width), (rows + EXTRA, 4 * width), LOW),
            ("f", whole(rows + EXTRA, 2 * hidden), (rows + EXTRA, 2 * hidden), LOW),
        ],
        moved=6 * rows * (4 * width + 2 * hidden),
    )
    return got.a, got.f


def attention(where, pieces, parts, keep, first, carried, last):
    rows = keep.shape[0]
    half = rows // 2
    width = pieces[0].shape[-1] // 4
    heads = width // HEAD
    wide = first[0].shape[1] if first else carried[0].shape[1]

    def body(r):
        w, extra = fetch(r)
        normed = r.n1_out if first else r.n1

        @at_step(0)
        def _():
            if not first:
                r.y_out[...] = r.y[...]
                return
            for at, ref in ((0, r.own), (half, r.far)):
                tokens = ref[...].astype(F32)
                normed[at : at + half] = layer_norm(tokens, r.g1[...], r.s1[...]).astype(LOW)
                r.y_out[at : at + half] = tokens + r.b_out[...]

        terms = extra[...]
        bias_q, bias_v = joined(terms[0:3, :width]), joined(terms[3:6, :width])
        bias = jnp.concatenate([bias_q, jnp.zeros_like(bias_q), bias_v], axis=1)
        low = (mm(normed[...], w[:, : 3 * width]) + bias).astype(LOW)
        r.p[0] = low
        seen = r.keep[...] > 0

        @pl.loop(0, heads // 2)
        def _(pair):
            base = pl.multiple_of(pair * 2 * HEAD, 2 * HEAD)
            mixed = []
            for side in range(2):
                at = slice(side * HEAD, (side + 1) * HEAD)
                query = r.p[0, :, pl.ds(base, 2 * HEAD)][:, at]
                key = r.p[0, :, pl.ds(width + base, 2 * HEAD)][:, at]
                value = r.p[0, :, pl.ds(2 * width + base, 2 * HEAD)][:, at]
                scores = jnp.where(seen, mm(key, query, NT) * HEAD**-0.5, -1e30)
                top = jnp.max(scores, axis=0, keepdims=True)
                exponent = jnp.exp(scores - top)
                total = jnp.sum(exponent, axis=0, keepdims=True)
                probability = (exponent * (1.0 / total)).astype(LOW)
                mixed.append(mm(probability, value, TN))
                r.l[0, pl.ds(2 * pair + side, 1), :] = top + jnp.log(total)
            r.o[0, :, pl.ds(base, 2 * HEAD)] = jnp.concatenate(mixed, axis=1).astype(LOW)

        r.y_out[...] += mm(r.o[0], w[:, 3 * width :], NT)

        if last:

            @at_end()
            def _():
                r.n2[...] = layer_norm(r.y_out[...], r.g2[...], r.s2[...]).astype(LOW)

    line = whole(1, wide)
    ins = [("keep", whole(rows, 1), keep)]
    outs = [
        ("p", part(rows, 3 * width), (parts, rows, 3 * width), LOW),
        ("o", part(rows, width), (parts, rows, width), LOW),
        ("l", part(heads, rows), (parts, heads, rows), F32),
        ("y_out", whole(rows, wide), (rows, wide), F32),
    ]
    if first:
        specs = [whole(half, wide)] * 2 + [line] * 3
        ins += list(zip(("own", "far", "b_out", "g1", "s1"), specs, first))
        outs.append(("n1_out", whole(rows, wide), (rows, wide), LOW))
    else:
        ins += list(zip(("n1", "y"), [whole(rows, wide)] * 2, carried))
    if last:
        ins += list(zip(("g2", "s2"), [line] * 2, last))
        outs.append(("n2", whole(rows, wide), (rows, wide), LOW))
    return call(
        body,
        parts,
        where,
        ins,
        outs,
        fetch_scratch(pieces, 4 * width, parts, wide),
        pieces,
        flops=8 * parts * rows * wide * width + 4 * parts * rows * rows * width,
        moved=8 * parts * wide * width + 12 * rows * wide,
        exps=parts * heads * rows * rows,
        vmem=24 if parts <= 2 else 56,
    )


def forward_up(where, pieces, parts, own, far, branch, residual):
    rows, wide = own.shape
    half = rows // 2
    width = pieces[0].shape[-1] // 2

    def body(r):
        w, extra = fetch(r)

        @at_step(0)
        def _():
            r.both[:rows] = r.own[...]
            r.both[rows:] = r.far[...]
            r.branch_sum[...] = r.branch_in[...]

        hidden = mm(r.both[...], w[:, :width]) + joined(extra[0:3, :width])
        bell = 0.5 * (1.0 + lax.erf(hidden * 0.5**0.5))
        active = (hidden * bell).astype(LOW)
        slope = bell + hidden * jnp.exp(hidden * hidden * -0.5) * 0.3989422804014327
        r.branch_sum[...] += mm(active, w[:, width:], NT)
        r.active[0] = active
        r.slope[0] = slope.astype(LOW)

        @at_end()
        def _():
            r.out_keep[:half] = r.y[:half] + r.branch_sum[:half]
            r.out_keep[half:] = r.branch_sum[rows + half :]
            r.out_send[:half] = (r.y[half:] + r.branch_sum[half:rows]).astype(LOW)
            r.out_send[half:] = r.branch_sum[rows : rows + half].astype(LOW)

    mine = whole(rows, wide)
    shape = (parts, 2 * rows, width)
    return call(
        body,
        parts,
        where,
        [
            ("own", mine, own),
            ("far", mine, far),
            ("branch_in", whole(2 * rows, wide), branch),
            ("y", mine, residual),
        ],
        [
            ("active", part(2 * rows, width), shape, LOW),
            ("slope", part(2 * rows, width), shape, LOW),
            ("out_keep", mine, (rows, wide), F32),
            ("out_send", mine, (rows, wide), LOW),
        ],
        [
            ("both", pltpu.VMEM((2 * rows, wide), LOW)),
            ("branch_sum", pltpu.VMEM((2 * rows, wide), F32)),
        ]
        + fetch_scratch(pieces, 2 * width, parts, wide),
        pieces,
        flops=8 * parts * rows * width * wide,
        moved=4 * parts * wide * width + 12 * rows * wide,
        exps=4 * parts * rows * width,
    )


def forward_down(where, pieces, own, far, grad, carried, active, slope):
    rows, wide = own.shape
    parts, _, width = active.shape

    def body(r):
        w, _ = fetch(r)

        @at_step(0)
        def _():
            r.turned[:, :rows] = r.own[...].T
            r.turned[:, rows:] = r.far[...].T
            r.turned_grad[...] = r.grad[...].T
            r.grad_sum[...] = r.grad_in[...]

        grad_active = mm(r.grad[...], w[:, width:])
        grad_hidden = (grad_active * r.slope[0].astype(F32)).astype(LOW)
        r.db[0] = row_sum(grad_hidden.astype(F32))
        r.grad_sum[...] += mm(grad_hidden, w[:, :width], NT)
        store_gradient(r, [(r.turned, grad_hidden), (r.turned_grad, r.active[0])])

        @at_end()
        def _():
            r.dn_keep[...] = r.grad_sum[:rows]
            r.dn_send[...] = r.grad_sum[rows:].astype(LOW)

    mine, double = whole(rows, wide), whole(2 * rows, wide)
    return call(
        body,
        parts,
        where,
        [
            ("own", mine, own),
            ("far", mine, far),
            ("grad", double, grad),
            ("grad_in", double, carried),
            ("active", part(2 * rows, width), active),
            ("slope", part(2 * rows, width), slope),
        ],
        [
            ("db", part(1, width), (parts, 1, width), F32),
            ("dn_keep", mine, (rows, wide), F32),
            ("dn_send", mine, (rows, wide), LOW),
        ]
        + gradient_outs(parts, wide, 2 * width, True),
        [
            ("turned", pltpu.VMEM((wide, 2 * rows), LOW)),
            ("turned_grad", pltpu.VMEM((wide, 2 * rows), LOW)),
            ("grad_sum", pltpu.VMEM((2 * rows, wide), F32)),
        ]
        + fetch_scratch(pieces, 2 * width, parts, wide),
        pieces,
        flops=16 * parts * rows * width * wide,
        moved=8 * parts * wide * width + 12 * rows * wide,
    )


def forward(where, pieces, parts, own, far, grad, carried, residual, stepwise):
    rows, wide = own.shape
    half = rows // 2
    width = pieces[0].shape[-1] // 2

    def body(r):
        w, extra = fetch(r)

        @at_step(0)
        def _():
            r.both[:rows] = r.own[...]
            r.both[rows:] = r.far[...]
            r.turned[...] = r.both[...].T
            r.turned_grad[...] = r.grad[...].T
            r.branch_sum[...] = r.branch_in[...] if carried else jnp.zeros((2 * rows, wide), F32)
            r.grad_sum[...] = r.grad_in[...] if carried else jnp.zeros((2 * rows, wide), F32)

        hidden = mm(r.both[...], w[:, :width]) + joined(extra[0:3, :width])
        bell = 0.5 * (1.0 + lax.erf(hidden * 0.5**0.5))
        active = (hidden * bell).astype(LOW)
        slope = bell + hidden * jnp.exp(hidden * hidden * -0.5) * 0.3989422804014327
        r.branch_sum[...] += mm(active, w[:, width:], NT)
        grad_hidden = (mm(r.grad[...], w[:, width:]) * slope).astype(LOW)
        r.db[0] = row_sum(grad_hidden.astype(F32))
        r.grad_sum[...] += mm(grad_hidden, w[:, :width], NT)
        store_gradient(r, [(r.turned, grad_hidden), (r.turned_grad, active)])

        if residual is None:
            return

        @at_end()
        def _():
            r.out_keep[:half] = r.y[:half] + r.branch_sum[:half]
            r.out_keep[half:] = r.branch_sum[rows + half :]
            r.out_send[:half] = (r.y[half:] + r.branch_sum[half:rows]).astype(LOW)
            r.out_send[half:] = r.branch_sum[rows : rows + half].astype(LOW)
            r.dn_keep[...] = r.grad_sum[:rows]
            r.dn_send[...] = r.grad_sum[rows:].astype(LOW)

    mine, double = whole(rows, wide), whole(2 * rows, wide)
    sums = [("branch_sum", (2 * rows, wide), F32), ("grad_sum", (2 * rows, wide), F32)]
    ins = [("own", mine, own), ("far", mine, far), ("grad", double, grad)]
    outs = [("db", part(1, width), (parts, 1, width), F32)]
    scratch = [
        ("both", pltpu.VMEM((2 * rows, wide), LOW)),
        ("turned", pltpu.VMEM((wide, 2 * rows), LOW)),
        ("turned_grad", pltpu.VMEM((wide, 2 * rows), LOW)),
    ]
    if carried:
        ins += [("branch_in", double, carried[0]), ("grad_in", double, carried[1])]
    if residual is None:
        outs += [(name, double, shape, kind) for name, shape, kind in sums]
    else:
        ins.append(("y", mine, residual))
        outs += [
            ("out_keep", mine, (rows, wide), F32),
            ("out_send", mine, (rows, wide), LOW),
            ("dn_keep", mine, (rows, wide), F32),
            ("dn_send", mine, (rows, wide), LOW),
        ]
        scratch += [(name, pltpu.VMEM(shape, kind)) for name, shape, kind in sums]
    outs += gradient_outs(parts, wide, 2 * width, stepwise)
    return call(
        body,
        parts,
        where,
        ins,
        outs,
        scratch + fetch_scratch(pieces, 2 * width, parts, wide),
        pieces,
        flops=24 * parts * rows * width * wide,
        moved=8 * parts * wide * width + 12 * rows * wide,
        exps=4 * parts * rows * width,
        vmem=24 if parts <= 2 else 56,
    )


def backward(where, pieces, parts, saved, keep, normed, first, carried, last, stepwise):
    rows, wide = normed.shape
    half = rows // 2
    width = saved.o.shape[2]
    heads = width // HEAD

    def body(r):
        w, _ = fetch(r)
        low_grad = r.dyb_out if first else r.dyb

        @at_step(0)
        def _():
            if first:
                grad_normed = r.dn_keep[...] + r.dn_came[...].astype(F32)
                back, gain_sum, shift_sum = layer_norm_back(r.y[...], r.g2[...], grad_normed)
                grad_out = r.grad[...].astype(F32)
                r.dy_sum[...] = grad_out + back
                low_grad[...] = r.dy_sum[...].astype(LOW)
                r.sums[0:1] = row_sum(low_grad[...].astype(F32))
                r.sums[1:2] = row_sum(grad_out)
                r.sums[2:3] = gain_sum
                r.sums[3:4] = shift_sum
                r.sums[4:8] = jnp.zeros((4, wide), F32)
                r.dn_sum[...] = jnp.zeros_like(r.dn_sum)
            else:
                r.dn_sum[...] = r.dn[...]
            r.turned[...] = r.n1[...].T
            r.turned_grad[...] = low_grad[...].T

        grad_mixed = mm(low_grad[...], w[:, 3 * width :]).astype(LOW)
        r.mixed[...] = grad_mixed
        seen = r.keep[...] > 0

        @pl.loop(0, heads // 2)
        def _(pair):
            base = pl.multiple_of(pair * 2 * HEAD, 2 * HEAD)
            grads = ([], [], [])
            for side in range(2):
                at = slice(side * HEAD, (side + 1) * HEAD)
                query = r.p[0, :, pl.ds(base, 2 * HEAD)][:, at]
                key = r.p[0, :, pl.ds(width + base, 2 * HEAD)][:, at]
                value = r.p[0, :, pl.ds(2 * width + base, 2 * HEAD)][:, at]
                grad = r.mixed[:, pl.ds(base, 2 * HEAD)][:, at]
                scores = jnp.where(seen, mm(key, query, NT) * HEAD**-0.5, -1e30)
                probability = jnp.exp(scores - r.l[0, pl.ds(2 * pair + side, 1), :])
                grad_probability = mm(value, grad, NT)
                grads[2].append(mm(probability.astype(LOW), grad))
                inner = jnp.sum(grad_probability * probability, axis=0, keepdims=True)
                grad_scores = (probability * (grad_probability - inner)).astype(LOW)
                grads[0].append(mm(grad_scores, key, TN) * HEAD**-0.5)
                grads[1].append(mm(grad_scores, query) * HEAD**-0.5)
            for which, pieces in enumerate(grads):
                joint = jnp.concatenate(pieces, axis=1).astype(LOW)
                r.dp[:, pl.ds(which * width + base, 2 * HEAD)] = joint

        r.db[0] = row_sum(r.dp[...].astype(F32))
        r.dn_sum[...] += mm(r.dp[...], w[:, : 3 * width], NT)
        store_gradient(r, [(r.turned, r.dp[...]), (r.turned_grad, r.o[0])])

        if not last:
            return

        @at_end()
        def _():
            dy = r.dy_sum if first else r.dy
            gain_sum = shift_sum = 0.0
            for at, ref, out in ((0, r.own, r.gi_own), (half, r.far, r.gi_far)):
                back, gain_add, shift_add = layer_norm_back(
                    ref[...].astype(F32), r.g1[...], r.dn_sum[at : at + half]
                )
                out[...] = (dy[at : at + half] + back).astype(LOW)
                gain_sum, shift_sum = gain_sum + gain_add, shift_sum + shift_add
            r.end_sums[0:1] = gain_sum
            r.end_sums[1:2] = shift_sum
            r.end_sums[2:8] = jnp.zeros((6, wide), F32)

    mine, line, eight = whole(rows, wide), whole(1, wide), whole(8, wide)
    ins = [
        ("p", part(rows, 3 * width), saved.p),
        ("o", part(rows, width), saved.o),
        ("l", part(heads, rows), saved.l),
        ("keep", whole(rows, 1), keep),
        ("n1", mine, normed),
    ]
    outs = [("db", part(1, 3 * width), (parts, 1, 3 * width), F32)]
    scratch = [
        ("dp", pltpu.VMEM((rows, 3 * width), LOW)),
        ("mixed", pltpu.VMEM((rows, width), LOW)),
        ("turned", pltpu.VMEM((wide, rows), LOW)),
        ("turned_grad", pltpu.VMEM((wide, rows), LOW)),
    ]
    sums = [("dn_sum", (rows, wide), F32)]
    if first:
        ins += list(zip(("y", "dn_keep", "dn_came", "grad", "g2"), [mine] * 4 + [line], first))
        outs += [("dyb_out", mine, (rows, wide), LOW), ("sums", eight, (8, wide), F32)]
        sums.append(("dy_sum", (rows, wide), F32))
    else:
        ins += list(zip(("dyb", "dy", "dn"), [mine] * 3, carried))
    if last:
        ins += list(zip(("own", "far", "g1"), [whole(half, wide)] * 2 + [line], last))
        outs += [
            ("gi_own", whole(half, wide), (half, wide), LOW),
            ("gi_far", whole(half, wide), (half, wide), LOW),
            ("end_sums", eight, (8, wide), F32),
        ]
        scratch += [(name, pltpu.VMEM(shape, kind)) for name, shape, kind in sums]
    else:
        outs += [(name, mine, shape, kind) for name, shape, kind in sums]
    outs += gradient_outs(parts, wide, 4 * width, stepwise)
    return call(
        body,
        parts,
        where,
        ins,
        outs,
        scratch + fetch_scratch(pieces, 4 * width, parts, wide),
        pieces,
        placed=("dyb_out", "dy_sum", "dn_sum", "kept", "sent", "gi_own", "gi_far")
        + ("dyb", "dy", "dn"),
        home=pltpu.HBM,
        flops=16 * parts * rows * wide * width + 10 * parts * rows * rows * width,
        moved=16 * parts * wide * width + 16 * rows * wide,
        exps=parts * heads * rows * rows,
        vmem=24 if parts <= 2 else 56,
    )


def spread(where, pieces, parts):
    def body(r):
        for at in range(parts):

            @at_step(at)
            def _(ref=getattr(r, f"piece{at}")):
                r.out[...] = ref[...].astype(F32)

    pair = pieces[0].shape
    block = pl.BlockSpec(pair, lambda t, at: (lax.rem(at[3] - t + parts, parts), 0, 0))
    return call(
        body,
        parts,
        where,
        [(f"piece{at}", whole(*pair), piece) for at, piece in enumerate(pieces)],
        [("out", block, (parts * pair[0],) + pair[1:], F32)],
        moved=6 * parts * pieces[0].size,
    ).out


def forward_total(where, own, far):
    rows, width = own.shape[0], own.shape[1] // 2

    def body(r):
        for flip, ref in ((0, r.own), (1, r.far)):
            block = r.where[0] + flip - 2 * r.where[0] * flip
            span = pl.ds(pl.multiple_of(block * width, width), width)
            r.up[:, span] = ref[:, :width].astype(F32)
            r.down[span, :] = ref[:, width:].astype(F32).T

    got = call(
        body,
        1,
        where,
        [("own", whole(rows, 2 * width), own), ("far", whole(rows, 2 * width), far)],
        [
            ("up", whole(rows, 2 * width), (rows, 2 * width), F32),
            ("down", whole(2 * width, rows), (2 * width, rows), F32),
        ],
        moved=24 * rows * width,
    )
    return got.up, got.down


def attention_total(where, grad):
    rows, width = grad.shape[0], grad.shape[1] // 4

    def body(r):
        for piece in range(3):
            r.qkv[piece] = r.grad[:, piece * width : (piece + 1) * width]
        r.out[...] = r.grad[:, 3 * width :].T

    got = call(
        body,
        1,
        where,
        [("grad", whole(rows, 4 * width), grad)],
        [
            ("qkv", whole(3, rows, width), (3, rows, width), F32),
            ("out", whole(width, rows), (width, rows), F32),
        ],
        moved=32 * rows * width,
    )
    return got.qkv, got.out


def on_device(
    inputs,
    cotangent,
    visible,
    w_qkv,
    b_qv,
    w_out,
    b_out,
    w_up,
    b_up,
    w_down,
    b_down,
    gain_one,
    shift_one,
    gain_two,
    shift_two,
):
    images, half, wide = inputs.shape
    ctx_at, tp_at, fsdp_at = (lax.axis_index(name) for name in ("ctx", "tp", "fsdp"))
    blocks, parts, owners = (lax.axis_size(name) for name in ("ctx", "tp", "fsdp"))
    assert blocks == 2 and images == blocks * parts
    first = blocks * tp_at
    mine, other = first + ctx_at, first + 1 - ctx_at
    where = jnp.stack([ctx_at, fsdp_at % 2, fsdp_at // 2, tp_at]).astype(jnp.int32)
    heads_width = w_qkv.shape[2]
    hidden_half = w_up.shape[1] // 2
    rows = 2 * half

    def swap(values):
        return lax.ppermute(values, "ctx", [(0, 1), (1, 0)])

    def pick(values, index):
        return lax.dynamic_index_in_dim(values, index, 0, keepdims=False)

    def in_order(own, received):
        return jnp.where(ctx_at == 0, own, received), jnp.where(ctx_at == 0, received, own)

    stepwise = owners == 4 and parts == 4
    behind = jnp.mod(tp_at - jnp.arange(parts), parts) if stepwise else jnp.arange(parts)

    def to_core(values):
        return lax.ppermute(values, "fsdp", [(0, 1), (1, 0), (2, 3), (3, 2)])

    def to_y(values):
        return lax.ppermute(values, "fsdp", [(0, 2), (2, 0), (1, 3), (3, 1)])

    def to_tp(values):
        return lax.ppermute(values, "tp", [(i, (i + 1) % parts) for i in range(parts)])

    def gather(shard):
        full = lax.all_gather(shard, ("tp", "fsdp"), axis=0, tiled=True)
        return [full.reshape(parts, owners, *shard.shape)]

    def scatter(gradient):
        flat = gradient.reshape(-1, gradient.shape[2])
        return lax.psum_scatter(flat, ("tp", "fsdp"), scatter_dimension=0, tiled=True)

    def raised(upper, came):
        return upper.astype(F32) + came.astype(F32)

    def onward(total):
        return to_tp(total.astype(LOW))

    tie = lax.optimization_barrier

    a0, b0 = shards(where, w_qkv.transpose(1, 0, 2), w_out, w_up, w_down, b_qv, b_up)
    own = pick(inputs, mine)
    cot_pair = jnp.stack([pick(cotangent, mine), pick(cotangent, other)])
    mine_seen = pick(visible, mine).reshape(blocks, half)
    other_seen = pick(visible, other).reshape(blocks, half)
    keep = jnp.concatenate([pick(mine_seen, ctx_at), pick(mine_seen, 1 - ctx_at)])
    keep_other = jnp.concatenate([pick(other_seen, 1 - ctx_at), pick(other_seen, ctx_at)])
    keep, keep_other = keep[:, None], keep_other[:, None]
    keep_all = jnp.concatenate([keep, keep_other]).astype(LOW)
    norm_one, norm_two = (gain_one[None], shift_one[None]), (gain_two[None], shift_two[None])

    def hidden_gradient(swapped):
        rows_of = [cot_pair[0], swapped[1], swapped[0], cot_pair[1]]
        return jnp.concatenate(rows_of) * keep_all

    def output_pair(kept, came):
        seen = jnp.concatenate([keep[:half], keep_other[half:]]).astype(F32)
        came = came.astype(F32)
        rows_of = kept + jnp.concatenate([came[half:], came[:half]]) + b_down
        rows_of = (rows_of * seen).astype(LOW)
        return jnp.stack(in_order(rows_of[:half], rows_of[half:]))

    if stepwise:
        far = pick(inputs, other)
        a0, b0, a1, ya0, far, cot_pair = tie((a0, b0, to_tp(a0), to_y(a0), far, cot_pair))

        a1, a2, ya1, ca0, cya0, far = tie(
            (a1, to_tp(a1), to_y(a1), to_core(a0), to_core(ya0), swap(far))
        )

        a2, a3, ya2, ca1, cya1 = tie((a2, to_tp(a2), to_y(a2), to_core(a1), to_core(ya1)))

        start = (own, far, b_out[None]) + norm_one
        early = attention(
            where, [a0, ya0, ca0, cya0, a1, ya1, ca1, cya1], 2, keep, start, None, None
        )
        cot_swapped = swap(cot_pair)
        normed, total_y, a3, b0, ya3, b1, ca2, cya2 = tie(
            (
                early.n1_out,
                early.y_out,
                a3,
                b0,
                to_y(a3),
                to_tp(b0),
                to_core(a2),
                to_core(ya2),
            )
        )

        b2, yb0 = to_tp(b1), to_y(b0)
        ca3, cya3 = to_core(a3), to_core(ya3)
        late = attention(
            where,
            [a2, ya2, ca2, cya2, a3, ya3, ca3, cya3],
            2,
            keep,
            None,
            (normed, total_y),
            norm_two,
        )
        normed_two, residual = late.n2, late.y_out
        b2, yb0, cot_swapped = tie((b2, yb0, cot_swapped))
        grad_low = hidden_gradient(cot_swapped)

        normed_far, b3, yb1, cb0, cyb0 = tie(
            (swap(normed_two), to_tp(b2), to_y(b1), to_core(b0), to_core(yb0))
        )

        def block(pieces, carried, last):
            return forward(
                where, pieces, 2, normed_two, normed_far, grad_low, carried, last, True
            )

        yb2, cb1, cyb1 = tie((to_y(b2), to_core(b1), to_core(yb1)))

        f01 = block([b0, yb0, cb0, cyb0, b1, yb1, cb1, cyb1], None, None)
        sums, sent, yb3, cb2, cyb2 = tie(
            (
                (f01.branch_sum, f01.grad_sum),
                f01.sent,
                to_y(b3),
                to_core(b2),
                to_core(yb2),
            )
        )

        came01, cb3, cyb3 = tie((to_core(sent), to_core(b3), to_core(yb3)))

        def upper(got, came, at):
            return to_y(raised(got.kept[1, at], came[1, at]).astype(LOW))

        def lower(got, came, at, lift):
            return raised(got.kept[0, at], came[0, at]) + lift.astype(F32)

        lift1 = upper(f01, came01, 1)
        late_pieces = [b2, yb2, cb2, cyb2, b3, yb3, cb3, cyb3]
        up23 = forward_up(
            where, late_pieces, 2, normed_two, normed_far, sums[0], residual
        )
        out_send, active, slope = tie((up23.out_send, up23.active, up23.slope))

        f23 = forward_down(
            where, late_pieces, normed_two, normed_far, grad_low, sums[1], active, slope
        )
        dn_send, sent, out_came, lift1 = tie((f23.dn_send, f23.sent, swap(out_send), lift1))

        ring_sum = onward(lower(f01, came01, 1, lift1))
        lift0 = upper(f01, came01, 0)
        h0 = output_pair(up23.out_keep, out_came)
        dn_came, came23, lift0, ring_sum, h0 = tie(
            (swap(dn_send), to_core(sent), lift0, ring_sum, h0)
        )

        h1 = to_tp(h0)
        lift2 = upper(f23, came23, 0)
        begin = (residual, f23.dn_keep, dn_came, grad_low[:rows], gain_two[None])
        g_early = backward(
            where,
            [a0, ya0, ca0, cya0, a1, ya1, ca1, cya1],
            2,
            early,
            keep,
            normed,
            begin,
            None,
            None,
            True,
        )
        carried, sent_early, h1, lift2 = tie(
            (
                (g_early.dyb_out, g_early.dy_sum, g_early.dn_sum),
                g_early.sent,
                h1,
                lift2,
            )
        )

        h2 = to_tp(h1)
        lift3 = upper(f23, came23, 1)
        came_early = to_core(sent_early)
        g_late = backward(
            where,
            [a2, ya2, ca2, cya2, a3, ya3, ca3, cya3],
            2,
            late,
            keep,
            normed,
            None,
            carried,
            (own, far, gain_one[None]),
            True,
        )
        gi_far, sent_late, came_early, h2, lift3 = tie(
            (g_late.gi_far, g_late.sent, came_early, h2, lift3)
        )

        quarter = wide // owners // 4

        def rows_of(values, axis, block):
            return lax.dynamic_slice_in_dim(values, block * quarter, quarter, axis)

        def both(kept, came, block):
            return raised(rows_of(kept, 2, block), rows_of(came, 2, block))

        def first_sends(got, came):
            across = swap(both(got.kept, came, 1 - ctx_at).astype(LOW))
            second = raised(got.kept[1, :, 2 * quarter :], came[1, :, 2 * quarter :])
            return across, to_y(second.astype(LOW))

        def second_sends(got, came, across, up):
            near = both(got.kept, came, ctx_at) + across.astype(F32)
            second = raised(got.kept[0, :, 2 * quarter :], came[0, :, 2 * quarter :])
            second = second + up.astype(F32)
            return (
                near[0],
                to_y(near[1].astype(LOW)),
                rows_of(second, 1, ctx_at),
                swap(rows_of(second, 1, 1 - ctx_at).astype(LOW)),
            )

        def third(near, lifted, second, across):
            return jnp.concatenate(
                [near + lifted.astype(F32), second + across.astype(F32)], axis=1
            )

        up_bias = jnp.concatenate([f01.db, f23.db])
        qkv_bias = jnp.concatenate([g_early.db, g_late.db])
        up_bias = lax.dynamic_update_slice(
            jnp.zeros((parts, 2, hidden_half), F32), up_bias, (0, ctx_at, 0)
        )
        small = jnp.concatenate(
            [
                g_early.sums[:4],
                g_late.end_sums[:2],
                up_bias[behind].reshape(-1, wide),
                qkv_bias[behind].reshape(-1, wide),
            ]
        )
        ring_sum = onward(ring_sum.astype(F32) + lower(f23, came23, 0, lift2))
        side0, up0 = first_sends(g_early, came_early)
        gi_far, came_late, small, small_came, ring_sum, up0 = tie(
            (
                swap(gi_far),
                to_core(sent_late),
                small,
                to_core(small),
                ring_sum,
                up0,
            )
        )

        ring_sum = onward(ring_sum.astype(F32) + lower(f23, came23, 1, lift3))
        g0 = jnp.stack(in_order(g_late.gi_own, gi_far))
        side1, up1 = first_sends(g_late, came_late)
        small = small + small_came
        g1, h3, side0, side1, up1, small, small_came = tie(
            (to_tp(g0), to_tp(h2), side0, side1, up1, small, to_y(small))
        )

        sends0 = second_sends(g_early, came_early, side0, up0)
        sends1 = second_sends(g_late, came_late, side1, up1)
        small = small + small_came
        ring_sum, sends0, sends1, small, small_came = tie(
            (ring_sum, sends0, sends1, small, swap(small))
        )

        halves0, halves1 = third(*sends0), third(*sends1)
        total = onward(halves0[1])
        forward_own = (ring_sum.astype(F32) + lower(f01, came01, 0, lift0)).astype(LOW)
        small = small + small_came
        total, forward_far, halves0, halves1, g2, small, small_came = tie(
            (
                total,
                swap(forward_own),
                halves0,
                halves1,
                to_tp(g1),
                small,
                lax.ppermute(small, "tp", [(0, 1), (1, 0), (2, 3), (3, 2)]),
            )
        )

        total = onward(total.astype(F32) + halves1[0])
        up_total, down_total = forward_total(where, forward_own, forward_far)
        result = spread(where, [h0, h1, h2, h3], parts)
        small = small + small_came
        small_came = lax.ppermute(small, "tp", [(0, 2), (2, 0), (1, 3), (3, 1)])
        total, g2, up_total, small, small_came, result = tie(
            (total, g2, up_total, small, small_came, result)
        )

        small = small + small_came

        total = tie(onward(total.astype(F32) + halves1[1]))
        g3 = to_tp(g2)

        mine_half = (total.astype(F32) + halves0[0]).astype(LOW)
        far_half = swap(mine_half)
        lows, highs = in_order(mine_half, far_half)
        attention_sum = jnp.concatenate(
            [lows[:quarter], highs[:quarter], lows[quarter:], highs[quarter:]]
        ).astype(F32)
        qkv_total, out_total = attention_total(where, attention_sum)
        g3, qkv_total = tie((g3, qkv_total))
        grad_inputs = spread(where, [g0, g1, g2, g3], parts)
    else:
        attention_w, forward_w = gather(a0), gather(b0)
        far = swap(pick(inputs, other))
        grad_low = hidden_gradient(swap(cot_pair))
        start = (own, far, b_out[None]) + norm_one
        got = attention(where, attention_w, parts, keep, start, None, norm_two)
        end = forward(
            where,
            forward_w,
            parts,
            got.n2,
            swap(got.n2),
            grad_low,
            None,
            got.y_out,
            False,
        )
        h0 = output_pair(end.out_keep, swap(end.out_send))
        result = lax.all_gather(h0, "tp", axis=0, tiled=True).astype(F32)
        begin = (got.y_out, end.dn_keep, swap(end.dn_send), grad_low[:rows], gain_two[None])
        back = backward(
            where,
            attention_w,
            parts,
            got,
            keep,
            got.n1_out,
            begin,
            None,
            (own, far, gain_one[None]),
            False,
        )
        g0 = jnp.stack(in_order(back.gi_own, swap(back.gi_far)))
        grad_inputs = lax.all_gather(g0, "tp", axis=0, tiled=True).astype(F32)
        forward_own = scatter(end.gradient)
        attention_own = scatter(back.gradient)
        attention_sum = attention_own.astype(F32) + swap(attention_own).astype(F32)
        up_total, down_total = forward_total(where, forward_own, swap(forward_own))
        up_bias = lax.dynamic_update_slice(
            jnp.zeros((parts, 2, hidden_half), F32), end.db, (0, ctx_at, 0)
        )
        small = jnp.concatenate(
            [
                back.sums[:4],
                back.end_sums[:2],
                up_bias.reshape(-1, wide),
                back.db.reshape(-1, wide),
            ]
        )
        small = lax.psum(small, ("fsdp", "ctx", "tp"))
        qkv_total, out_total = attention_total(where, attention_sum)
    up_rows = parts * 2 * hidden_half // wide
    up_small = small[6 : 6 + up_rows].reshape(parts, 2 * hidden_half)
    qkv_small = small[6 + up_rows :].reshape(parts, 3, heads_width)
    return (
        result,
        grad_inputs,
        qkv_total.transpose(1, 0, 2),
        pick(qkv_small, tp_at)[0::2],
        out_total,
        small[0],
        up_total,
        pick(up_small, tp_at),
        down_total,
        small[1],
        small[4],
        small[5],
        small[2],
        small[3],
    )


def solution(mesh):
    placed = (
        P("fsdp", "ctx", None),
        P("fsdp", "ctx", None),
        P("fsdp", None),
        P("fsdp", None, "tp"),
        P(None, "tp"),
        P("tp", "fsdp"),
        P(),
        P("fsdp", "tp"),
        P("tp"),
        P("tp", "fsdp"),
        P(),
        P(),
        P(),
        P(),
        P(),
    )
    return jax.shard_map(
        on_device,
        mesh=mesh,
        in_specs=placed,
        out_specs=(
            P("fsdp", "ctx", None),
            P("fsdp", "ctx", None),
            P("fsdp", None, "tp"),
            P(None, "tp"),
            P("tp", "fsdp"),
            P(),
            P("fsdp", "tp"),
            P("tp"),
            P("tp", "fsdp"),
            P(),
            P(),
            P(),
            P(),
            P(),
        ),
        check_vma=False,
    )
```

```python
import types

import jax
import jax.numpy as jnp
from jax import lax
from jax.experimental import pallas as pl
from jax.experimental.pallas import tpu as pltpu
from jax.sharding import PartitionSpec as P

HEAD = 64
EPSILON = 1e-06
EXTRA = 16
F32 = jnp.float32
LOW = jnp.bfloat16

NN = (((1,), (0,)), ((), ()))
NT = (((1,), (1,)), ((), ()))
TN = (((0,), (0,)), ((), ()))


def mm(left, right, dims=NN):
    return lax.dot_general(left, right, dims, preferred_element_type=F32)


def whole(*shape):
    return pl.BlockSpec(shape, lambda t, _: (0,) * len(shape))


def part(*shape):
    return pl.BlockSpec((1,) + shape, lambda t, _: (t,) + (0,) * len(shape))


def call(
    body, grid, where, ins, outs, scratch=(), pieces=(), flops=0, moved=0, exps=0, vmem=24, placed=(), home=pltpu.HBM,
    aliases=()
):
    names = [entry[0] for entry in ins]
    later = [entry[0] for entry in outs] + [entry[0] for entry in scratch]

    def kernel(where_ref, *refs):
        r = types.SimpleNamespace(where=where_ref)
        count = len(names) + len(pieces)
        r.pieces = refs[len(names) : count]
        for name, ref in zip(names + later, refs[: len(names)] + refs[count:]):
            setattr(r, name, ref)
        body(r)

    results = pl.pallas_call(
        kernel,
        grid_spec=pltpu.PrefetchScalarGridSpec(
            num_scalar_prefetch=1,
            grid=(grid,),
            in_specs=[entry[1] for entry in ins]
            + [pl.BlockSpec(memory_space=home)] * len(pieces),
            out_specs=[entry[1] for entry in outs],
            scratch_shapes=[entry[1] for entry in scratch],
        ),
        input_output_aliases=dict(aliases),
        out_shape=[
            (pltpu.HBM if entry[0] in placed else jax.ShapeDtypeStruct)(entry[2], entry[3])
            for entry in outs
        ],
        compiler_params=pltpu.CompilerParams(
            dimension_semantics=("arbitrary",), vmem_limit_bytes=vmem << 20
        ),
        cost_estimate=pl.CostEstimate(flops=flops, bytes_accessed=moved, transcendentals=exps),
    )(
        where,
        *(
            pltpu.with_memory_space_constraint(entry[2], pltpu.HBM)
            if entry[0] in placed
            else entry[2]
            for entry in ins
        ),
        *(pltpu.with_memory_space_constraint(piece, home) for piece in pieces),
    )
    return types.SimpleNamespace(**{entry[0]: value for entry, value in zip(outs, results)})


def at_step(step):
    return pl.when(pl.program_id(0) == step)


def at_end():
    return pl.when(pl.program_id(0) == pl.num_programs(0) - 1)


def layer_norm(values, gain, shift):
    center = values - jnp.mean(values, axis=-1, keepdims=True)
    spread = jnp.mean(center * center, axis=-1, keepdims=True)
    return center * lax.rsqrt(spread + EPSILON) * gain + shift


def layer_norm_back(values, gain, grad):
    center = values - jnp.mean(values, axis=-1, keepdims=True)
    scale = lax.rsqrt(jnp.mean(center * center, axis=-1, keepdims=True) + EPSILON)
    unit = center * scale
    scaled = grad * gain
    back = scale * (
        scaled
        - jnp.mean(scaled, axis=-1, keepdims=True)
        - unit * jnp.mean(scaled * unit, axis=-1, keepdims=True)
    )
    return back, row_sum(grad * unit), row_sum(grad)


def row_sum(values):
    return jnp.sum(values, axis=0, keepdims=True)


def fetch_scratch(pieces, width, parts, wide):
    copies = pieces[0].shape[1] if len(pieces) == 1 else 4
    return [
        ("weights", pltpu.VMEM((parts, wide, width), LOW)),
        ("extras", pltpu.VMEM((parts, EXTRA, width), LOW)),
        ("sems", pltpu.SemaphoreType.DMA((parts, copies + 1))),
    ]


def fetch(r):
    parts = r.weights.shape[0]

    def copies(at):
        if len(r.pieces) == 1:
            sources = [r.pieces[0].at[at, owner] for owner in range(r.pieces[0].shape[1])]
            owners = list(range(len(sources)))
        else:
            core, row = r.where[1], r.where[2]
            sources = [r.pieces[4 * at + which] for which in range(4)]
            owners = [
                2 * (row + up - 2 * row * up) + (core + over - 2 * core * over)
                for over in range(2)
                for up in range(2)
            ]
        rows = sources[0].shape[0] - EXTRA
        extra = sources[0].at[pl.ds(rows, EXTRA), :]
        result = [pltpu.make_async_copy(extra, r.extras.at[at], r.sems.at[at, len(sources)])]
        for which, (source, owner) in enumerate(zip(sources, owners)):
            target = r.weights.at[at, pl.ds(pl.multiple_of(owner * rows, rows), rows), :]
            result.append(
                pltpu.make_async_copy(source.at[pl.ds(0, rows), :], target, r.sems.at[at, which])
            )
        return result

    @at_step(0)
    def _():
        for at in range(parts):
            for copy in copies(at):
                copy.start()

    def wait(at):
        @at_step(at)
        def _():
            for copy in copies(at):
                copy.wait()

    for at in range(parts):
        wait(at)
    return r.weights.at[pl.program_id(0)], r.extras.at[pl.program_id(0)]


def joined(terms):
    wide = terms.astype(F32)
    return wide[0:1] + (wide[1:2] + wide[2:3])


def gradient_outs(parts, wide, total, stepwise):
    if not stepwise:
        return [("gradient", part(wide, total), (parts, wide, total), LOW)]
    shape = (2, parts, wide // 4, total)
    block = pl.BlockSpec((2, 1, wide // 4, total), lambda t, _: (0, t, 0, 0))
    return [("kept", block, shape, LOW), ("sent", block, shape, LOW)]


def store_gradient(r, pairs):
    column = 0
    for turned, right in pairs:
        span = slice(column, column + right.shape[1])
        column += right.shape[1]
        if hasattr(r, "gradient"):
            r.gradient[0, :, span] = mm(turned[...], right).astype(LOW)
            continue
        core, row = r.where[1], r.where[2]
        rows = r.kept.shape[2]
        for which, out in enumerate((r.kept, r.sent)):
            for far in range(2):
                owner = 2 * (row + far - 2 * row * far) + (core + which - 2 * core * which)
                start = pl.multiple_of(owner * rows, rows)
                out[far, 0, :, span] = mm(turned[pl.ds(start, rows), :], right).astype(LOW)


def add_biases(shard, rows, lines):
    shard[rows:] = jnp.zeros((EXTRA, shard.shape[1]), LOW)
    for row, left in enumerate(lines):
        for piece in range(3):
            low = left.astype(LOW)
            left = left - low.astype(F32)
            at = rows + 3 * row + piece
            shard[at : at + 1, : low.shape[1]] = low


def attention_shard(where, w_qkv, w_out, b_qv):
    _, rows, width = w_qkv.shape

    def body(r):
        for piece in range(3):
            r.shard[:rows, piece * width : (piece + 1) * width] = r.qkv[piece].astype(LOW)
        r.shard[:rows, 3 * width :] = r.out[...].T.astype(LOW)
        add_biases(r.shard, rows, [r.bias[0:1], r.bias[1:2]])

    shape = (rows + EXTRA, 4 * width)
    return call(
        body,
        1,
        where,
        [
            ("qkv", whole(3, rows, width), w_qkv),
            ("out", whole(width, rows), w_out),
            ("bias", whole(2, width), b_qv),
        ],
        [("shard", whole(*shape), shape, LOW)],
        placed=("qkv", "out", "bias", "shard"),
        moved=24 * rows * width,
    ).shard


def forward_shard(where, w_up, w_down, b_up):
    rows = w_up.shape[0]
    hidden = w_up.shape[1] // 2

    def body(r):
        r.shard[:rows, :hidden] = r.up[...].astype(LOW)
        r.shard[:rows, hidden:] = r.down[...].T.astype(LOW)
        add_biases(r.shard, rows, [r.bias[...]])

    shape = (rows + EXTRA, 2 * hidden)
    return call(
        body,
        1,
        where,
        [
            ("up", pl.BlockSpec((rows, hidden), lambda t, at: (0, at[0])), w_up),
            ("down", pl.BlockSpec((hidden, rows), lambda t, at: (at[0], 0)), w_down),
            ("bias", pl.BlockSpec((1, hidden), lambda t, at: (0, at[0])), b_up[None]),
        ],
        [("shard", whole(*shape), shape, LOW)],
        placed=("up", "down", "bias", "shard"),
        moved=12 * rows * hidden,
    ).shard


def attention(where, pieces, parts, keep, first, carried, last):
    rows = keep.shape[0]
    half = rows // 2
    width = pieces[0].shape[-1] // 4
    heads = width // HEAD
    wide = first[0].shape[1] if first else carried[0].shape[1]

    def body(r):
        w, extra = fetch(r)
        normed = r.n1_out if first else r.n1

        @at_step(0)
        def _():
            if not first:
                r.y_out[...] = r.y[...]
                return
            for at, ref in ((0, r.own), (half, r.far)):
                tokens = ref[...].astype(F32)
                normed[at : at + half] = layer_norm(tokens, r.g1[...], r.s1[...]).astype(LOW)
                r.y_out[at : at + half] = tokens + r.b_out[...]

        terms = extra[...]
        bias_q, bias_v = joined(terms[0:3, :width]), joined(terms[3:6, :width])
        bias = jnp.concatenate([bias_q, jnp.zeros_like(bias_q), bias_v], axis=1)
        low = (mm(normed[...], w[:, : 3 * width]) + bias).astype(LOW)
        r.p[0] = low
        seen = r.keep[...] > 0
        for head in range(heads):
            at = head * HEAD
            query = low[:, at : at + HEAD]
            key = low[:, width + at : width + at + HEAD]
            value = low[:, 2 * width + at : 2 * width + at + HEAD]
            scores = jnp.where(seen, mm(key, query, NT) * HEAD**-0.5, -1e30)
            top = jnp.max(scores, axis=0, keepdims=True)
            exponent = jnp.exp(scores - top)
            total = jnp.sum(exponent, axis=0, keepdims=True)
            probability = (exponent * (1.0 / total)).astype(LOW)
            r.o[0, :, at : at + HEAD] = mm(probability, value, TN).astype(LOW)
            r.l[0, head : head + 1, :] = top + jnp.log(total)
        r.y_out[...] += mm(r.o[0], w[:, 3 * width :], NT)

        if last:

            @at_end()
            def _():
                r.n2[...] = layer_norm(r.y_out[...], r.g2[...], r.s2[...]).astype(LOW)

    line = whole(1, wide)
    ins = [("keep", whole(rows, 1), keep)]
    outs = [
        ("p", part(rows, 3 * width), (parts, rows, 3 * width), LOW),
        ("o", part(rows, width), (parts, rows, width), LOW),
        ("l", part(heads, rows), (parts, heads, rows), F32),
        ("y_out", whole(rows, wide), (rows, wide), F32),
    ]
    if first:
        specs = [whole(half, wide)] * 2 + [line] * 3
        ins += list(zip(("own", "far", "b_out", "g1", "s1"), specs, first))
        outs.append(("n1_out", whole(rows, wide), (rows, wide), LOW))
    else:
        ins += list(zip(("n1", "y"), [whole(rows, wide)] * 2, carried))
    if last:
        ins += list(zip(("g2", "s2"), [line] * 2, last))
        outs.append(("n2", whole(rows, wide), (rows, wide), LOW))
    return call(
        body,
        parts,
        where,
        ins,
        outs,
        fetch_scratch(pieces, 4 * width, parts, wide),
        pieces,
        flops=8 * parts * rows * wide * width + 4 * parts * rows * rows * width,
        moved=8 * parts * wide * width + 12 * rows * wide,
        exps=parts * heads * rows * rows,
        vmem=24 if parts <= 2 else 56,
    )


def forward_up(where, pieces, parts, own, far, branch, residual):
    rows, wide = own.shape
    half = rows // 2
    width = pieces[0].shape[-1] // 2

    def body(r):
        w, extra = fetch(r)

        @at_step(0)
        def _():
            r.both[:rows] = r.own[...]
            r.both[rows:] = r.far[...]
            r.branch_sum[...] = r.branch_in[...]

        hidden = mm(r.both[...], w[:, :width]) + joined(extra[0:3, :width])
        bell = 0.5 * (1.0 + lax.erf(hidden * 0.5**0.5))
        active = (hidden * bell).astype(LOW)
        slope = bell + hidden * jnp.exp(hidden * hidden * -0.5) * 0.3989422804014327
        r.branch_sum[...] += mm(active, w[:, width:], NT)
        r.active[0] = active
        r.slope[0] = slope.astype(LOW)

        @at_end()
        def _():
            r.out_keep[:half] = r.y[:half] + r.branch_sum[:half]
            r.out_keep[half:] = r.branch_sum[rows + half :]
            r.out_send[:half] = (r.y[half:] + r.branch_sum[half:rows]).astype(LOW)
            r.out_send[half:] = r.branch_sum[rows : rows + half].astype(LOW)

    mine = whole(rows, wide)
    shape = (parts, 2 * rows, width)
    return call(
        body,
        parts,
        where,
        [
            ("own", mine, own),
            ("far", mine, far),
            ("branch_in", whole(2 * rows, wide), branch),
            ("y", mine, residual),
        ],
        [
            ("active", part(2 * rows, width), shape, LOW),
            ("slope", part(2 * rows, width), shape, LOW),
            ("out_keep", mine, (rows, wide), F32),
            ("out_send", mine, (rows, wide), LOW),
        ],
        [
            ("both", pltpu.VMEM((2 * rows, wide), LOW)),
            ("branch_sum", pltpu.VMEM((2 * rows, wide), F32)),
        ]
        + fetch_scratch(pieces, 2 * width, parts, wide),
        pieces,
        flops=8 * parts * rows * width * wide,
        moved=4 * parts * wide * width + 12 * rows * wide,
        exps=4 * parts * rows * width,
    )


def forward_down(where, pieces, own, far, grad, carried, active, slope):
    rows, wide = own.shape
    parts, _, width = active.shape

    def body(r):
        w, _ = fetch(r)

        @at_step(0)
        def _():
            r.turned[:, :rows] = r.own[...].T
            r.turned[:, rows:] = r.far[...].T
            r.turned_grad[...] = r.grad[...].T
            r.grad_sum[...] = r.grad_in[...]

        grad_active = mm(r.grad[...], w[:, width:])
        grad_hidden = (grad_active * r.slope[0].astype(F32)).astype(LOW)
        r.db[0] = row_sum(grad_hidden.astype(F32))
        r.grad_sum[...] += mm(grad_hidden, w[:, :width], NT)
        store_gradient(r, [(r.turned, grad_hidden), (r.turned_grad, r.active[0])])

        @at_end()
        def _():
            r.dn_keep[...] = r.grad_sum[:rows]
            r.dn_send[...] = r.grad_sum[rows:].astype(LOW)

    mine, double = whole(rows, wide), whole(2 * rows, wide)
    return call(
        body,
        parts,
        where,
        [
            ("own", mine, own),
            ("far", mine, far),
            ("grad", double, grad),
            ("grad_in", double, carried),
            ("active", part(2 * rows, width), active),
            ("slope", part(2 * rows, width), slope),
        ],
        [
            ("db", part(1, width), (parts, 1, width), F32),
            ("dn_keep", mine, (rows, wide), F32),
            ("dn_send", mine, (rows, wide), LOW),
        ]
        + gradient_outs(parts, wide, 2 * width, True),
        [
            ("turned", pltpu.VMEM((wide, 2 * rows), LOW)),
            ("turned_grad", pltpu.VMEM((wide, 2 * rows), LOW)),
            ("grad_sum", pltpu.VMEM((2 * rows, wide), F32)),
        ]
        + fetch_scratch(pieces, 2 * width, parts, wide),
        pieces,
        flops=16 * parts * rows * width * wide,
        moved=8 * parts * wide * width + 12 * rows * wide,
    )


def forward(where, pieces, parts, own, far, grad, carried, residual, stepwise):
    rows, wide = own.shape
    half = rows // 2
    width = pieces[0].shape[-1] // 2

    def body(r):
        w, extra = fetch(r)

        @at_step(0)
        def _():
            r.both[:rows] = r.own[...]
            r.both[rows:] = r.far[...]
            r.turned[...] = r.both[...].T
            r.turned_grad[...] = r.grad[...].T
            r.branch_sum[...] = r.branch_in[...] if carried else jnp.zeros((2 * rows, wide), F32)
            r.grad_sum[...] = r.grad_in[...] if carried else jnp.zeros((2 * rows, wide), F32)

        hidden = mm(r.both[...], w[:, :width]) + joined(extra[0:3, :width])
        bell = 0.5 * (1.0 + lax.erf(hidden * 0.5**0.5))
        active = (hidden * bell).astype(LOW)
        slope = bell + hidden * jnp.exp(hidden * hidden * -0.5) * 0.3989422804014327
        r.branch_sum[...] += mm(active, w[:, width:], NT)
        grad_hidden = (mm(r.grad[...], w[:, width:]) * slope).astype(LOW)
        r.db[0] = row_sum(grad_hidden.astype(F32))
        r.grad_sum[...] += mm(grad_hidden, w[:, :width], NT)
        store_gradient(r, [(r.turned, grad_hidden), (r.turned_grad, active)])

        if residual is None:
            return

        @at_end()
        def _():
            r.out_keep[:half] = r.y[:half] + r.branch_sum[:half]
            r.out_keep[half:] = r.branch_sum[rows + half :]
            r.out_send[:half] = (r.y[half:] + r.branch_sum[half:rows]).astype(LOW)
            r.out_send[half:] = r.branch_sum[rows : rows + half].astype(LOW)
            r.dn_keep[...] = r.grad_sum[:rows]
            r.dn_send[...] = r.grad_sum[rows:].astype(LOW)

    mine, double = whole(rows, wide), whole(2 * rows, wide)
    sums = [("branch_sum", (2 * rows, wide), F32), ("grad_sum", (2 * rows, wide), F32)]
    ins = [("own", mine, own), ("far", mine, far), ("grad", double, grad)]
    outs = [("db", part(1, width), (parts, 1, width), F32)]
    scratch = [
        ("both", pltpu.VMEM((2 * rows, wide), LOW)),
        ("turned", pltpu.VMEM((wide, 2 * rows), LOW)),
        ("turned_grad", pltpu.VMEM((wide, 2 * rows), LOW)),
    ]
    if carried:
        ins += [("branch_in", double, carried[0]), ("grad_in", double, carried[1])]
    if residual is None:
        outs += [(name, double, shape, kind) for name, shape, kind in sums]
    else:
        ins.append(("y", mine, residual))
        outs += [
            ("out_keep", mine, (rows, wide), F32),
            ("out_send", mine, (rows, wide), LOW),
            ("dn_keep", mine, (rows, wide), F32),
            ("dn_send", mine, (rows, wide), LOW),
        ]
        scratch += [(name, pltpu.VMEM(shape, kind)) for name, shape, kind in sums]
    outs += gradient_outs(parts, wide, 2 * width, stepwise)
    return call(
        body,
        parts,
        where,
        ins,
        outs,
        scratch + fetch_scratch(pieces, 2 * width, parts, wide),
        pieces,
        flops=24 * parts * rows * width * wide,
        moved=8 * parts * wide * width + 12 * rows * wide,
        exps=4 * parts * rows * width,
        vmem=24 if parts <= 2 else 56,
    )


def backward(where, pieces, parts, saved, keep, normed, first, carried, last, stepwise):
    rows, wide = normed.shape
    half = rows // 2
    width = saved.o.shape[2]
    heads = width // HEAD

    def body(r):
        w, _ = fetch(r)
        low_grad = r.dyb_out if first else r.dyb

        @at_step(0)
        def _():
            if first:
                grad_normed = r.dn_keep[...] + r.dn_came[...].astype(F32)
                back, gain_sum, shift_sum = layer_norm_back(r.y[...], r.g2[...], grad_normed)
                grad_out = r.grad[...].astype(F32)
                r.dy_sum[...] = grad_out + back
                low_grad[...] = r.dy_sum[...].astype(LOW)
                r.sums[0:1] = row_sum(low_grad[...].astype(F32))
                r.sums[1:2] = row_sum(grad_out)
                r.sums[2:3] = gain_sum
                r.sums[3:4] = shift_sum
                r.sums[4:8] = jnp.zeros((4, wide), F32)
                r.dn_sum[...] = jnp.zeros_like(r.dn_sum)
            else:
                r.dn_sum[...] = r.dn[...]
            r.turned[...] = r.n1[...].T
            r.turned_grad[...] = low_grad[...].T

        grad_mixed = mm(low_grad[...], w[:, 3 * width :]).astype(LOW)
        seen = r.keep[...] > 0
        for head in range(heads):
            at = head * HEAD
            query = r.p[0, :, at : at + HEAD]
            key = r.p[0, :, width + at : width + at + HEAD]
            value = r.p[0, :, 2 * width + at : 2 * width + at + HEAD]
            grad = grad_mixed[:, at : at + HEAD]
            scores = jnp.where(seen, mm(key, query, NT) * HEAD**-0.5, -1e30)
            probability = jnp.exp(scores - r.l[0, head : head + 1, :])
            grad_probability = mm(value, grad, NT)
            grad_value = mm(probability.astype(LOW), grad)
            inner = jnp.sum(grad_probability * probability, axis=0, keepdims=True)
            grad_scores = (probability * (grad_probability - inner)).astype(LOW)
            grad_query = mm(grad_scores, key, TN) * HEAD**-0.5
            grad_key = mm(grad_scores, query) * HEAD**-0.5
            r.dp[:, at : at + HEAD] = grad_query.astype(LOW)
            r.dp[:, width + at : width + at + HEAD] = grad_key.astype(LOW)
            r.dp[:, 2 * width + at : 2 * width + at + HEAD] = grad_value.astype(LOW)
        r.db[0] = row_sum(r.dp[...].astype(F32))
        r.dn_sum[...] += mm(r.dp[...], w[:, : 3 * width], NT)
        store_gradient(r, [(r.turned, r.dp[...]), (r.turned_grad, r.o[0])])

        if not last:
            return

        @at_end()
        def _():
            dy = r.dy_sum if first else r.dy
            gain_sum = shift_sum = 0.0
            for at, ref, out in ((0, r.own, r.gi_own), (half, r.far, r.gi_far)):
                back, gain_add, shift_add = layer_norm_back(
                    ref[...].astype(F32), r.g1[...], r.dn_sum[at : at + half]
                )
                out[...] = (dy[at : at + half] + back).astype(LOW)
                gain_sum, shift_sum = gain_sum + gain_add, shift_sum + shift_add
            r.end_sums[0:1] = gain_sum
            r.end_sums[1:2] = shift_sum
            r.end_sums[2:8] = jnp.zeros((6, wide), F32)

    mine, line, eight = whole(rows, wide), whole(1, wide), whole(8, wide)
    ins = [
        ("p", part(rows, 3 * width), saved.p),
        ("o", part(rows, width), saved.o),
        ("l", part(heads, rows), saved.l),
        ("keep", whole(rows, 1), keep),
        ("n1", mine, normed),
    ]
    outs = [("db", part(1, 3 * width), (parts, 1, 3 * width), F32)]
    scratch = [
        ("dp", pltpu.VMEM((rows, 3 * width), LOW)),
        ("turned", pltpu.VMEM((wide, rows), LOW)),
        ("turned_grad", pltpu.VMEM((wide, rows), LOW)),
    ]
    sums = [("dn_sum", (rows, wide), F32)]
    if first:
        ins += list(zip(("y", "dn_keep", "dn_came", "grad", "g2"), [mine] * 4 + [line], first))
        outs += [("dyb_out", mine, (rows, wide), LOW), ("sums", eight, (8, wide), F32)]
        sums.append(("dy_sum", (rows, wide), F32))
    else:
        ins += list(zip(("dyb", "dy", "dn"), [mine] * 3, carried))
    if last:
        ins += list(zip(("own", "far", "g1"), [whole(half, wide)] * 2 + [line], last))
        outs += [
            ("gi_own", whole(half, wide), (half, wide), LOW),
            ("gi_far", whole(half, wide), (half, wide), LOW),
            ("end_sums", eight, (8, wide), F32),
        ]
        scratch += [(name, pltpu.VMEM(shape, kind)) for name, shape, kind in sums]
    else:
        outs += [(name, mine, shape, kind) for name, shape, kind in sums]
    outs += gradient_outs(parts, wide, 4 * width, stepwise)
    return call(
        body,
        parts,
        where,
        ins,
        outs,
        scratch + fetch_scratch(pieces, 4 * width, parts, wide),
        pieces,
        placed=("dyb_out", "dy_sum", "dn_sum", "kept", "sent", "gi_own", "gi_far")
        + ("dyb", "dy", "dn"),
        home=pltpu.HBM,
        flops=16 * parts * rows * wide * width + 10 * parts * rows * rows * width,
        moved=16 * parts * wide * width + 16 * rows * wide,
        exps=parts * heads * rows * rows,
        vmem=24 if parts <= 2 else 56,
    )


def spread(where, pieces, parts, first=0, before=None):
    def body(r):
        for at in range(len(pieces)):

            @at_step(at)
            def _(ref=getattr(r, f"piece{at}")):
                r.out[...] = ref[...].astype(F32)

    pair = pieces[0].shape
    block = pl.BlockSpec(
        pair, lambda t, at: (lax.rem(at[3] - first - t + 2 * parts, parts), 0, 0)
    )
    ins = [(f"piece{at}", whole(*pair), piece) for at, piece in enumerate(pieces)]
    if before is not None:
        ins.append(("before", pl.BlockSpec(memory_space=pl.ANY), before))
    return call(
        body,
        len(pieces),
        where,
        ins,
        [("out", block, (parts * pair[0],) + pair[1:], F32)],
        moved=6 * len(pieces) * pieces[0].size,
        aliases=() if before is None else ((len(ins), 0),),
    ).out


def forward_total(where, own, far):
    rows, width = own.shape[0], own.shape[1] // 2

    def body(r):
        for flip, ref in ((0, r.own), (1, r.far)):
            block = r.where[0] + flip - 2 * r.where[0] * flip
            span = pl.ds(pl.multiple_of(block * width, width), width)
            r.up[:, span] = ref[:, :width].astype(F32)
            r.down[span, :] = ref[:, width:].astype(F32).T

    got = call(
        body,
        1,
        where,
        [("own", whole(rows, 2 * width), own), ("far", whole(rows, 2 * width), far)],
        [
            ("up", whole(rows, 2 * width), (rows, 2 * width), F32),
            ("down", whole(2 * width, rows), (2 * width, rows), F32),
        ],
        moved=24 * rows * width,
    )
    return got.up, got.down


def attention_total(where, grad):
    rows, width = grad.shape[0], grad.shape[1] // 4

    def body(r):
        for piece in range(3):
            r.qkv[piece] = r.grad[:, piece * width : (piece + 1) * width]
        r.out[...] = r.grad[:, 3 * width :].T

    got = call(
        body,
        1,
        where,
        [("grad", whole(rows, 4 * width), grad)],
        [
            ("qkv", whole(3, rows, width), (3, rows, width), F32),
            ("out", whole(width, rows), (width, rows), F32),
        ],
        moved=32 * rows * width,
    )
    return got.qkv, got.out


def on_device(
    inputs,
    cotangent,
    visible,
    w_qkv,
    b_qv,
    w_out,
    b_out,
    w_up,
    b_up,
    w_down,
    b_down,
    gain_one,
    shift_one,
    gain_two,
    shift_two,
):
    images, half, wide = inputs.shape
    ctx_at, tp_at, fsdp_at = (lax.axis_index(name) for name in ("ctx", "tp", "fsdp"))
    blocks, parts, owners = (lax.axis_size(name) for name in ("ctx", "tp", "fsdp"))
    assert blocks == 2 and images == blocks * parts
    first = blocks * tp_at
    mine, other = first + ctx_at, first + 1 - ctx_at
    where = jnp.stack([ctx_at, fsdp_at % 2, fsdp_at // 2, tp_at]).astype(jnp.int32)
    heads_width = w_qkv.shape[2]
    hidden_half = w_up.shape[1] // 2
    rows = 2 * half

    def swap(values):
        return lax.ppermute(values, "ctx", [(0, 1), (1, 0)])

    def pick(values, index):
        return lax.dynamic_index_in_dim(values, index, 0, keepdims=False)

    def in_order(own, received):
        return jnp.where(ctx_at == 0, own, received), jnp.where(ctx_at == 0, received, own)

    stepwise = owners == 4 and parts == 4
    behind = jnp.mod(tp_at - jnp.arange(parts), parts) if stepwise else jnp.arange(parts)

    def to_core(values):
        return lax.ppermute(values, "fsdp", [(0, 1), (1, 0), (2, 3), (3, 2)])

    def to_y(values):
        return lax.ppermute(values, "fsdp", [(0, 2), (2, 0), (1, 3), (3, 1)])

    def to_tp(values):
        return lax.ppermute(values, "tp", [(i, (i + 1) % parts) for i in range(parts)])

    def gather(shard):
        full = lax.all_gather(shard, ("tp", "fsdp"), axis=0, tiled=True)
        return [full.reshape(parts, owners, *shard.shape)]

    def scatter(gradient):
        flat = gradient.reshape(-1, gradient.shape[2])
        return lax.psum_scatter(flat, ("tp", "fsdp"), scatter_dimension=0, tiled=True)

    def raised(upper, came):
        return upper.astype(F32) + came.astype(F32)

    def onward(total):
        return to_tp(total.astype(LOW))

    tie = lax.optimization_barrier

    a0 = attention_shard(where, w_qkv.transpose(1, 0, 2), w_out, b_qv)
    b0 = forward_shard(where, w_up, w_down, b_up)
    own = pick(inputs, mine)
    cot_pair = jnp.stack([pick(cotangent, mine), pick(cotangent, other)])
    mine_seen = pick(visible, mine).reshape(blocks, half)
    other_seen = pick(visible, other).reshape(blocks, half)
    keep = jnp.concatenate([pick(mine_seen, ctx_at), pick(mine_seen, 1 - ctx_at)])
    keep_other = jnp.concatenate([pick(other_seen, 1 - ctx_at), pick(other_seen, ctx_at)])
    keep, keep_other = keep[:, None], keep_other[:, None]
    keep_all = jnp.concatenate([keep, keep_other]).astype(LOW)
    norm_one, norm_two = (gain_one[None], shift_one[None]), (gain_two[None], shift_two[None])

    def hidden_gradient(swapped):
        rows_of = [cot_pair[0], swapped[1], swapped[0], cot_pair[1]]
        return jnp.concatenate(rows_of) * keep_all

    def output_pair(kept, came):
        seen = jnp.concatenate([keep[:half], keep_other[half:]]).astype(F32)
        came = came.astype(F32)
        rows_of = kept + jnp.concatenate([came[half:], came[:half]]) + b_down
        rows_of = (rows_of * seen).astype(LOW)
        return jnp.stack(in_order(rows_of[:half], rows_of[half:]))

    if stepwise:
        far = pick(inputs, other)
        a0, b0, a1, ya0, far, cot_pair = tie((a0, b0, to_tp(a0), to_y(a0), far, cot_pair))

        a1, a2, ya1, ca0, cya0, far = tie(
            (a1, to_tp(a1), to_y(a1), to_core(a0), to_core(ya0), swap(far))
        )

        a2, a3, ya2, ca1, cya1, cot_swapped = tie(
            (a2, to_tp(a2), to_y(a2), to_core(a1), to_core(ya1), swap(cot_pair))
        )

        start = (own, far, b_out[None]) + norm_one
        early = attention(
            where, [a0, ya0, ca0, cya0, a1, ya1, ca1, cya1], 2, keep, start, None, None
        )
        normed, total_y, a3, b0, ya3, b1, ca2, cya2 = tie(
            (
                early.n1_out,
                early.y_out,
                a3,
                b0,
                to_y(a3),
                to_tp(b0),
                to_core(a2),
                to_core(ya2),
            )
        )

        b2, yb0 = to_tp(b1), to_y(b0)
        ca3, cya3 = to_core(a3), to_core(ya3)
        late = attention(
            where,
            [a2, ya2, ca2, cya2, a3, ya3, ca3, cya3],
            2,
            keep,
            None,
            (normed, total_y),
            norm_two,
        )
        normed_two, residual = late.n2, late.y_out
        b2, yb0 = tie((b2, yb0))
        grad_low = hidden_gradient(cot_swapped)

        normed_far, b3, yb1, cb0, cyb0 = tie(
            (swap(normed_two), to_tp(b2), to_y(b1), to_core(b0), to_core(yb0))
        )

        def block(pieces, carried, last):
            return forward(
                where, pieces, 2, normed_two, normed_far, grad_low, carried, last, True
            )

        yb2, cb1, cyb1 = tie((to_y(b2), to_core(b1), to_core(yb1)))

        f01 = block([b0, yb0, cb0, cyb0, b1, yb1, cb1, cyb1], None, None)
        sums, sent, yb3, cb2, cyb2 = tie(
            (
                (f01.branch_sum, f01.grad_sum),
                f01.sent,
                to_y(b3),
                to_core(b2),
                to_core(yb2),
            )
        )

        came01, cb3, cyb3 = tie((to_core(sent), to_core(b3), to_core(yb3)))

        def upper(got, came, at):
            return to_y(raised(got.kept[1, at], came[1, at]).astype(LOW))

        def lower(got, came, at, lift):
            return raised(got.kept[0, at], came[0, at]) + lift.astype(F32)

        lift1 = upper(f01, came01, 1)
        late_pieces = [b2, yb2, cb2, cyb2, b3, yb3, cb3, cyb3]
        up23 = forward_up(
            where, late_pieces, 2, normed_two, normed_far, sums[0], residual
        )
        out_send, active, slope = tie((up23.out_send, up23.active, up23.slope))

        f23 = forward_down(
            where, late_pieces, normed_two, normed_far, grad_low, sums[1], active, slope
        )
        dn_send, sent, out_came, lift1 = tie((f23.dn_send, f23.sent, swap(out_send), lift1))

        ring_sum = onward(lower(f01, came01, 1, lift1))
        lift0 = upper(f01, came01, 0)
        h0 = output_pair(up23.out_keep, out_came)
        dn_came, came23, lift0, ring_sum, h0 = tie(
            (swap(dn_send), to_core(sent), lift0, ring_sum, h0)
        )

        h1 = to_tp(h0)
        lift2 = upper(f23, came23, 0)
        begin = (residual, f23.dn_keep, dn_came, grad_low[:rows], gain_two[None])
        g_early = backward(
            where,
            [a0, ya0, ca0, cya0, a1, ya1, ca1, cya1],
            2,
            early,
            keep,
            normed,
            begin,
            None,
            None,
            True,
        )
        carried, sent_early, h1, lift2 = tie(
            (
                (g_early.dyb_out, g_early.dy_sum, g_early.dn_sum),
                g_early.sent,
                h1,
                lift2,
            )
        )

        h2 = to_tp(h1)
        lift3 = upper(f23, came23, 1)
        came_early = to_core(sent_early)
        g_late = backward(
            where,
            [a2, ya2, ca2, cya2, a3, ya3, ca3, cya3],
            2,
            late,
            keep,
            normed,
            None,
            carried,
            (own, far, gain_one[None]),
            True,
        )
        gi_far, sent_late, came_early, h2, lift3 = tie(
            (g_late.gi_far, g_late.sent, came_early, h2, lift3)
        )

        quarter = wide // owners // 4

        def rows_of(values, axis, block):
            return lax.dynamic_slice_in_dim(values, block * quarter, quarter, axis)

        def both(kept, came, block):
            return raised(rows_of(kept, 2, block), rows_of(came, 2, block))

        def first_sends(got, came):
            across = swap(both(got.kept, came, 1 - ctx_at).astype(LOW))
            second = raised(got.kept[1, :, 2 * quarter :], came[1, :, 2 * quarter :])
            return across, to_y(second.astype(LOW))

        def second_sends(got, came, across, up):
            near = both(got.kept, came, ctx_at) + across.astype(F32)
            second = raised(got.kept[0, :, 2 * quarter :], came[0, :, 2 * quarter :])
            second = second + up.astype(F32)
            return (
                near[0],
                to_y(near[1].astype(LOW)),
                rows_of(second, 1, ctx_at),
                swap(rows_of(second, 1, 1 - ctx_at).astype(LOW)),
            )

        def third(near, lifted, second, across):
            return jnp.concatenate(
                [near + lifted.astype(F32), second + across.astype(F32)], axis=1
            )

        up_bias = jnp.concatenate([f01.db, f23.db])
        qkv_bias = jnp.concatenate([g_early.db, g_late.db])
        up_bias = lax.dynamic_update_slice(
            jnp.zeros((parts, 2, hidden_half), F32), up_bias, (0, ctx_at, 0)
        )
        small = jnp.concatenate(
            [
                g_early.sums[:4],
                g_late.end_sums[:2],
                up_bias[behind].reshape(-1, wide),
                qkv_bias[behind].reshape(-1, wide),
            ]
        )
        ring_sum = onward(ring_sum.astype(F32) + lower(f23, came23, 0, lift2))
        side0, up0 = first_sends(g_early, came_early)
        gi_far, came_late, small, small_came, ring_sum, up0 = tie(
            (
                swap(gi_far),
                to_core(sent_late),
                small,
                to_core(small),
                ring_sum,
                up0,
            )
        )

        ring_sum = onward(ring_sum.astype(F32) + lower(f23, came23, 1, lift3))
        g0 = jnp.stack(in_order(g_late.gi_own, gi_far))
        side1, up1 = first_sends(g_late, came_late)
        small = small + small_came
        g1, h3, side0, side1, up1, small, small_came = tie(
            (to_tp(g0), to_tp(h2), side0, side1, up1, small, to_y(small))
        )

        sends0 = second_sends(g_early, came_early, side0, up0)
        sends1 = second_sends(g_late, came_late, side1, up1)
        small = small + small_came
        ring_sum, sends0, sends1, small, small_came = tie(
            (ring_sum, sends0, sends1, small, swap(small))
        )

        halves0, halves1 = third(*sends0), third(*sends1)
        total = onward(halves0[1])
        forward_own = (ring_sum.astype(F32) + lower(f01, came01, 0, lift0)).astype(LOW)
        small = small + small_came
        total, forward_far, halves0, halves1, g2, small, small_came = tie(
            (
                total,
                swap(forward_own),
                halves0,
                halves1,
                to_tp(g1),
                small,
                lax.ppermute(small, "tp", [(0, 1), (1, 0), (2, 3), (3, 2)]),
            )
        )

        total = onward(total.astype(F32) + halves1[0])
        up_total, down_total = forward_total(where, forward_own, forward_far)
        result = spread(where, [h0, h1, h2, h3], parts)
        small = small + small_came
        small_came = lax.ppermute(small, "tp", [(0, 2), (2, 0), (1, 3), (3, 1)])
        total, g2, up_total, small, small_came, result = tie(
            (total, g2, up_total, small, small_came, result)
        )

        small = small + small_came

        total = tie(onward(total.astype(F32) + halves1[1]))
        g3 = to_tp(g2)

        mine_half = (total.astype(F32) + halves0[0]).astype(LOW)
        far_half = swap(mine_half)
        lows, highs = in_order(mine_half, far_half)
        attention_sum = jnp.concatenate(
            [lows[:quarter], highs[:quarter], lows[quarter:], highs[quarter:]]
        ).astype(F32)
        qkv_total, out_total = attention_total(where, attention_sum)
        grad_inputs = spread(where, [g0, g1, g2], parts)
        g3, qkv_total, grad_inputs = tie((g3, qkv_total, grad_inputs))
        grad_inputs = spread(where, [g3], parts, 3, grad_inputs)
    else:
        attention_w, forward_w = gather(a0), gather(b0)
        far = swap(pick(inputs, other))
        grad_low = hidden_gradient(swap(cot_pair))
        start = (own, far, b_out[None]) + norm_one
        got = attention(where, attention_w, parts, keep, start, None, norm_two)
        end = forward(
            where,
            forward_w,
            parts,
            got.n2,
            swap(got.n2),
            grad_low,
            None,
            got.y_out,
            False,
        )
        h0 = output_pair(end.out_keep, swap(end.out_send))
        result = lax.all_gather(h0, "tp", axis=0, tiled=True).astype(F32)
        begin = (got.y_out, end.dn_keep, swap(end.dn_send), grad_low[:rows], gain_two[None])
        back = backward(
            where,
            attention_w,
            parts,
            got,
            keep,
            got.n1_out,
            begin,
            None,
            (own, far, gain_one[None]),
            False,
        )
        g0 = jnp.stack(in_order(back.gi_own, swap(back.gi_far)))
        grad_inputs = lax.all_gather(g0, "tp", axis=0, tiled=True).astype(F32)
        forward_own = scatter(end.gradient)
        attention_own = scatter(back.gradient)
        attention_sum = attention_own.astype(F32) + swap(attention_own).astype(F32)
        up_total, down_total = forward_total(where, forward_own, swap(forward_own))
        up_bias = lax.dynamic_update_slice(
            jnp.zeros((parts, 2, hidden_half), F32), end.db, (0, ctx_at, 0)
        )
        small = jnp.concatenate(
            [
                back.sums[:4],
                back.end_sums[:2],
                up_bias.reshape(-1, wide),
                back.db.reshape(-1, wide),
            ]
        )
        small = lax.psum(small, ("fsdp", "ctx", "tp"))
        qkv_total, out_total = attention_total(where, attention_sum)
    up_rows = parts * 2 * hidden_half // wide
    up_small = small[6 : 6 + up_rows].reshape(parts, 2 * hidden_half)
    qkv_small = small[6 + up_rows :].reshape(parts, 3, heads_width)
    return (
        result,
        grad_inputs,
        qkv_total.transpose(1, 0, 2),
        pick(qkv_small, tp_at)[0::2],
        out_total,
        small[0],
        up_total,
        pick(up_small, tp_at),
        down_total,
        small[1],
        small[4],
        small[5],
        small[2],
        small[3],
    )


def solution(mesh):
    placed = (
        P("fsdp", "ctx", None),
        P("fsdp", "ctx", None),
        P("fsdp", None),
        P("fsdp", None, "tp"),
        P(None, "tp"),
        P("tp", "fsdp"),
        P(),
        P("fsdp", "tp"),
        P("tp"),
        P("tp", "fsdp"),
        P(),
        P(),
        P(),
        P(),
        P(),
    )
    return jax.shard_map(
        on_device,
        mesh=mesh,
        in_specs=placed,
        out_specs=(
            P("fsdp", "ctx", None),
            P("fsdp", "ctx", None),
            P("fsdp", None, "tp"),
            P(None, "tp"),
            P("tp", "fsdp"),
            P(),
            P("fsdp", "tp"),
            P("tp"),
            P("tp", "fsdp"),
            P(),
            P(),
            P(),
            P(),
            P(),
        ),
        check_vma=False,
    )
```

```python
import types

import jax
import jax.numpy as jnp
from jax import lax
from jax.experimental import pallas as pl
from jax.experimental.pallas import tpu as pltpu
from jax.sharding import PartitionSpec as P

HEAD = 64
EPSILON = 1e-06
EXTRA = 16
F32 = jnp.float32
LOW = jnp.bfloat16

NN = (((1,), (0,)), ((), ()))
NT = (((1,), (1,)), ((), ()))
TN = (((0,), (0,)), ((), ()))


def mm(left, right, dims=NN):
    return lax.dot_general(left, right, dims, preferred_element_type=F32)


def whole(*shape):
    return pl.BlockSpec(shape, lambda t, _: (0,) * len(shape))


def part(*shape):
    return pl.BlockSpec((1,) + shape, lambda t, _: (t,) + (0,) * len(shape))


def call(
    body, grid, where, ins, outs, scratch=(), pieces=(), flops=0, moved=0, exps=0, vmem=30, placed=(), home=pltpu.HBM,
    aliases=()
):
    names = [entry[0] for entry in ins]
    later = [entry[0] for entry in outs] + [entry[0] for entry in scratch]

    def kernel(where_ref, *refs):
        r = types.SimpleNamespace(where=where_ref)
        count = len(names) + len(pieces)
        r.pieces = refs[len(names) : count]
        for name, ref in zip(names + later, refs[: len(names)] + refs[count:]):
            setattr(r, name, ref)
        body(r)

    results = pl.pallas_call(
        kernel,
        grid_spec=pltpu.PrefetchScalarGridSpec(
            num_scalar_prefetch=1,
            grid=(grid,),
            in_specs=[entry[1] for entry in ins]
            + [pl.BlockSpec(memory_space=home)] * len(pieces),
            out_specs=[entry[1] for entry in outs],
            scratch_shapes=[entry[1] for entry in scratch],
        ),
        input_output_aliases=dict(aliases),
        out_shape=[
            (pltpu.HBM if entry[0] in placed else jax.ShapeDtypeStruct)(entry[2], entry[3])
            for entry in outs
        ],
        compiler_params=pltpu.CompilerParams(
            dimension_semantics=("arbitrary",), vmem_limit_bytes=vmem << 20
        ),
        cost_estimate=pl.CostEstimate(flops=flops, bytes_accessed=moved, transcendentals=exps),
    )(
        where,
        *(
            pltpu.with_memory_space_constraint(entry[2], pltpu.HBM)
            if entry[0] in placed
            else entry[2]
            for entry in ins
        ),
        *(pltpu.with_memory_space_constraint(piece, home) for piece in pieces),
    )
    return types.SimpleNamespace(**{entry[0]: value for entry, value in zip(outs, results)})


def at_step(step):
    return pl.when(pl.program_id(0) == step)


def at_end():
    return pl.when(pl.program_id(0) == pl.num_programs(0) - 1)


def layer_norm(values, gain, shift):
    center = values - jnp.mean(values, axis=-1, keepdims=True)
    spread = jnp.mean(center * center, axis=-1, keepdims=True)
    return center * lax.rsqrt(spread + EPSILON) * gain + shift


def layer_norm_back(values, gain, grad):
    center = values - jnp.mean(values, axis=-1, keepdims=True)
    scale = lax.rsqrt(jnp.mean(center * center, axis=-1, keepdims=True) + EPSILON)
    unit = center * scale
    scaled = grad * gain
    back = scale * (
        scaled
        - jnp.mean(scaled, axis=-1, keepdims=True)
        - unit * jnp.mean(scaled * unit, axis=-1, keepdims=True)
    )
    return back, row_sum(grad * unit), row_sum(grad)


def row_sum(values):
    return jnp.sum(values, axis=0, keepdims=True)


def fetch_scratch(pieces, width, parts, wide):
    copies = pieces[0].shape[1] if len(pieces) == 1 else 4
    return [
        ("weights", pltpu.VMEM((parts, wide, width), LOW)),
        ("extras", pltpu.VMEM((parts, EXTRA, width), LOW)),
        ("sems", pltpu.SemaphoreType.DMA((parts, copies + 1))),
    ]


def fetch(r):
    parts = r.weights.shape[0]

    def copies(at):
        if len(r.pieces) == 1:
            sources = [r.pieces[0].at[at, owner] for owner in range(r.pieces[0].shape[1])]
            owners = list(range(len(sources)))
        else:
            core, row = r.where[1], r.where[2]
            sources = [r.pieces[4 * at + which] for which in range(4)]
            owners = [
                2 * (row + up - 2 * row * up) + (core + over - 2 * core * over)
                for over in range(2)
                for up in range(2)
            ]
        rows = sources[0].shape[0] - EXTRA
        extra = sources[0].at[pl.ds(rows, EXTRA), :]
        result = [pltpu.make_async_copy(extra, r.extras.at[at], r.sems.at[at, len(sources)])]
        for which, (source, owner) in enumerate(zip(sources, owners)):
            target = r.weights.at[at, pl.ds(pl.multiple_of(owner * rows, rows), rows), :]
            result.append(
                pltpu.make_async_copy(source.at[pl.ds(0, rows), :], target, r.sems.at[at, which])
            )
        return result

    @at_step(0)
    def _():
        for at in range(parts):
            for copy in copies(at):
                copy.start()

    def wait(at):
        @at_step(at)
        def _():
            for copy in copies(at):
                copy.wait()

    for at in range(parts):
        wait(at)
    return r.weights.at[pl.program_id(0)], r.extras.at[pl.program_id(0)]


def joined(terms):
    wide = terms.astype(F32)
    return wide[0:1] + (wide[1:2] + wide[2:3])


def gradient_outs(parts, wide, total, stepwise):
    if not stepwise:
        return [("gradient", part(wide, total), (parts, wide, total), LOW)]
    shape = (2, parts, wide // 4, total)
    block = pl.BlockSpec((2, 1, wide // 4, total), lambda t, _: (0, t, 0, 0))
    return [("kept", block, shape, LOW), ("sent", block, shape, LOW)]


def store_gradient(r, pairs):
    column = 0
    for turned, right in pairs:
        span = slice(column, column + right.shape[1])
        column += right.shape[1]
        if hasattr(r, "gradient"):
            r.gradient[0, :, span] = mm(turned[...], right).astype(LOW)
            continue
        core, row = r.where[1], r.where[2]
        rows = r.kept.shape[2]
        for which, out in enumerate((r.kept, r.sent)):
            for far in range(2):
                owner = 2 * (row + far - 2 * row * far) + (core + which - 2 * core * which)
                start = pl.multiple_of(owner * rows, rows)
                out[far, 0, :, span] = mm(turned[pl.ds(start, rows), :], right).astype(LOW)


def add_biases(shard, rows, lines):
    shard[rows:] = jnp.zeros((EXTRA, shard.shape[1]), LOW)
    for row, left in enumerate(lines):
        for piece in range(3):
            low = left.astype(LOW)
            left = left - low.astype(F32)
            at = rows + 3 * row + piece
            shard[at : at + 1, : low.shape[1]] = low


def attention_shard(where, w_qkv, w_out, b_qv):
    _, rows, width = w_qkv.shape

    def body(r):
        for piece in range(3):
            r.shard[:rows, piece * width : (piece + 1) * width] = r.qkv[piece].astype(LOW)
        r.shard[:rows, 3 * width :] = r.out[...].T.astype(LOW)
        add_biases(r.shard, rows, [r.bias[0:1], r.bias[1:2]])

    shape = (rows + EXTRA, 4 * width)
    return call(
        body,
        1,
        where,
        [
            ("qkv", whole(3, rows, width), w_qkv),
            ("out", whole(width, rows), w_out),
            ("bias", whole(2, width), b_qv),
        ],
        [("shard", whole(*shape), shape, LOW)],
        placed=("qkv", "out", "bias", "shard"),
        moved=24 * rows * width,
    ).shard


def forward_shard(where, w_up, w_down, b_up):
    rows = w_up.shape[0]
    hidden = w_up.shape[1] // 2

    def body(r):
        r.shard[:rows, :hidden] = r.up[...].astype(LOW)
        r.shard[:rows, hidden:] = r.down[...].T.astype(LOW)
        add_biases(r.shard, rows, [r.bias[...]])

    shape = (rows + EXTRA, 2 * hidden)
    return call(
        body,
        1,
        where,
        [
            ("up", pl.BlockSpec((rows, hidden), lambda t, at: (0, at[0])), w_up),
            ("down", pl.BlockSpec((hidden, rows), lambda t, at: (at[0], 0)), w_down),
            ("bias", pl.BlockSpec((1, hidden), lambda t, at: (0, at[0])), b_up[None]),
        ],
        [("shard", whole(*shape), shape, LOW)],
        placed=("up", "down", "bias", "shard"),
        moved=12 * rows * hidden,
    ).shard


def attention(where, pieces, parts, keep, first, carried, last):
    rows = keep.shape[0]
    half = rows // 2
    width = pieces[0].shape[-1] // 4
    heads = width // HEAD
    wide = first[0].shape[1] if first else carried[0].shape[1]

    def body(r):
        w, extra = fetch(r)
        normed = r.n1_out if first else r.n1

        @at_step(0)
        def _():
            if not first:
                r.y_out[...] = r.y[...]
                return
            for at, ref in ((0, r.own), (half, r.far)):
                tokens = ref[...].astype(F32)
                normed[at : at + half] = layer_norm(tokens, r.g1[...], r.s1[...]).astype(LOW)
                r.y_out[at : at + half] = tokens + r.b_out[...]

        terms = extra[...]
        bias_q, bias_v = joined(terms[0:3, :width]), joined(terms[3:6, :width])
        bias = jnp.concatenate([bias_q, jnp.zeros_like(bias_q), bias_v], axis=1)
        low = (mm(normed[...], w[:, : 3 * width]) + bias).astype(LOW)
        r.p[0] = low
        seen = r.keep[...] > 0
        for head in range(heads):
            at = head * HEAD
            query = low[:, at : at + HEAD]
            key = low[:, width + at : width + at + HEAD]
            value = low[:, 2 * width + at : 2 * width + at + HEAD]
            scores = jnp.where(seen, mm(key, query, NT) * HEAD**-0.5, -1e30)
            top = jnp.max(scores, axis=0, keepdims=True)
            exponent = jnp.exp(scores - top)
            total = jnp.sum(exponent, axis=0, keepdims=True)
            probability = (exponent * (1.0 / total)).astype(LOW)
            r.o[0, :, at : at + HEAD] = mm(probability, value, TN).astype(LOW)
            r.l[0, head : head + 1, :] = top + jnp.log(total)
        r.y_out[...] += mm(r.o[0], w[:, 3 * width :], NT)

        if last:

            @at_end()
            def _():
                r.n2[...] = layer_norm(r.y_out[...], r.g2[...], r.s2[...]).astype(LOW)

    line = whole(1, wide)
    ins = [("keep", whole(rows, 1), keep)]
    outs = [
        ("p", part(rows, 3 * width), (parts, rows, 3 * width), LOW),
        ("o", part(rows, width), (parts, rows, width), LOW),
        ("l", part(heads, rows), (parts, heads, rows), F32),
        ("y_out", whole(rows, wide), (rows, wide), F32),
    ]
    if first:
        specs = [whole(half, wide)] * 2 + [line] * 3
        ins += list(zip(("own", "far", "b_out", "g1", "s1"), specs, first))
        outs.append(("n1_out", whole(rows, wide), (rows, wide), LOW))
    else:
        ins += list(zip(("n1", "y"), [whole(rows, wide)] * 2, carried))
    if last:
        ins += list(zip(("g2", "s2"), [line] * 2, last))
        outs.append(("n2", whole(rows, wide), (rows, wide), LOW))
    return call(
        body,
        parts,
        where,
        ins,
        outs,
        fetch_scratch(pieces, 4 * width, parts, wide),
        pieces,
        flops=8 * parts * rows * wide * width + 4 * parts * rows * rows * width,
        moved=8 * parts * wide * width + 12 * rows * wide,
        exps=parts * heads * rows * rows,
        vmem=30 if parts <= 2 else 56,
    )


def forward_up(where, pieces, parts, own, far, branch, residual):
    rows, wide = own.shape
    half = rows // 2
    width = pieces[0].shape[-1] // 2

    def body(r):
        w, extra = fetch(r)

        @at_step(0)
        def _():
            r.both[:rows] = r.own[...]
            r.both[rows:] = r.far[...]
            r.branch_sum[...] = r.branch_in[...]

        hidden = mm(r.both[...], w[:, :width]) + joined(extra[0:3, :width])
        bell = 0.5 * (1.0 + lax.erf(hidden * 0.5**0.5))
        active = (hidden * bell).astype(LOW)
        slope = bell + hidden * jnp.exp(hidden * hidden * -0.5) * 0.3989422804014327
        r.branch_sum[...] += mm(active, w[:, width:], NT)
        r.active[0] = active
        r.slope[0] = slope.astype(LOW)

        @at_end()
        def _():
            r.out_keep[:half] = r.y[:half] + r.branch_sum[:half]
            r.out_keep[half:] = r.branch_sum[rows + half :]
            r.out_send[:half] = (r.y[half:] + r.branch_sum[half:rows]).astype(LOW)
            r.out_send[half:] = r.branch_sum[rows : rows + half].astype(LOW)

    mine = whole(rows, wide)
    shape = (parts, 2 * rows, width)
    return call(
        body,
        parts,
        where,
        [
            ("own", mine, own),
            ("far", mine, far),
            ("branch_in", whole(2 * rows, wide), branch),
            ("y", mine, residual),
        ],
        [
            ("active", part(2 * rows, width), shape, LOW),
            ("slope", part(2 * rows, width), shape, LOW),
            ("out_keep", mine, (rows, wide), F32),
            ("out_send", mine, (rows, wide), LOW),
        ],
        [
            ("both", pltpu.VMEM((2 * rows, wide), LOW)),
            ("branch_sum", pltpu.VMEM((2 * rows, wide), F32)),
        ]
        + fetch_scratch(pieces, 2 * width, parts, wide),
        pieces,
        flops=8 * parts * rows * width * wide,
        moved=4 * parts * wide * width + 12 * rows * wide,
        exps=4 * parts * rows * width,
    )


def forward_down(where, pieces, own, far, grad, carried, active, slope):
    rows, wide = own.shape
    parts, _, width = active.shape

    def body(r):
        w, _ = fetch(r)

        @at_step(0)
        def _():
            r.turned[:, :rows] = r.own[...].T
            r.turned[:, rows:] = r.far[...].T
            r.turned_grad[...] = r.grad[...].T
            r.grad_sum[...] = r.grad_in[...]

        grad_active = mm(r.grad[...], w[:, width:])
        grad_hidden = (grad_active * r.slope[0].astype(F32)).astype(LOW)
        r.db[0] = row_sum(grad_hidden.astype(F32))
        r.grad_sum[...] += mm(grad_hidden, w[:, :width], NT)
        store_gradient(r, [(r.turned, grad_hidden), (r.turned_grad, r.active[0])])

        @at_end()
        def _():
            r.dn_keep[...] = r.grad_sum[:rows]
            r.dn_send[...] = r.grad_sum[rows:].astype(LOW)

    mine, double = whole(rows, wide), whole(2 * rows, wide)
    return call(
        body,
        parts,
        where,
        [
            ("own", mine, own),
            ("far", mine, far),
            ("grad", double, grad),
            ("grad_in", double, carried),
            ("active", part(2 * rows, width), active),
            ("slope", part(2 * rows, width), slope),
        ],
        [
            ("db", part(1, width), (parts, 1, width), F32),
            ("dn_keep", mine, (rows, wide), F32),
            ("dn_send", mine, (rows, wide), LOW),
        ]
        + gradient_outs(parts, wide, 2 * width, True),
        [
            ("turned", pltpu.VMEM((wide, 2 * rows), LOW)),
            ("turned_grad", pltpu.VMEM((wide, 2 * rows), LOW)),
            ("grad_sum", pltpu.VMEM((2 * rows, wide), F32)),
        ]
        + fetch_scratch(pieces, 2 * width, parts, wide),
        pieces,
        flops=16 * parts * rows * width * wide,
        moved=8 * parts * wide * width + 12 * rows * wide,
    )


def forward(where, pieces, parts, own, far, grad, carried, residual, stepwise):
    rows, wide = own.shape
    half = rows // 2
    width = pieces[0].shape[-1] // 2

    def body(r):
        w, extra = fetch(r)

        @at_step(0)
        def _():
            r.both[:rows] = r.own[...]
            r.both[rows:] = r.far[...]
            r.turned[...] = r.both[...].T
            r.turned_grad[...] = r.grad[...].T
            r.branch_sum[...] = r.branch_in[...] if carried else jnp.zeros((2 * rows, wide), F32)
            r.grad_sum[...] = r.grad_in[...] if carried else jnp.zeros((2 * rows, wide), F32)

        hidden = mm(r.both[...], w[:, :width]) + joined(extra[0:3, :width])
        bell = 0.5 * (1.0 + lax.erf(hidden * 0.5**0.5))
        active = (hidden * bell).astype(LOW)
        slope = bell + hidden * jnp.exp(hidden * hidden * -0.5) * 0.3989422804014327
        r.branch_sum[...] += mm(active, w[:, width:], NT)
        grad_hidden = (mm(r.grad[...], w[:, width:]) * slope).astype(LOW)
        r.db[0] = row_sum(grad_hidden.astype(F32))
        r.grad_sum[...] += mm(grad_hidden, w[:, :width], NT)
        store_gradient(r, [(r.turned, grad_hidden), (r.turned_grad, active)])

        if residual is None:
            return

        @at_end()
        def _():
            r.out_keep[:half] = r.y[:half] + r.branch_sum[:half]
            r.out_keep[half:] = r.branch_sum[rows + half :]
            r.out_send[:half] = (r.y[half:] + r.branch_sum[half:rows]).astype(LOW)
            r.out_send[half:] = r.branch_sum[rows : rows + half].astype(LOW)
            r.dn_keep[...] = r.grad_sum[:rows]
            r.dn_send[...] = r.grad_sum[rows:].astype(LOW)

    mine, double = whole(rows, wide), whole(2 * rows, wide)
    sums = [("branch_sum", (2 * rows, wide), F32), ("grad_sum", (2 * rows, wide), F32)]
    ins = [("own", mine, own), ("far", mine, far), ("grad", double, grad)]
    outs = [("db", part(1, width), (parts, 1, width), F32)]
    scratch = [
        ("both", pltpu.VMEM((2 * rows, wide), LOW)),
        ("turned", pltpu.VMEM((wide, 2 * rows), LOW)),
        ("turned_grad", pltpu.VMEM((wide, 2 * rows), LOW)),
    ]
    if carried:
        ins += [("branch_in", double, carried[0]), ("grad_in", double, carried[1])]
    if residual is None:
        outs += [(name, double, shape, kind) for name, shape, kind in sums]
    else:
        ins.append(("y", mine, residual))
        outs += [
            ("out_keep", mine, (rows, wide), F32),
            ("out_send", mine, (rows, wide), LOW),
            ("dn_keep", mine, (rows, wide), F32),
            ("dn_send", mine, (rows, wide), LOW),
        ]
        scratch += [(name, pltpu.VMEM(shape, kind)) for name, shape, kind in sums]
    outs += gradient_outs(parts, wide, 2 * width, stepwise)
    return call(
        body,
        parts,
        where,
        ins,
        outs,
        scratch + fetch_scratch(pieces, 2 * width, parts, wide),
        pieces,
        flops=24 * parts * rows * width * wide,
        moved=8 * parts * wide * width + 12 * rows * wide,
        exps=4 * parts * rows * width,
        vmem=30 if parts <= 2 else 56,
    )


def backward(where, pieces, parts, saved, keep, normed, first, carried, last, stepwise):
    rows, wide = normed.shape
    half = rows // 2
    width = saved.o.shape[2]
    heads = width // HEAD

    def body(r):
        w, _ = fetch(r)
        low_grad = r.dyb_out if first else r.dyb

        @at_step(0)
        def _():
            if first:
                grad_normed = r.dn_keep[...] + r.dn_came[...].astype(F32)
                back, gain_sum, shift_sum = layer_norm_back(r.y[...], r.g2[...], grad_normed)
                grad_out = r.grad[...].astype(F32)
                r.dy_sum[...] = grad_out + back
                low_grad[...] = r.dy_sum[...].astype(LOW)
                r.sums[0:1] = row_sum(low_grad[...].astype(F32))
                r.sums[1:2] = row_sum(grad_out)
                r.sums[2:3] = gain_sum
                r.sums[3:4] = shift_sum
                r.sums[4:8] = jnp.zeros((4, wide), F32)
                r.dn_sum[...] = jnp.zeros_like(r.dn_sum)
            else:
                r.dn_sum[...] = r.dn[...]
            r.turned[...] = r.n1[...].T
            r.turned_grad[...] = low_grad[...].T

        grad_mixed = mm(low_grad[...], w[:, 3 * width :]).astype(LOW)
        seen = r.keep[...] > 0
        for head in range(heads):
            at = head * HEAD
            query = r.p[0, :, at : at + HEAD]
            key = r.p[0, :, width + at : width + at + HEAD]
            value = r.p[0, :, 2 * width + at : 2 * width + at + HEAD]
            grad = grad_mixed[:, at : at + HEAD]
            scores = jnp.where(seen, mm(key, query, NT) * HEAD**-0.5, -1e30)
            probability = jnp.exp(scores - r.l[0, head : head + 1, :])
            grad_probability = mm(value, grad, NT)
            grad_value = mm(probability.astype(LOW), grad)
            inner = jnp.sum(grad_probability * probability, axis=0, keepdims=True)
            grad_scores = (probability * (grad_probability - inner)).astype(LOW)
            grad_query = mm(grad_scores, key, TN) * HEAD**-0.5
            grad_key = mm(grad_scores, query) * HEAD**-0.5
            r.dp[:, at : at + HEAD] = grad_query.astype(LOW)
            r.dp[:, width + at : width + at + HEAD] = grad_key.astype(LOW)
            r.dp[:, 2 * width + at : 2 * width + at + HEAD] = grad_value.astype(LOW)
        r.db[0] = row_sum(r.dp[...].astype(F32))
        r.dn_sum[...] += mm(r.dp[...], w[:, : 3 * width], NT)
        store_gradient(r, [(r.turned, r.dp[...]), (r.turned_grad, r.o[0])])

        if not last:
            return

        @at_end()
        def _():
            dy = r.dy_sum if first else r.dy
            gain_sum = shift_sum = 0.0
            for at, ref, out in ((0, r.own, r.gi_own), (half, r.far, r.gi_far)):
                back, gain_add, shift_add = layer_norm_back(
                    ref[...].astype(F32), r.g1[...], r.dn_sum[at : at + half]
                )
                out[...] = (dy[at : at + half] + back).astype(LOW)
                gain_sum, shift_sum = gain_sum + gain_add, shift_sum + shift_add
            r.end_sums[0:1] = gain_sum
            r.end_sums[1:2] = shift_sum
            r.end_sums[2:8] = jnp.zeros((6, wide), F32)

    mine, line, eight = whole(rows, wide), whole(1, wide), whole(8, wide)
    ins = [
        ("p", part(rows, 3 * width), saved.p),
        ("o", part(rows, width), saved.o),
        ("l", part(heads, rows), saved.l),
        ("keep", whole(rows, 1), keep),
        ("n1", mine, normed),
    ]
    outs = [("db", part(1, 3 * width), (parts, 1, 3 * width), F32)]
    scratch = [
        ("dp", pltpu.VMEM((rows, 3 * width), LOW)),
        ("turned", pltpu.VMEM((wide, rows), LOW)),
        ("turned_grad", pltpu.VMEM((wide, rows), LOW)),
    ]
    sums = [("dn_sum", (rows, wide), F32)]
    if first:
        ins += list(zip(("y", "dn_keep", "dn_came", "grad", "g2"), [mine] * 4 + [line], first))
        outs += [("dyb_out", mine, (rows, wide), LOW), ("sums", eight, (8, wide), F32)]
        sums.append(("dy_sum", (rows, wide), F32))
    else:
        ins += list(zip(("dyb", "dy", "dn"), [mine] * 3, carried))
    if last:
        ins += list(zip(("own", "far", "g1"), [whole(half, wide)] * 2 + [line], last))
        outs += [
            ("gi_own", whole(half, wide), (half, wide), LOW),
            ("gi_far", whole(half, wide), (half, wide), LOW),
            ("end_sums", eight, (8, wide), F32),
        ]
        scratch += [(name, pltpu.VMEM(shape, kind)) for name, shape, kind in sums]
    else:
        outs += [(name, mine, shape, kind) for name, shape, kind in sums]
    outs += gradient_outs(parts, wide, 4 * width, stepwise)
    return call(
        body,
        parts,
        where,
        ins,
        outs,
        scratch + fetch_scratch(pieces, 4 * width, parts, wide),
        pieces,
        placed=("kept", "sent"),
        home=pltpu.HBM,
        flops=16 * parts * rows * wide * width + 10 * parts * rows * rows * width,
        moved=16 * parts * wide * width + 16 * rows * wide,
        exps=parts * heads * rows * rows,
        vmem=30 if parts <= 2 else 56,
    )


def spread(where, pieces, parts, first=0, before=None):
    def body(r):
        for at in range(len(pieces)):

            @at_step(at)
            def _(ref=getattr(r, f"piece{at}")):
                r.out[...] = ref[...].astype(F32)

    pair = pieces[0].shape
    block = pl.BlockSpec(
        pair, lambda t, at: (lax.rem(at[3] - first - t + 2 * parts, parts), 0, 0)
    )
    ins = [(f"piece{at}", whole(*pair), piece) for at, piece in enumerate(pieces)]
    if before is not None:
        ins.append(("before", pl.BlockSpec(memory_space=pl.ANY), before))
    return call(
        body,
        len(pieces),
        where,
        ins,
        [("out", block, (parts * pair[0],) + pair[1:], F32)],
        moved=6 * len(pieces) * pieces[0].size,
        aliases=() if before is None else ((len(ins), 0),),
    ).out


def forward_total(where, own, far):
    rows, width = own.shape[0], own.shape[1] // 2

    def body(r):
        for flip, ref in ((0, r.own), (1, r.far)):
            block = r.where[0] + flip - 2 * r.where[0] * flip
            span = pl.ds(pl.multiple_of(block * width, width), width)
            r.up[:, span] = ref[:, :width].astype(F32)
            r.down[span, :] = ref[:, width:].astype(F32).T

    got = call(
        body,
        1,
        where,
        [("own", whole(rows, 2 * width), own), ("far", whole(rows, 2 * width), far)],
        [
            ("up", whole(rows, 2 * width), (rows, 2 * width), F32),
            ("down", whole(2 * width, rows), (2 * width, rows), F32),
        ],
        moved=24 * rows * width,
    )
    return got.up, got.down


def attention_total(where, grad):
    rows, width = grad.shape[0], grad.shape[1] // 4

    def body(r):
        for piece in range(3):
            r.qkv[piece] = r.grad[:, piece * width : (piece + 1) * width]
        r.out[...] = r.grad[:, 3 * width :].T

    got = call(
        body,
        1,
        where,
        [("grad", whole(rows, 4 * width), grad)],
        [
            ("qkv", whole(3, rows, width), (3, rows, width), F32),
            ("out", whole(width, rows), (width, rows), F32),
        ],
        moved=32 * rows * width,
    )
    return got.qkv, got.out


def on_device(
    inputs,
    cotangent,
    visible,
    w_qkv,
    b_qv,
    w_out,
    b_out,
    w_up,
    b_up,
    w_down,
    b_down,
    gain_one,
    shift_one,
    gain_two,
    shift_two,
):
    images, half, wide = inputs.shape
    ctx_at, tp_at, fsdp_at = (lax.axis_index(name) for name in ("ctx", "tp", "fsdp"))
    blocks, parts, owners = (lax.axis_size(name) for name in ("ctx", "tp", "fsdp"))
    assert blocks == 2 and images == blocks * parts
    first = blocks * tp_at
    mine, other = first + ctx_at, first + 1 - ctx_at
    where = jnp.stack([ctx_at, fsdp_at % 2, fsdp_at // 2, tp_at]).astype(jnp.int32)
    heads_width = w_qkv.shape[2]
    hidden_half = w_up.shape[1] // 2
    rows = 2 * half

    def swap(values):
        return lax.ppermute(values, "ctx", [(0, 1), (1, 0)])

    def pick(values, index):
        return lax.dynamic_index_in_dim(values, index, 0, keepdims=False)

    def in_order(own, received):
        return jnp.where(ctx_at == 0, own, received), jnp.where(ctx_at == 0, received, own)

    stepwise = owners == 4 and parts == 4
    behind = jnp.mod(tp_at - jnp.arange(parts), parts) if stepwise else jnp.arange(parts)

    def to_core(values):
        return lax.ppermute(values, "fsdp", [(0, 1), (1, 0), (2, 3), (3, 2)])

    def to_y(values):
        return lax.ppermute(values, "fsdp", [(0, 2), (2, 0), (1, 3), (3, 1)])

    def to_tp(values):
        return lax.ppermute(values, "tp", [(i, (i + 1) % parts) for i in range(parts)])

    def gather(shard):
        full = lax.all_gather(shard, ("tp", "fsdp"), axis=0, tiled=True)
        return [full.reshape(parts, owners, *shard.shape)]

    def scatter(gradient):
        flat = gradient.reshape(-1, gradient.shape[2])
        return lax.psum_scatter(flat, ("tp", "fsdp"), scatter_dimension=0, tiled=True)

    def raised(upper, came):
        return upper.astype(F32) + came.astype(F32)

    def onward(total):
        return to_tp(total.astype(LOW))

    tie = lax.optimization_barrier

    a0 = attention_shard(where, w_qkv.transpose(1, 0, 2), w_out, b_qv)
    b0 = forward_shard(where, w_up, w_down, b_up)
    own = pick(inputs, mine)
    cot_pair = jnp.stack([pick(cotangent, mine), pick(cotangent, other)])
    mine_seen = pick(visible, mine).reshape(blocks, half)
    other_seen = pick(visible, other).reshape(blocks, half)
    keep = jnp.concatenate([pick(mine_seen, ctx_at), pick(mine_seen, 1 - ctx_at)])
    keep_other = jnp.concatenate([pick(other_seen, 1 - ctx_at), pick(other_seen, ctx_at)])
    keep, keep_other = keep[:, None], keep_other[:, None]
    keep_all = jnp.concatenate([keep, keep_other]).astype(LOW)
    norm_one, norm_two = (gain_one[None], shift_one[None]), (gain_two[None], shift_two[None])

    def hidden_gradient(swapped):
        rows_of = [cot_pair[0], swapped[1], swapped[0], cot_pair[1]]
        return jnp.concatenate(rows_of) * keep_all

    def output_pair(kept, came):
        seen = jnp.concatenate([keep[:half], keep_other[half:]]).astype(F32)
        came = came.astype(F32)
        rows_of = kept + jnp.concatenate([came[half:], came[:half]]) + b_down
        rows_of = (rows_of * seen).astype(LOW)
        return jnp.stack(in_order(rows_of[:half], rows_of[half:]))

    if stepwise:
        far = pick(inputs, other)
        a0, b0, a1, ya0, far, cot_pair = tie((a0, b0, to_tp(a0), to_y(a0), far, cot_pair))

        a1, a2, ya1, ca0, cya0, far = tie(
            (a1, to_tp(a1), to_y(a1), to_core(a0), to_core(ya0), swap(far))
        )

        a2, a3, ya2, ca1, cya1, cot_swapped = tie(
            (a2, to_tp(a2), to_y(a2), to_core(a1), to_core(ya1), swap(cot_pair))
        )

        start = (own, far, b_out[None]) + norm_one
        early = attention(
            where, [a0, ya0, ca0, cya0, a1, ya1, ca1, cya1], 2, keep, start, None, None
        )
        normed, total_y, a3, b0, ya3, b1, ca2, cya2 = tie(
            (
                early.n1_out,
                early.y_out,
                a3,
                b0,
                to_y(a3),
                to_tp(b0),
                to_core(a2),
                to_core(ya2),
            )
        )

        b2, yb0 = to_tp(b1), to_y(b0)
        ca3, cya3 = to_core(a3), to_core(ya3)
        late = attention(
            where,
            [a2, ya2, ca2, cya2, a3, ya3, ca3, cya3],
            2,
            keep,
            None,
            (normed, total_y),
            norm_two,
        )
        normed_two, residual = late.n2, late.y_out
        b2, yb0 = tie((b2, yb0))
        grad_low = hidden_gradient(cot_swapped)

        normed_far, b3, yb1, cb0, cyb0 = tie(
            (swap(normed_two), to_tp(b2), to_y(b1), to_core(b0), to_core(yb0))
        )

        def block(pieces, carried, last):
            return forward(
                where, pieces, 2, normed_two, normed_far, grad_low, carried, last, True
            )

        yb2, cb1, cyb1 = tie((to_y(b2), to_core(b1), to_core(yb1)))

        f01 = block([b0, yb0, cb0, cyb0, b1, yb1, cb1, cyb1], None, None)
        sums, sent, yb3, cb2, cyb2 = tie(
            (
                (f01.branch_sum, f01.grad_sum),
                f01.sent,
                to_y(b3),
                to_core(b2),
                to_core(yb2),
            )
        )

        came01, cb3, cyb3 = tie((to_core(sent), to_core(b3), to_core(yb3)))

        def upper(got, came, at):
            return to_y(raised(got.kept[1, at], came[1, at]).astype(LOW))

        def lower(got, came, at, lift):
            return raised(got.kept[0, at], came[0, at]) + lift.astype(F32)

        lift1 = upper(f01, came01, 1)
        late_pieces = [b2, yb2, cb2, cyb2, b3, yb3, cb3, cyb3]
        up23 = forward_up(
            where, late_pieces, 2, normed_two, normed_far, sums[0], residual
        )
        out_send, active, slope = tie((up23.out_send, up23.active, up23.slope))

        f23 = forward_down(
            where, late_pieces, normed_two, normed_far, grad_low, sums[1], active, slope
        )
        dn_send, sent, out_came, lift1 = tie((f23.dn_send, f23.sent, swap(out_send), lift1))

        ring_sum = onward(lower(f01, came01, 1, lift1))
        lift0 = upper(f01, came01, 0)
        h0 = output_pair(up23.out_keep, out_came)
        dn_came, came23, lift0, h0 = tie((swap(dn_send), to_core(sent), lift0, h0))

        h1 = to_tp(h0)
        lift2 = upper(f23, came23, 0)
        begin = (residual, f23.dn_keep, dn_came, grad_low[:rows], gain_two[None])
        g_early = backward(
            where,
            [a0, ya0, ca0, cya0, a1, ya1, ca1, cya1],
            2,
            early,
            keep,
            normed,
            begin,
            None,
            None,
            True,
        )
        carried, sent_early, h1, lift2, ring_sum = tie(
            (
                (g_early.dyb_out, g_early.dy_sum, g_early.dn_sum),
                g_early.sent,
                h1,
                lift2,
                ring_sum,
            )
        )

        h2 = to_tp(h1)
        lift3 = upper(f23, came23, 1)
        came_early = to_core(sent_early)
        g_late = backward(
            where,
            [a2, ya2, ca2, cya2, a3, ya3, ca3, cya3],
            2,
            late,
            keep,
            normed,
            None,
            carried,
            (own, far, gain_one[None]),
            True,
        )
        gi_far, sent_late, came_early, h2, lift3 = tie(
            (g_late.gi_far, g_late.sent, came_early, h2, lift3)
        )

        quarter = wide // owners // 4

        def rows_of(values, axis, block):
            return lax.dynamic_slice_in_dim(values, block * quarter, quarter, axis)

        def both(kept, came, block):
            return raised(rows_of(kept, 2, block), rows_of(came, 2, block))

        def first_sends(got, came):
            across = swap(both(got.kept, came, 1 - ctx_at).astype(LOW))
            second = raised(got.kept[1, :, 2 * quarter :], came[1, :, 2 * quarter :])
            return across, to_y(second.astype(LOW))

        def second_sends(got, came, across, up):
            near = both(got.kept, came, ctx_at) + across.astype(F32)
            second = raised(got.kept[0, :, 2 * quarter :], came[0, :, 2 * quarter :])
            second = second + up.astype(F32)
            return (
                near[0],
                to_y(near[1].astype(LOW)),
                rows_of(second, 1, ctx_at),
                swap(rows_of(second, 1, 1 - ctx_at).astype(LOW)),
            )

        def third(near, lifted, second, across):
            return jnp.concatenate(
                [near + lifted.astype(F32), second + across.astype(F32)], axis=1
            )

        up_bias = jnp.concatenate([f01.db, f23.db])
        qkv_bias = jnp.concatenate([g_early.db, g_late.db])
        up_bias = lax.dynamic_update_slice(
            jnp.zeros((parts, 2, hidden_half), F32), up_bias, (0, ctx_at, 0)
        )
        small = jnp.concatenate(
            [
                g_early.sums[:4],
                g_late.end_sums[:2],
                up_bias[behind].reshape(-1, wide),
                qkv_bias[behind].reshape(-1, wide),
            ]
        )
        ring_sum = onward(ring_sum.astype(F32) + lower(f23, came23, 0, lift2))
        side0, up0 = first_sends(g_early, came_early)
        gi_far, came_late, small, small_came, ring_sum, up0 = tie(
            (
                swap(gi_far),
                to_core(sent_late),
                small,
                to_core(small),
                ring_sum,
                up0,
            )
        )

        ring_sum = onward(ring_sum.astype(F32) + lower(f23, came23, 1, lift3))
        g0 = jnp.stack(in_order(g_late.gi_own, gi_far))
        side1, up1 = first_sends(g_late, came_late)
        small = small + small_came
        g1, h3, side0, side1, up1, small, small_came = tie(
            (to_tp(g0), to_tp(h2), side0, side1, up1, small, to_y(small))
        )

        sends0 = second_sends(g_early, came_early, side0, up0)
        sends1 = second_sends(g_late, came_late, side1, up1)
        small = small + small_came
        ring_sum, sends0, sends1, small, small_came = tie(
            (ring_sum, sends0, sends1, small, swap(small))
        )

        halves0, halves1 = third(*sends0), third(*sends1)
        total = onward(halves0[1])
        forward_own = (ring_sum.astype(F32) + lower(f01, came01, 0, lift0)).astype(LOW)
        small = small + small_came
        total, forward_far, halves0, halves1, g2, small, small_came = tie(
            (
                total,
                swap(forward_own),
                halves0,
                halves1,
                to_tp(g1),
                small,
                lax.ppermute(small, "tp", [(0, 1), (1, 0), (2, 3), (3, 2)]),
            )
        )

        total = onward(total.astype(F32) + halves1[0])
        up_total, down_total = forward_total(where, forward_own, forward_far)
        result = spread(where, [h0, h1, h2, h3], parts)
        small = small + small_came
        small_came = lax.ppermute(small, "tp", [(0, 2), (2, 0), (1, 3), (3, 1)])
        total, g2, up_total, small, small_came, result = tie(
            (total, g2, up_total, small, small_came, result)
        )

        small = small + small_came

        total = tie(onward(total.astype(F32) + halves1[1]))
        g3 = to_tp(g2)

        mine_half = (total.astype(F32) + halves0[0]).astype(LOW)
        far_half = swap(mine_half)
        lows, highs = in_order(mine_half, far_half)
        attention_sum = jnp.concatenate(
            [lows[:quarter], highs[:quarter], lows[quarter:], highs[quarter:]]
        ).astype(F32)
        qkv_total, out_total = attention_total(where, attention_sum)
        grad_inputs = spread(where, [g0, g1, g2], parts)
        g3, qkv_total, grad_inputs = tie((g3, qkv_total, grad_inputs))
        grad_inputs = spread(where, [g3], parts, 3, grad_inputs)
    else:
        attention_w, forward_w = gather(a0), gather(b0)
        far = swap(pick(inputs, other))
        grad_low = hidden_gradient(swap(cot_pair))
        start = (own, far, b_out[None]) + norm_one
        got = attention(where, attention_w, parts, keep, start, None, norm_two)
        end = forward(
            where,
            forward_w,
            parts,
            got.n2,
            swap(got.n2),
            grad_low,
            None,
            got.y_out,
            False,
        )
        h0 = output_pair(end.out_keep, swap(end.out_send))
        result = lax.all_gather(h0, "tp", axis=0, tiled=True).astype(F32)
        begin = (got.y_out, end.dn_keep, swap(end.dn_send), grad_low[:rows], gain_two[None])
        back = backward(
            where,
            attention_w,
            parts,
            got,
            keep,
            got.n1_out,
            begin,
            None,
            (own, far, gain_one[None]),
            False,
        )
        g0 = jnp.stack(in_order(back.gi_own, swap(back.gi_far)))
        grad_inputs = lax.all_gather(g0, "tp", axis=0, tiled=True).astype(F32)
        forward_own = scatter(end.gradient)
        attention_own = scatter(back.gradient)
        attention_sum = attention_own.astype(F32) + swap(attention_own).astype(F32)
        up_total, down_total = forward_total(where, forward_own, swap(forward_own))
        up_bias = lax.dynamic_update_slice(
            jnp.zeros((parts, 2, hidden_half), F32), end.db, (0, ctx_at, 0)
        )
        small = jnp.concatenate(
            [
                back.sums[:4],
                back.end_sums[:2],
                up_bias.reshape(-1, wide),
                back.db.reshape(-1, wide),
            ]
        )
        small = lax.psum(small, ("fsdp", "ctx", "tp"))
        qkv_total, out_total = attention_total(where, attention_sum)
    up_rows = parts * 2 * hidden_half // wide
    up_small = small[6 : 6 + up_rows].reshape(parts, 2 * hidden_half)
    qkv_small = small[6 + up_rows :].reshape(parts, 3, heads_width)
    return (
        result,
        grad_inputs,
        qkv_total.transpose(1, 0, 2),
        pick(qkv_small, tp_at)[0::2],
        out_total,
        small[0],
        up_total,
        pick(up_small, tp_at),
        down_total,
        small[1],
        small[4],
        small[5],
        small[2],
        small[3],
    )


def solution(mesh):
    placed = (
        P("fsdp", "ctx", None),
        P("fsdp", "ctx", None),
        P("fsdp", None),
        P("fsdp", None, "tp"),
        P(None, "tp"),
        P("tp", "fsdp"),
        P(),
        P("fsdp", "tp"),
        P("tp"),
        P("tp", "fsdp"),
        P(),
        P(),
        P(),
        P(),
        P(),
    )
    return jax.shard_map(
        on_device,
        mesh=mesh,
        in_specs=placed,
        out_specs=(
            P("fsdp", "ctx", None),
            P("fsdp", "ctx", None),
            P("fsdp", None, "tp"),
            P(None, "tp"),
            P("tp", "fsdp"),
            P(),
            P("fsdp", "tp"),
            P("tp"),
            P("tp", "fsdp"),
            P(),
            P(),
            P(),
            P(),
            P(),
        ),
        check_vma=False,
    )
```
